32 devices in a mesh: src: 8 (over z, y), rcv: 4 (over x, core).
Axes of the slice: x: 2, y: 2, z: 4, core: 2. Of those that a mesh axis runs over, the one named last changes fastest.
Arguments:
- traces: bfloat16 [65536, 2048], P(('src', 'rcv'))
- trace_source: int32 [65536], P(('src', 'rcv')), may hold values from 0 to 63, as said below
- trace_offset: int32 [65536], P(('src', 'rcv')), may hold values from 0 to 63
- trace_slot: int32 [65536], P(('src', 'rcv')), may hold values from 0 to 255, as said below
- request_list: int32 [32, 32, 8], P(('src', 'rcv')), may hold values from 0 to 63, as said below
- source_terms: float32 [64, 1024], P('src'), may hold values from -3 to 3
- receiver_terms: float32 [2048, 1024], P(('src', 'rcv')), may hold values from -3 to 3
- offset_terms: float32 [64, 1024], replicated, may hold values from -3 to 3
Outputs:
- source_new: float32 [64, 1024], P('src')
- receiver_new: float32 [2048, 1024], P(('src', 'rcv'))
- offset_new: float32 [64, 1024], replicated
The draws below stay inside these ranges and needn't reach their ends.
Inputs may be any that keep to these rules, and one draw needn't show every extreme that they name: `trace_source`: trace t's source is one of the 8 sources of the src index that holds t. `request_list`: within one device's list for one owner the 8 entries are distinct. `trace_slot`: a slot names an owner and a position in the holding device's own request list.
All inputs are finite; a program needn't handle non-finite values.
Results may differ from the reference program's by a relative error of at most 0.0023.
Values sent between devices are 32-bit elements; how exact they have to be, the bound alone decides.
No kernel may reach another device: no remote copies, remote signals or barrier semaphores. Data moves between devices by JAX's collectives and lax.ppermute only.
A program may use at most 128 MiB of HBM per device.

```python
import math
import jax
import jax.numpy as jnp
from jax import lax

NS = 2048
F = 1024
TR_DEV = 2048
SRC_DEV = 8
RCV_DEV = 64
CAP = 8
NOFF = 64
PEERS = 32
TRACES = 65536
NSRC = 64
NRCV = 2048


def request_plan(key):
    base = jax.random.fold_in(key, 7)
    key_count, key_full, key_order, key_owner, key_pick = jax.random.split(base, 5)
    counts = jax.random.randint(key_count, (PEERS, PEERS), 1, CAP + 1)
    full = jax.random.randint(key_full, (PEERS,), 0, PEERS)
    full = full.at[0].set(PEERS - 1)
    column = jnp.arange(PEERS, dtype=jnp.int32)[None, :]
    counts = jnp.where(column == full[:, None], CAP, counts).astype(jnp.int32)
    scores = jax.random.randint(key_order, (PEERS, PEERS, RCV_DEV), 0, 2 ** 20)
    scores = scores * RCV_DEV + jnp.arange(RCV_DEV, dtype=jnp.int32)[None, None, :]
    scores = scores.at[0, 0, RCV_DEV - 1].set(-1)
    lists = jnp.argsort(scores, axis=2)[:, :, :CAP].astype(jnp.int32)
    device = (jnp.arange(TRACES, dtype=jnp.int32) // TR_DEV).astype(jnp.int32)
    owner = jax.random.randint(key_owner, (TRACES,), 0, PEERS).astype(jnp.int32)
    owner = owner.at[0].set(PEERS - 1)
    live = counts[device, owner]
    within = jax.random.randint(key_pick, (TRACES,), 0, live).astype(jnp.int32)
    within = within.at[0].set(CAP - 1)
    slots = (owner * CAP + within).astype(jnp.int32)
    return (lists, slots)


def draw_request_list(key, part):
    return request_plan(key)[0]


def draw_trace_slot(key, part):
    return request_plan(key)[1]


def draw_trace_source(key, part):
    per_group = TRACES * SRC_DEV // NSRC
    group = (jnp.arange(TRACES, dtype=jnp.int32) // per_group).astype(jnp.int32)
    pick = jax.random.randint(jax.random.fold_in(key, 11), (TRACES,), 0, SRC_DEV)
    return (group * SRC_DEV + pick).astype(jnp.int32)


def draw_traces(key, part):
    key_a, key_b = jax.random.split(jax.random.fold_in(key, 13), 2)
    device = (jnp.arange(TRACES) // TR_DEV).astype(jnp.float32)
    rise = 3.0 ** (device / max(PEERS - 1, 1))
    spread = jnp.exp(jax.random.uniform(key_b, (TRACES,), jnp.float32, -0.7, 0.7))
    samples = jnp.clip(jax.random.normal(key_a, (TRACES, NS), jnp.float32), -6.0, 6.0)
    return (samples * (rise * spread)[:, None]).astype(jnp.bfloat16)


def plant(array, rng, low, top_value):
    longest = array.shape.index(max(array.shape))
    spots = []
    for shift in (0, 1):
        where = [jax.random.randint(jax.random.fold_in(rng, axis), (), 0, length) for axis, length in enumerate(array.shape)]
        where[longest] = (where[longest] + shift) % array.shape[longest]
        spots.append(tuple(where))
    return array.at[spots[0]].set(low).at[spots[1]].set(top_value)


def shard_levels(stream_key, extent, pieces, smallest, top_value):
    loudness, own = 1.0, jax.random.fold_in(stream_key, 6)
    for axis_at, shards_of in pieces:
        heights = jnp.exp(jax.random.uniform(jax.random.fold_in(own, axis_at), (shards_of,), jnp.float32, smallest / len(pieces), top_value / len(pieces)))
        loudness = loudness * jnp.repeat(heights, extent[axis_at] // shards_of).reshape([-1 if axis == axis_at else 1 for axis in range(len(extent))])
    return loudness


def noise(stream_key, extent, deviation, most, cuts=(), held_as=jnp.bfloat16):
    loudness = shard_levels(stream_key, extent, cuts, -0.22, 0.18) if cuts else 1.0
    result = jax.random.normal(stream_key, extent, jnp.float32) * deviation * loudness
    return jnp.minimum(jnp.maximum(result, -most), most).astype(held_as)


def setup_inputs(seed: int = 0) -> dict:
    key_of = jax.random.split(jax.random.key(seed), 9)
    return {
        "traces": draw_traces(jax.random.fold_in(key_of[8], 71), 0),
        "trace_source": draw_trace_source(jax.random.fold_in(key_of[8], 71), 0),
        "trace_offset": plant(jax.random.randint(key_of[2], (TRACES,), 0, NOFF), jax.random.fold_in(key_of[2], 1), 0, NOFF - 1).astype(jnp.int32),
        "trace_slot": draw_trace_slot(jax.random.fold_in(key_of[8], 71), 0),
        "request_list": draw_request_list(jax.random.fold_in(key_of[8], 71), 0),
        "source_terms": noise(key_of[5], (NSRC, F), 0.5, 3.0, ((0, 8),), jnp.float32),
        "receiver_terms": noise(key_of[6], (NRCV, F), 0.5, 3.0, ((0, 32),), jnp.float32),
        "offset_terms": noise(key_of[7], (NOFF, F), 0.5, 3.0, (), jnp.float32),
    }


def dft_table(samples):
    freq = samples // 2
    index_n = lax.broadcasted_iota(jnp.int32, (samples, freq), 0)
    index_f = lax.broadcasted_iota(jnp.int32, (samples, freq), 1)
    phase = (index_n * index_f % samples).astype(jnp.float32) * (2.0 * math.pi / samples)
    taper = 0.5 - 0.5 * jnp.cos((index_n.astype(jnp.float32) + 0.5) * (2.0 * math.pi / samples))
    scaled = taper / math.sqrt(samples)
    return jnp.concatenate([scaled * jnp.cos(phase), -scaled * jnp.sin(phase)], axis=1).astype(jnp.bfloat16)

def log_amp(block, table):
    freq = table.shape[1] // 2
    spectra = jnp.dot(block, table, preferred_element_type=jnp.float32)
    real_part = spectra[:, :freq]
    imag_part = spectra[:, freq:]
    return 0.5 * jnp.log(real_part * real_part + imag_part * imag_part + 0.01)

def reference(traces, trace_source, trace_offset, trace_slot, request_list, source_terms, receiver_terms, offset_terms):
    table = dft_table(NS)
    blocks = traces.reshape(PEERS, TR_DEV, NS)
    logamp = lax.map(lambda blk: log_amp(blk, table), blocks).reshape(TRACES, F)
    device = (jnp.arange(TRACES, dtype=jnp.int32) // TR_DEV).astype(jnp.int32)
    owner = (trace_slot // CAP).astype(jnp.int32)
    within = (trace_slot % CAP).astype(jnp.int32)
    receiver = (owner * RCV_DEV + request_list[device, owner, within]).astype(jnp.int32)
    residual = logamp - source_terms[trace_source] - receiver_terms[receiver] - offset_terms[trace_offset]
    ones = jnp.ones((TRACES,), jnp.float32)
    src_sum = jax.ops.segment_sum(residual, trace_source, num_segments=NSRC)
    src_cnt = jax.ops.segment_sum(ones, trace_source, num_segments=NSRC)
    rcv_sum = jax.ops.segment_sum(residual, receiver, num_segments=NRCV)
    rcv_cnt = jax.ops.segment_sum(ones, receiver, num_segments=NRCV)
    off_sum = jax.ops.segment_sum(residual, trace_offset, num_segments=NOFF)
    off_cnt = jax.ops.segment_sum(ones, trace_offset, num_segments=NOFF)
    source_new = source_terms + src_sum / (src_cnt + 1.0)[:, None]
    receiver_new = receiver_terms + rcv_sum / (rcv_cnt + 1.0)[:, None]
    offset_new = offset_terms + off_sum / (off_cnt + 1.0)[:, None]
    return (source_new, receiver_new, offset_new)
```

```python
import math

import jax
import jax.numpy as jnp
import numpy as np
from jax import lax
from jax.experimental import pallas as pl
from jax.experimental.pallas import tpu as pltpu
from jax.sharding import PartitionSpec as P

AXES = ("src", "rcv")
LANES = 128
F32 = jnp.float32
BF16 = jnp.bfloat16
NT = (((1,), (1,)), ((), ()))
TN = (((0,), (0,)), ((), ()))
NN = (((1,), (0,)), ((), ()))


def twiddles(samples):
    half = samples // 2
    quarter = samples // 4
    lane = np.arange(LANES)
    even = np.where(lane % 2 == 0, lane, half - 1 + lane)
    odd = np.where(lane % 2 == 1, lane, half - 1 + lane + np.where(lane == 0, LANES, 0))
    freq = np.arange(quarter)
    groups = half // LANES
    unit = 2.0 * math.pi / samples
    base = []
    taper = []
    for rows, fold in ((even, -np.cos(even * quarter * unit)), (odd, np.sin(odd * quarter * unit))):
        phase = (rows[:, None] * freq[None, :] % samples) * unit
        sine = np.sin(phase)
        sine[:, 0] = np.round(fold)
        base += [np.cos(phase), sine]
        at = rows[:, None] + LANES * np.arange(groups)[None, :]
        taper.append((0.5 - 0.5 * np.cos((at + 0.5) * unit)) / math.sqrt(samples))
    turn = (LANES * np.arange(groups)[:, None] * freq[None, :] % samples) * unit
    return (
        np.stack(base).astype(np.float32),
        np.stack([np.cos(turn), np.sin(turn)]).astype(np.float32),
        np.stack(taper).astype(np.float32),
    )


def dot(a, b, dims=NN):
    return lax.dot_general(a, b, dims, preferred_element_type=F32)


def exact(a, b, dims=NN):
    return lax.dot_general(
        a, b, dims, precision=lax.Precision.HIGHEST, preferred_element_type=F32
    )


def iota(shape, axis):
    return lax.broadcasted_iota(jnp.int32, shape, axis)


def hot(mask):
    return jnp.where(mask, 1.0, 0.0).astype(F32)


def ident_rows(num_slot, num_off, rows, slot, off, src):
    at = iota((rows, slot.shape[1]), 0)
    top = at[:num_slot] == slot
    low = at[: rows - num_slot]
    low = (low == off) | (low == src + num_off)
    return jnp.concatenate([hot(top), hot(low)], axis=0).astype(BF16)


def count_kernel(num_off, num_src, rcv_n, where, slot, off, src, lists, sent, counts):
    peers, slots = lists.shape
    num_slot = peers * slots
    rows = counts.shape[0]
    group = where[0]
    src_local = src[...] - group * num_src
    every = ident_rows(num_slot, num_off, rows, slot[...], off[...], src_local)
    width = counts.shape[1]
    at = iota((width, slot.shape[1]), 0)
    joint = hot((at == off[...]) | (at == src_local + num_off)).astype(BF16)
    table = dot(every, joint, NT)
    counts[...] = table
    part = table[:num_slot]
    total = jnp.sum(part, axis=0, keepdims=True)
    row = iota((num_slot, width), 0)
    col = iota((num_slot, width), 1)
    peer = row // slots
    inner = row % slots
    off_rows = num_off // (peers // rcv_n)
    is_off = (col == peer // rcv_n * off_rows + inner) & (inner < off_rows)
    is_src = (col == num_off + inner) & (peer // rcv_n == group) & (inner < num_src)
    num_o = jnp.sum(jnp.where(is_off, total, 0.0), axis=1, keepdims=True)
    num_s = jnp.sum(jnp.where(is_src, total, 0.0), axis=1, keepdims=True)
    spread = hot(iota((num_slot, peers), 0) // slots == iota((num_slot, peers), 1))
    listed = exact(spread, lists[...].astype(F32))
    mine = iota((num_slot, slots), 0) % slots == iota((num_slot, slots), 1)
    asked = jnp.sum(jnp.where(mine, listed, 0.0), axis=1, keepdims=True)
    base = num_off + num_src
    part = jnp.where(col == base, asked, part)
    part = jnp.where(col == base + 1, num_o, part)
    sent[...] = jnp.where(col == base + 2, num_s, part)


def build_table(base, turn, taper, table):
    groups = taper.shape[2]
    for side in range(2):
        for g in range(groups):
            cos0 = base[2 * side]
            sin0 = base[2 * side + 1]
            cos1 = turn[0, g : g + 1, :]
            sin1 = turn[1, g : g + 1, :]
            scale = taper[side, :, g : g + 1]
            at = slice(g * LANES, (g + 1) * LANES)
            table[2 * side, at, :] = ((cos0 * cos1 - sin0 * sin1) * scale).astype(BF16)
            table[2 * side + 1, at, :] = ((sin0 * cos1 + cos0 * sin1) * -scale).astype(BF16)


def main_kernel(
    num_slot, num_off, num_src, chunk,
    where, x, slot, off, src, counts, offset_terms, source_terms, base, turn, taper,
    slot_out, joint_out, table, total, terms,
):
    step = pl.program_id(0)
    rows = counts.shape[0]
    quarter = base.shape[2]
    half = 2 * quarter

    @pl.when(step == 0)
    def _():
        build_table(base, turn, taper, table)
        total[...] = jnp.zeros_like(total)
        terms[...] = jnp.zeros_like(terms)
        terms[:num_off, :] = offset_terms[...]
        terms[num_off : num_off + num_src, :] = source_terms[...]

    src_local = src[...] - where[0] * num_src
    every = ident_rows(num_slot, num_off, rows, slot[...], off[...], src_local)
    lane = iota((x.shape[0], LANES), 1) % 2 == 0
    even = []
    odd = []
    for g in range(half // LANES):
        front = x[:, g * LANES : (g + 1) * LANES]
        back = pltpu.roll(x[:, half + g * LANES : half + (g + 1) * LANES].astype(F32), 1, 1).astype(BF16)
        even.append(jnp.where(lane, front, back))
        odd.append(jnp.where(lane, back, front))
    even = jnp.concatenate(even, axis=1)
    odd = jnp.concatenate(odd, axis=1)
    for c in range(quarter // chunk):
        at = slice(c * chunk, (c + 1) * chunk)
        ec = dot(even, table[0, :, at])
        es = dot(even, table[1, :, at])
        oc = dot(odd, table[2, :, at])
        os = dot(odd, table[3, :, at])
        re_low = ec + oc
        im_low = es + os
        re_high = ec - oc
        im_high = es - os
        if c == 0:
            first = iota((x.shape[0], chunk), 1) == 0
            im_low = jnp.where(first, 0.0, im_low)
            re_high = jnp.where(first, es, re_high)
            im_high = jnp.where(first, os, im_high)
        for k, (re, im) in enumerate(((re_low, im_low), (re_high, im_high))):
            amp = 0.5 * jnp.log(re * re + im * im + 0.01)
            upper = amp.astype(BF16)
            lower = (amp - upper.astype(F32)).astype(BF16)
            to = slice(k * quarter + c * chunk, k * quarter + (c + 1) * chunk)
            total[:, to] += dot(every, upper) + dot(every, lower)

    @pl.when(step == pl.num_programs(0) - 1)
    def _():
        q = iota((quarter, quarter), 0)
        j = iota((quarter, quarter), 1)
        turn_back = hot(q == jnp.where(j == 0, 0, quarter - j)).astype(BF16)
        value = total[:, quarter:]
        one = value.astype(BF16)
        rest = value - one.astype(F32)
        two = rest.astype(BF16)
        three = (rest - two.astype(F32)).astype(BF16)
        natural = dot(one, turn_back) + dot(two, turn_back) + dot(three, turn_back)
        known = exact(counts[...], terms[...])
        low = total[:, :quarter] - known[:, :quarter]
        high = natural - known[:, quarter:]
        slot_out[:, :quarter] = low[:num_slot]
        slot_out[:, quarter:half] = high[:num_slot]
        joint_out[:, :quarter] = low[num_slot:]
        joint_out[:, quarter:] = high[num_slot:]


def owner_hot(got, base, owned):
    num = got.shape[0]
    col = iota(got.shape, 1)
    asked = jnp.sum(jnp.where(col == base, got, 0.0), axis=1, keepdims=True).astype(jnp.int32)
    return hot(iota((num, owned), 1) == asked)


def pack_kernel(num_off, num_src, slots, src_n, rcv_n, where, got, joint, terms, _, out):
    num = got.shape[0]
    width = got.shape[1]
    freq = terms.shape[1]
    owned = terms.shape[0]
    group = where[0]
    sent = got[...]
    chosen = owner_hot(sent, num_off + num_src, owned)
    every_src = src_n * num_src
    col = iota((width, every_src), 0)
    pick = hot(col == num_off + iota((width, every_src), 1) % num_src)
    by_src = exact(sent, pick)
    from_group = iota((num, every_src), 0) // (slots * rcv_n)
    by_src = jnp.where(from_group == iota((num, every_src), 1) // num_src, by_src, 0.0)
    off_of = exact(chosen, sent, TN)[:, :num_off]
    src_of = exact(chosen, by_src, TN)
    off_sum = joint[:num_off, :] - exact(off_of, terms[...], TN)
    src_sum = -exact(src_of, terms[...], TN)
    own = joint[num_off : num_off + num_src, :]
    off_rows = num_off // src_n
    piece = freq // rcv_n
    pad = [] if off_rows == slots else [jnp.zeros((slots - off_rows, piece), F32)]
    for i in range(src_n):
        mine = src_sum[i * num_src : (i + 1) * num_src] + jnp.where(group == i, own, 0.0)
        for m in range(rcv_n):
            to = slice((i * rcv_n + m) * slots, (i * rcv_n + m + 1) * slots)
            at = slice(m * piece, (m + 1) * piece)
            block = off_sum[i * off_rows : (i + 1) * off_rows, at]
            if pad:
                block = jnp.concatenate([block] + pad, axis=0)
            out[to, :piece] = block
            out[to, piece:] = mine[:, at]


def update_kernel(num_off, num_src, slots, piece, sums, got, terms, off_piece, src_piece,
                  rcv_new, off_out, src_out):
    freq = terms.shape[1]
    sent = got[...]
    peers = sent.shape[0] // slots
    base = num_off + num_src
    chosen = owner_hot(sent, base, terms.shape[0])
    col = iota(sent.shape, 1)
    per_slot = jnp.where(col < num_off, sent, 0.0)
    num = jnp.sum(exact(chosen, per_slot, TN), axis=1, keepdims=True)
    total = exact(chosen, sums[:, :freq], TN)
    value = terms[...]
    rcv_new[...] = value + (total - num * value) / (num + 1.0)
    tail = sums[0:slots, freq : freq + 2 * piece]
    both = sent[0:slots]
    for d in range(1, peers):
        tail = tail + sums[d * slots : (d + 1) * slots, freq : freq + 2 * piece]
        both = both + sent[d * slots : (d + 1) * slots]
    col = iota(both.shape, 1)
    num_o = jnp.sum(jnp.where(col == base + 1, both, 0.0), axis=1, keepdims=True)
    num_s = jnp.sum(jnp.where(col == base + 2, both, 0.0), axis=1, keepdims=True)
    off_new = off_piece[...] + tail[:, :piece] / (num_o + 1.0)
    src_out[...] = src_piece[...] + tail[:, piece:] / (num_s + 1.0)
    for d in range(peers):
        off_out[d * slots : (d + 1) * slots, :] = off_new


def swap(value, slots):
    shape = value.shape
    value = value.reshape(shape[0] // slots, slots, shape[1])
    value = lax.all_to_all(value, AXES, split_axis=0, concat_axis=0, tiled=True)
    return value.reshape(shape)


def local(
    traces,
    trace_source,
    trace_offset,
    trace_slot,
    request_list,
    source_terms,
    receiver_terms,
    offset_terms,
):
    src_n = lax.axis_size("src")
    rcv_n = lax.axis_size("rcv")
    peers = src_n * rcv_n
    slots = request_list.shape[2]
    num_tr, samples = traces.shape
    owned, freq = receiver_terms.shape
    num_src = source_terms.shape[0]
    num_off = offset_terms.shape[0]
    num_slot = peers * slots
    joint = -(-(num_off + num_src) // 16) * 16
    rows = num_slot + joint
    width = LANES
    piece = freq // rcv_n
    off_rows = num_off // src_n
    assert slots == num_src and off_rows <= slots and num_off + num_src + 3 <= width
    assert samples == 2 * freq and freq % (2 * LANES) == 0
    src_at = lax.axis_index("src")
    rcv_at = lax.axis_index("rcv")
    where = src_at.astype(jnp.int32).reshape(1)
    slot = trace_slot.reshape(1, num_tr)
    off = trace_offset.reshape(1, num_tr)
    src = trace_source.reshape(1, num_tr)
    smem = pl.BlockSpec(memory_space=pltpu.SMEM)
    vmem = pl.BlockSpec(memory_space=pltpu.VMEM)

    def static(kernel, *args):
        return lambda *refs: kernel(*args, *refs)

    sent, counts = pl.pallas_call(
        static(count_kernel, num_off, num_src, rcv_n),
        out_shape=(
            jax.ShapeDtypeStruct((num_slot, width), F32),
            jax.ShapeDtypeStruct((rows, width), F32),
        ),
        in_specs=[smem] + [vmem] * 4,
        out_specs=(vmem, vmem),
        name="count",
    )(where, slot, off, src, request_list.reshape(peers, slots))
    got = swap(sent, slots)

    base, turn, taper = (jnp.asarray(v) for v in twiddles(samples))
    tile = min(512, num_tr)
    quarter = freq // 2
    whole = lambda *shape: pl.BlockSpec(shape, lambda i: (0,) * len(shape))
    ids = pl.BlockSpec((1, tile), lambda i: (0, i))
    pay, joint_sum = pl.pallas_call(
        static(main_kernel, num_slot, num_off, num_src, min(256, quarter)),
        grid=(num_tr // tile,),
        out_shape=(
            jax.ShapeDtypeStruct((num_slot, freq + 2 * piece), F32),
            jax.ShapeDtypeStruct((joint, freq), F32),
        ),
        in_specs=[
            smem,
            pl.BlockSpec((tile, samples), lambda i: (i, 0)),
            ids, ids, ids,
            whole(rows, width),
            whole(num_off, freq),
            whole(num_src, freq),
            whole(*base.shape), whole(*turn.shape), whole(*taper.shape),
        ],
        out_specs=(whole(num_slot, freq), whole(joint, freq)),
        scratch_shapes=[
            pltpu.VMEM((4, freq, quarter), BF16),
            pltpu.VMEM((rows, freq), F32),
            pltpu.VMEM((width, freq), F32),
        ],
        compiler_params=pltpu.CompilerParams(
            dimension_semantics=("arbitrary",), vmem_limit_bytes=48 * 2**20
        ),
        name="spectra",
    )(where, traces, slot, off, src, counts, offset_terms, source_terms, base, turn, taper)

    pay = pl.pallas_call(
        static(pack_kernel, num_off, num_src, slots, src_n, rcv_n),
        grid=(1,),
        out_shape=jax.ShapeDtypeStruct(pay.shape, F32),
        in_specs=[
            smem, whole(num_slot, width), whole(joint, freq), whole(owned, freq),
            pl.BlockSpec(memory_space=pl.ANY),
        ],
        out_specs=pl.BlockSpec((num_slot, 2 * piece), lambda i: (0, freq // (2 * piece))),
        input_output_aliases={4: 0},
        name="pack",
    )(where, got, joint_sum, receiver_terms, pay)
    sums = swap(pay, slots)

    off_piece = lax.dynamic_slice(
        offset_terms, (src_at * off_rows, rcv_at * piece), (off_rows, piece)
    )
    off_piece = jnp.pad(off_piece, ((0, slots - off_rows), (0, 0)))
    src_piece = lax.dynamic_slice(source_terms, (0, rcv_at * piece), (num_src, piece))
    receiver_new, off_new, src_new = pl.pallas_call(
        static(update_kernel, num_off, num_src, slots, piece),
        out_shape=(
            jax.ShapeDtypeStruct((owned, freq), F32),
            jax.ShapeDtypeStruct((num_slot, piece), F32),
            jax.ShapeDtypeStruct((num_src, piece), F32),
        ),
        in_specs=[vmem] * 5,
        out_specs=(vmem, vmem, vmem),
        name="update",
    )(sums, got, receiver_terms, off_piece, src_piece)

    parts = [src_new]
    for k in range(1, rcv_n):
        ring = [(j, (j + k) % rcv_n) for j in range(rcv_n)]
        parts.append(lax.ppermute(src_new, "rcv", ring))
    source_new = jnp.zeros((num_src, freq), F32)
    for k, part in enumerate(parts):
        at = (rcv_at - k) % rcv_n
        source_new = lax.dynamic_update_slice(source_new, part, (0, at * piece))
    every = swap(off_new, slots).reshape(src_n, rcv_n, slots, piece)[:, :, :off_rows]
    offset_new = every.transpose(0, 2, 1, 3).reshape(num_off, freq)
    return (source_new, receiver_new, offset_new)


def solution(mesh):
    return jax.shard_map(
        local,
        mesh=mesh,
        in_specs=(
            P(AXES, None),
            P(AXES),
            P(AXES),
            P(AXES),
            P(AXES, None, None),
            P("src", None),
            P(AXES, None),
            P(),
        ),
        out_specs=(P("src", None), P(AXES, None), P()),
        check_vma=False,
    )
```

```python
import math

import jax
import jax.numpy as jnp
import numpy as np
from jax import lax
from jax.experimental import pallas as pl
from jax.experimental.pallas import tpu as pltpu
from jax.sharding import PartitionSpec as P

AXES = ("src", "rcv")
LANES = 128
F32 = jnp.float32
BF16 = jnp.bfloat16
NT = (((1,), (1,)), ((), ()))
TN = (((0,), (0,)), ((), ()))
NN = (((1,), (0,)), ((), ()))


def twiddles(samples, first, last):
    half = samples // 2
    quarter = samples // 4
    lane = np.arange(LANES)
    even = np.where(lane % 2 == 0, lane, half - 1 + lane)
    odd = np.where(lane % 2 == 1, lane, half - 1 + lane + np.where(lane == 0, LANES, 0))
    freq = np.arange(quarter)
    groups = half // LANES
    unit = 2.0 * math.pi / samples
    base = []
    taper = []
    for rows, fold in ((even, -np.cos(even * quarter * unit)), (odd, np.sin(odd * quarter * unit))):
        phase = (rows[:, None] * freq[None, :] % samples) * unit
        sine = np.sin(phase)
        sine[:, 0] = np.round(fold)
        base += [np.cos(phase), sine]
        at = rows[:, None] + LANES * np.arange(groups)[None, :]
        taper.append((0.5 - 0.5 * np.cos((at + 0.5) * unit)) / math.sqrt(samples))
    turn = (LANES * np.arange(groups)[:, None] * freq[None, :] % samples) * unit
    turn = np.stack([np.cos(turn), np.sin(turn)])
    return (
        np.stack(base)[:, :, first:last].astype(np.float32),
        turn[:, :, first:last].astype(np.float32),
        np.stack(taper).astype(np.float32),
    )


def dot(a, b, dims=NN):
    return lax.dot_general(a, b, dims, preferred_element_type=F32)


def exact(a, b, dims=NN):
    return lax.dot_general(
        a, b, dims, precision=lax.Precision.HIGHEST, preferred_element_type=F32
    )


def iota(shape, axis):
    return lax.broadcasted_iota(jnp.int32, shape, axis)


def hot(mask):
    return jnp.where(mask, 1.0, 0.0).astype(F32)


def reorder(value, width=None):
    half = value.shape[1]
    width = width or (0, half)
    row = iota((half, width[1] - width[0]), 0)
    col = iota(row.shape, 1) + width[0]
    pick = hot(row == jnp.where(col == 0, 0, half - col)).astype(BF16)
    one = value.astype(BF16)
    rest = value - one.astype(F32)
    two = rest.astype(BF16)
    three = (rest - two.astype(F32)).astype(BF16)
    return dot(one, pick) + dot(two, pick) + dot(three, pick)


def natural(low0, high0, low1, high1):
    return jnp.concatenate(
        [low0, low1, reorder(jnp.concatenate([high0, high1], axis=1))], axis=1
    )


def start(copies):
    for copy in copies:
        copy.start()


def wait(copies):
    for copy in copies:
        copy.wait()


def build_table(base, turn, taper, table):
    groups = taper.shape[2]
    width = base.shape[2]
    for side in range(2):
        for g in range(groups):
            cos0 = base[2 * side]
            sin0 = base[2 * side + 1]
            cos1 = turn[0, g : g + 1, :]
            sin1 = turn[1, g : g + 1, :]
            scale = taper[side, :, g : g + 1]
            at = slice(g * LANES, (g + 1) * LANES)
            table[side, at, :width] = ((cos0 * cos1 - sin0 * sin1) * scale).astype(BF16)
            table[side, at, width:] = ((sin0 * cos1 + cos0 * sin1) * -scale).astype(BF16)


def ident_rows(num_slot, num_off, rows, slot, off, src):
    top = iota((num_slot, slot.shape[1]), 0) == slot
    low = iota((rows - num_slot, slot.shape[1]), 0)
    low = (low == off) | (low == src + num_off)
    return jnp.concatenate([hot(top).astype(BF16), hot(low).astype(BF16)], axis=0)


def sum_tiles(x, copies, every, table, total, tile, has_first):
    samples = x.shape[1]
    half = samples // 2
    width = table.shape[2] // 2
    total[...] = jnp.zeros_like(total)
    for t in range(x.shape[0] // tile):
        copies[t].wait()

    def step(t, _):
        rows = pl.ds(pl.multiple_of(t * tile, tile), tile)
        lane = iota((tile, LANES), 1) % 2 == 0
        even = []
        odd = []
        for g in range(half // LANES):
            front = x[rows, g * LANES : (g + 1) * LANES]
            back = x[rows, half + g * LANES : half + (g + 1) * LANES]
            back = pltpu.roll(back.astype(F32), 1, 1).astype(BF16)
            even.append(jnp.where(lane, front, back))
            odd.append(jnp.where(lane, back, front))
        even = dot(jnp.concatenate(even, axis=1), table[0])
        odd = dot(jnp.concatenate(odd, axis=1), table[1])
        ec, es = even[:, :width], even[:, width:]
        oc, os = odd[:, :width], odd[:, width:]
        re_low, im_low = ec + oc, es + os
        re_high, im_high = ec - oc, es - os
        if has_first:
            first = iota((tile, width), 1) == 0
            im_low = jnp.where(first, 0.0, im_low)
            re_high = jnp.where(first, es, re_high)
            im_high = jnp.where(first, os, im_high)
        ids = every[:, rows]
        for k, (re, im) in enumerate(((re_low, im_low), (re_high, im_high))):
            amp = 0.5 * jnp.log(re * re + im * im + 0.01)
            upper = amp.astype(BF16)
            lower = (amp - upper.astype(F32)).astype(BF16)
            total[:, k * width : (k + 1) * width] += dot(ids, upper) + dot(ids, lower)
        return 0

    lax.fori_loop(0, x.shape[0] // tile, step, 0)


def known_terms(terms, low, width):
    half = terms.shape[1] // 2
    return jnp.concatenate(
        [terms[:, low : low + width], reorder(terms[:, half:], (low, low + width))], axis=1
    )


def spectra_kernel(
    num_off, num_src, rcv_n, first, tile,
    where, x_hbm, slot_hbm, off_hbm, src_hbm, lists_hbm, offset_hbm, source_hbm, own_hbm,
    base_hbm, turn_hbm, taper_hbm, pay_hbm, joint_hbm, own_out_hbm,
    x, ids, lists, terms, own, base, turn, taper, table, every, total, stage, own_out, sems, x_sems,
):
    slots, peers = lists.shape
    num_slot = peers * slots
    rows = total.shape[0]
    width = base.shape[2]
    lead = first == 0
    group = where[0]
    near = [
        pltpu.make_async_copy(slot_hbm, ids.at[0], sems.at[0]),
        pltpu.make_async_copy(off_hbm, ids.at[1], sems.at[1]),
        pltpu.make_async_copy(src_hbm, ids.at[2], sems.at[2]),
        pltpu.make_async_copy(base_hbm, base, sems.at[3]),
        pltpu.make_async_copy(turn_hbm, turn, sems.at[4]),
        pltpu.make_async_copy(taper_hbm, taper, sems.at[5]),
    ]
    tiles = [
        pltpu.make_async_copy(x_hbm.at[t * tile : (t + 1) * tile], x.at[t * tile : (t + 1) * tile], x_sems.at[t])
        for t in range(x.shape[0] // tile)
    ]
    far = [
        pltpu.make_async_copy(lists_hbm, lists, sems.at[6]),
        pltpu.make_async_copy(offset_hbm, terms.at[0:num_off], sems.at[7]),
        pltpu.make_async_copy(source_hbm, terms.at[num_off : num_off + num_src], sems.at[8]),
        pltpu.make_async_copy(own_hbm, own, sems.at[9]),
    ]
    start(near + tiles + far)
    spare = num_off + num_src
    terms[spare:, :] = jnp.zeros((terms.shape[0] - spare, terms.shape[1]), F32)
    wait(near)
    src = ids[2] - group * num_src
    every[...] = ident_rows(num_slot, num_off, rows, ids[0], ids[1], src)
    at = iota((LANES, x.shape[0]), 0)
    joint = hot((at == ids[1]) | (at == src + num_off)).astype(BF16)
    counts = dot(every[...], joint, NT)
    build_table(base, turn, taper, table)
    wait(far)
    known = exact(counts, known_terms(terms[...], first, width))
    sum_tiles(x, tiles, every, table, total, tile, lead)
    stage[:, : 2 * width] = total[...] - known
    out = []
    if lead:
        part = counts[:num_slot]
        whole = jnp.sum(part, axis=0, keepdims=True)
        row = iota((num_slot, LANES), 0)
        col = iota((num_slot, LANES), 1)
        peer = row // slots
        inner = row % slots
        off_rows = num_off // (peers // rcv_n)
        is_off = (col == peer // rcv_n * off_rows + inner) & (inner < off_rows)
        is_src = (col == num_off + inner) & (peer // rcv_n == group) & (inner < num_src)
        num_o = jnp.sum(jnp.where(is_off, whole, 0.0), axis=1, keepdims=True)
        num_s = jnp.sum(jnp.where(is_src, whole, 0.0), axis=1, keepdims=True)
        spread = hot(iota((num_slot, peers), 0) // slots == iota((num_slot, peers), 1))
        listed = exact(spread, lists[...].astype(F32), NT)
        mine = iota((num_slot, slots), 0) % slots == iota((num_slot, slots), 1)
        asked = jnp.sum(jnp.where(mine, listed, 0.0), axis=1, keepdims=True)
        part = jnp.where(col == spare, asked, part)
        part = jnp.where(col == spare + 1, num_o, part)
        stage[:num_slot, 2 * width :] = jnp.where(col == spare + 2, num_s, part)
        out.append(pltpu.make_async_copy(stage.at[:num_slot], pay_hbm, sems.at[0]))
    else:
        half = 2 * width
        kept = own[...]
        own_out[:, :half] = known_terms(kept, 0, width)
        own_out[:, half:] = known_terms(kept, first, width)
        out.append(
            pltpu.make_async_copy(stage.at[:num_slot, :half], pay_hbm.at[:, :half], sems.at[0])
        )
        out.append(pltpu.make_async_copy(own_out, own_out_hbm, sems.at[2]))
    out.append(
        pltpu.make_async_copy(stage.at[num_slot:, : 2 * width], joint_hbm, sems.at[1])
    )
    start(out)
    wait(out)


def owner_hot(sent, base, owned):
    col = iota(sent.shape, 1)
    asked = jnp.sum(jnp.where(col == base, sent, 0.0), axis=1, keepdims=True).astype(jnp.int32)
    return hot(iota((sent.shape[0], owned), 1) == asked)


def pack_kernel(
    num_off, num_src, slots, src_n, rcv_n, where, got_hbm, joint0_hbm, joint1_hbm, own_hbm, _,
    out_hbm, got, joint, own, out, sems,
):
    half = joint0_hbm.shape[1]
    freq = 2 * half
    copies = [
        pltpu.make_async_copy(got_hbm.at[:, half : half + LANES], got, sems.at[0]),
        pltpu.make_async_copy(joint0_hbm, joint.at[:, :half], sems.at[1]),
        pltpu.make_async_copy(joint1_hbm, joint.at[:, half:], sems.at[2]),
        pltpu.make_async_copy(own_hbm, own, sems.at[3]),
    ]
    start(copies)
    wait(copies)
    num = got.shape[0]
    group = where[0]
    sent = got[...]
    chosen = owner_hot(sent, num_off + num_src, own.shape[0])
    every_src = src_n * num_src
    col = iota((LANES, every_src), 0)
    pick = hot(col == num_off + iota((LANES, every_src), 1) % num_src)
    by_src = exact(sent, pick)
    from_group = iota((num, every_src), 0) // (slots * rcv_n)
    by_src = jnp.where(from_group == iota((num, every_src), 1) // num_src, by_src, 0.0)
    off_of = exact(chosen, sent, TN)[:, :num_off]
    src_of = exact(chosen, by_src, TN)
    off_sum = joint[:num_off, :] - exact(off_of, own[...], TN)
    src_sum = -exact(src_of, own[...], TN)
    mine = joint[num_off : num_off + num_src, :]
    off_rows = num_off // src_n
    piece = freq // rcv_n
    pad = [] if off_rows == slots else [jnp.zeros((slots - off_rows, piece), F32)]
    for i in range(src_n):
        source = src_sum[i * num_src : (i + 1) * num_src] + jnp.where(group == i, mine, 0.0)
        for m in range(rcv_n):
            to = slice((i * rcv_n + m) * slots, (i * rcv_n + m + 1) * slots)
            at = slice(m * piece, (m + 1) * piece)
            block = off_sum[i * off_rows : (i + 1) * off_rows, at]
            if pad:
                block = jnp.concatenate([block] + pad, axis=0)
            out[to, :piece] = block
            out[to, piece:] = source[:, at]
    copy = pltpu.make_async_copy(out, out_hbm.at[:, half : half + 2 * piece], sems.at[0])
    copy.start()
    copy.wait()


def shares_kernel(num_off, num_src, slots, got_hbm, sums_hbm, off_out, src_out, sent, tail, sems):
    piece = src_out.shape[1]
    at = got_hbm.shape[1] - LANES
    copies = [
        pltpu.make_async_copy(got_hbm.at[:, at:], sent, sems.at[0]),
        pltpu.make_async_copy(sums_hbm.at[:, at:], tail, sems.at[1]),
    ]
    start(copies)
    wait(copies)
    peers = sent.shape[0] // slots
    base = num_off + num_src
    both = sent[0:slots]
    value = tail[0:slots]
    for d in range(1, peers):
        both = both + sent[d * slots : (d + 1) * slots]
        value = value + tail[d * slots : (d + 1) * slots]
    col = iota(both.shape, 1)
    num_o = jnp.sum(jnp.where(col == base + 1, both, 0.0), axis=1, keepdims=True)
    num_s = jnp.sum(jnp.where(col == base + 2, both, 0.0), axis=1, keepdims=True)
    off_new = value[:, :piece] / (num_o + 1.0)
    src_out[...] = value[:, piece:] / (num_s + 1.0)
    for d in range(peers):
        off_out[d * slots : (d + 1) * slots, :] = off_new


def receiver_kernel(num_off, num_src, got_hbm, sums_hbm, terms_hbm, out, got, sums, terms, sems):
    half = got.shape[1] - LANES
    copies = [
        pltpu.make_async_copy(got_hbm, got, sems.at[0]),
        pltpu.make_async_copy(sums_hbm.at[:, :half], sums, sems.at[1]),
        pltpu.make_async_copy(terms_hbm, terms, sems.at[2]),
    ]
    start(copies)
    wait(copies)
    sent = got[:, half:]
    value = terms[...]
    chosen = owner_hot(sent, num_off + num_src, value.shape[0])
    per_slot = jnp.where(iota(sent.shape, 1) < num_off, sent, 0.0)
    num = jnp.sum(exact(chosen, per_slot, TN), axis=1, keepdims=True)
    one = exact(chosen, got[:, :half], TN)
    two = exact(chosen, sums[...], TN)
    width = half // 2
    total = natural(one[:, :width], one[:, width:], two[:, :width], two[:, width:])
    out[...] = value + (total - num * value) / (num + 1.0)


def final_kernel(src_n, rcv_n, off_rows, slots, where, every_hbm, source, offset, *refs):
    src_out, off_out, every, rest, sems = refs[rcv_n:]
    copies = [pltpu.make_async_copy(refs[k], rest.at[k], sems.at[k]) for k in range(rcv_n)]
    copy = pltpu.make_async_copy(every_hbm, every, sems.at[rcv_n])
    start([copy] + copies)
    wait(copies)
    piece = every.shape[1]
    here = where[1]
    parts = []
    for j in range(rcv_n):
        value = jnp.zeros(rest.shape[1:], F32)
        for k in range(rcv_n):
            value = value + jnp.where((here + rcv_n - k) % rcv_n == j, rest[k], 0.0)
        parts.append(value)

    def columns(parts):
        whole = jnp.concatenate(parts, axis=1)
        width = whole.shape[1] // 4
        return natural(*(whole[:, k * width : (k + 1) * width] for k in range(4)))

    src_out[...] = source[...] + columns(parts)
    copy.wait()
    parts = []
    for m in range(rcv_n):
        at = [(i * rcv_n + m) * slots for i in range(src_n)]
        parts.append(jnp.concatenate([every[a : a + off_rows, :] for a in at], axis=0))
    off_out[...] = offset[...] + columns(parts)


def swap(value, slots):
    shape = value.shape
    value = value.reshape(shape[0] // slots, slots, shape[1])
    value = lax.all_to_all(value, AXES, split_axis=0, concat_axis=0, tiled=True)
    return value.reshape(shape)


def local(
    traces,
    trace_source,
    trace_offset,
    trace_slot,
    request_list,
    source_terms,
    receiver_terms,
    offset_terms,
):
    src_n = lax.axis_size("src")
    rcv_n = lax.axis_size("rcv")
    peers = src_n * rcv_n
    slots = request_list.shape[2]
    num_tr, samples = traces.shape
    owned, freq = receiver_terms.shape
    num_src = source_terms.shape[0]
    num_off = offset_terms.shape[0]
    num_slot = peers * slots
    joint = -(-(num_off + num_src) // 16) * 16
    rows = num_slot + joint
    half = freq // 2
    width = half // 2
    piece = freq // rcv_n
    off_rows = num_off // src_n
    tile = min(512, num_tr)
    assert slots == num_src and off_rows <= slots and num_off + num_src + 3 <= LANES
    assert samples == 2 * freq and freq % (4 * LANES) == 0 and 2 * piece == half
    where = jnp.stack([lax.axis_index("src"), lax.axis_index("rcv")]).astype(jnp.int32)
    ids = [v.reshape(1, num_tr) for v in (trace_slot, trace_offset, trace_source)]
    lists = jnp.swapaxes(request_list, 1, 2).reshape(slots, peers)
    smem = pl.BlockSpec(memory_space=pltpu.SMEM)
    vmem = pl.BlockSpec(memory_space=pltpu.VMEM)
    hbm = pl.BlockSpec(memory_space=pltpu.HBM)
    anywhere = pl.BlockSpec(memory_space=pl.ANY)

    def static(kernel, *args):
        return lambda *refs: kernel(*args, *refs)

    def shape(*dims):
        return jax.ShapeDtypeStruct(dims, F32)

    def spectra(first):
        consts = [jnp.asarray(v) for v in twiddles(samples, first, first + width)]
        pay = half + LANES if first == 0 else half + 2 * piece
        return pl.pallas_call(
            static(spectra_kernel, num_off, num_src, rcv_n, first, tile),
            out_shape=(shape(num_slot, pay), shape(joint, half), shape(owned, freq)),
            in_specs=[smem] + [hbm] * 11,
            out_specs=(hbm, hbm, hbm),
            scratch_shapes=[
                pltpu.VMEM((num_tr, samples), BF16),
                pltpu.VMEM((3, 1, num_tr), jnp.int32),
                pltpu.VMEM((slots, peers), jnp.int32),
                pltpu.VMEM((LANES, freq), F32),
                pltpu.VMEM((owned, freq), F32),
                pltpu.VMEM(consts[0].shape, F32),
                pltpu.VMEM(consts[1].shape, F32),
                pltpu.VMEM(consts[2].shape, F32),
                pltpu.VMEM((2, freq, half), BF16),
                pltpu.VMEM((rows, num_tr), BF16),
                pltpu.VMEM((rows, half), F32),
                pltpu.VMEM((rows, half + LANES), F32),
                pltpu.VMEM((owned, freq), F32),
                pltpu.SemaphoreType.DMA((10,)),
                pltpu.SemaphoreType.DMA((num_tr // tile,)),
            ],
            compiler_params=pltpu.CompilerParams(vmem_limit_bytes=56 * 2**20),
            name="spectra%d" % first,
        )(where, traces, *ids, lists, offset_terms, source_terms, receiver_terms, *consts)

    pay, joint0, _ = spectra(0)
    got = swap(pay, slots)
    pay, joint1, own = spectra(width)
    pay = pl.pallas_call(
        static(pack_kernel, num_off, num_src, slots, src_n, rcv_n),
        out_shape=shape(*pay.shape),
        in_specs=[smem, anywhere] + [hbm] * 4,
        out_specs=hbm,
        scratch_shapes=[
            pltpu.VMEM((num_slot, LANES), F32),
            pltpu.VMEM((joint, freq), F32),
            pltpu.VMEM((owned, freq), F32),
            pltpu.VMEM((num_slot, 2 * piece), F32),
            pltpu.SemaphoreType.DMA((4,)),
        ],
        input_output_aliases={5: 0},
        name="pack",
    )(where, got, joint0, joint1, own, pay)
    sums = swap(pay, slots)

    off_new, src_new = pl.pallas_call(
        static(shares_kernel, num_off, num_src, slots),
        out_shape=(shape(num_slot, piece), shape(num_src, piece)),
        in_specs=[anywhere, anywhere],
        out_specs=(vmem, vmem),
        scratch_shapes=[
            pltpu.VMEM((num_slot, LANES), F32),
            pltpu.VMEM((num_slot, 2 * piece), F32),
            pltpu.SemaphoreType.DMA((2,)),
        ],
        name="shares",
    )(got, sums)
    every = swap(off_new, slots)
    parts = [src_new]
    for k in range(1, rcv_n):
        ring = [(j, (j + k) % rcv_n) for j in range(rcv_n)]
        parts.append(lax.ppermute(src_new, "rcv", ring))
    receiver_new = pl.pallas_call(
        static(receiver_kernel, num_off, num_src),
        out_shape=shape(owned, freq),
        in_specs=[anywhere, anywhere, hbm],
        out_specs=vmem,
        scratch_shapes=[
            pltpu.VMEM((num_slot, half + LANES), F32),
            pltpu.VMEM((num_slot, half), F32),
            pltpu.VMEM((owned, freq), F32),
            pltpu.SemaphoreType.DMA((3,)),
        ],
        name="receiver",
    )(got, sums, receiver_terms)
    source_new, offset_new = pl.pallas_call(
        static(final_kernel, src_n, rcv_n, off_rows, slots),
        out_shape=(shape(num_src, freq), shape(num_off, freq)),
        in_specs=[smem, anywhere, vmem, vmem] + [anywhere] * rcv_n,
        out_specs=(vmem, vmem),
        scratch_shapes=[
            pltpu.VMEM((num_slot, piece), F32),
            pltpu.VMEM((rcv_n, num_src, piece), F32),
            pltpu.SemaphoreType.DMA((rcv_n + 1,)),
        ],
        name="final",
    )(where, every, source_terms, offset_terms, *parts)
    return (source_new, receiver_new, offset_new)


def solution(mesh):
    return jax.shard_map(
        local,
        mesh=mesh,
        in_specs=(
            P(AXES, None),
            P(AXES),
            P(AXES),
            P(AXES),
            P(AXES, None, None),
            P("src", None),
            P(AXES, None),
            P(),
        ),
        out_specs=(P("src", None), P(AXES, None), P()),
        check_vma=False,
    )
```

```python
import math

import jax
import jax.numpy as jnp
import numpy as np
from jax import lax
from jax.experimental import pallas as pl
from jax.experimental.pallas import tpu as pltpu
from jax.sharding import PartitionSpec as P

AXES = ("src", "rcv")
LANES = 128
F32 = jnp.float32
BF16 = jnp.bfloat16
NT = (((1,), (1,)), ((), ()))
TN = (((0,), (0,)), ((), ()))
NN = (((1,), (0,)), ((), ()))


def twiddles(samples, first, last):
    half = samples // 2
    quarter = samples // 4
    lane = np.arange(LANES)
    even = np.where(lane % 2 == 0, lane, half - 1 + lane)
    odd = np.where(lane % 2 == 1, lane, half - 1 + lane + np.where(lane == 0, LANES, 0))
    freq = np.arange(quarter)
    groups = half // LANES
    unit = 2.0 * math.pi / samples
    base = []
    taper = []
    for rows, fold in ((even, -np.cos(even * quarter * unit)), (odd, np.sin(odd * quarter * unit))):
        phase = (rows[:, None] * freq[None, :] % samples) * unit
        sine = np.sin(phase)
        sine[:, 0] = np.round(fold)
        base += [np.cos(phase), sine]
        at = rows[:, None] + LANES * np.arange(groups)[None, :]
        taper.append((0.5 - 0.5 * np.cos((at + 0.5) * unit)) / math.sqrt(samples))
    turn = (LANES * np.arange(groups)[:, None] * freq[None, :] % samples) * unit
    turn = np.stack([np.cos(turn), np.sin(turn)])
    return (
        np.stack(base)[:, :, first:last].astype(np.float32),
        turn[:, :, first:last].astype(np.float32),
        np.stack(taper).astype(np.float32),
    )


def dot(a, b, dims=NN):
    return lax.dot_general(a, b, dims, preferred_element_type=F32)


def exact(a, b, dims=NN):
    return lax.dot_general(
        a, b, dims, precision=lax.Precision.HIGHEST, preferred_element_type=F32
    )


def iota(shape, axis):
    return lax.broadcasted_iota(jnp.int32, shape, axis)


def hot(mask):
    return jnp.where(mask, 1.0, 0.0).astype(F32)


def ascend(value, lead):
    width = value.shape[1]
    row = iota((width, width), 0)
    col = iota((width, width), 1)
    if lead:
        pick = row == jnp.where(col == 0, 0, width - col)
    else:
        pick = row == width - 1 - col
    pick = hot(pick).astype(BF16)
    one = value.astype(BF16)
    rest = value - one.astype(F32)
    two = rest.astype(BF16)
    three = (rest - two.astype(F32)).astype(BF16)
    return dot(one, pick) + dot(two, pick) + dot(three, pick)


def join(low0, high0, low1, high1):
    edge = high1.shape[1]
    whole = jnp.concatenate([high1, high0], axis=1)
    col = iota(whole.shape, 1)
    shifted = pltpu.roll(whole, 1, 1)
    high = jnp.where(col <= edge, shifted, whole)
    high = jnp.where(col == 0, high0[:, :1], high)
    return jnp.concatenate([low0, low1, high], axis=1)


def part_of(value, first, width):
    half = value.shape[1] // 2
    high = value[:, half:]
    if first == 0:
        tail = high[:, half - width :]
        tail = jnp.where(iota(tail.shape, 1) == 0, high[:, :1], tail)
    else:
        tail = pltpu.roll(high, half - 1, 1)[:, :width]
    return jnp.concatenate([value[:, first : first + width], tail], axis=1)


def start(copies):
    for copy in copies:
        copy.start()


def wait(copies):
    for copy in copies:
        copy.wait()


def build_table(base, turn, taper, table):
    groups = taper.shape[2]
    width = base.shape[2]
    for side in range(2):
        for g in range(groups):
            cos0 = base[2 * side]
            sin0 = base[2 * side + 1]
            cos1 = turn[0, g : g + 1, :]
            sin1 = turn[1, g : g + 1, :]
            scale = taper[side, :, g : g + 1]
            at = slice(g * LANES, (g + 1) * LANES)
            table[side, at, :width] = ((cos0 * cos1 - sin0 * sin1) * scale).astype(BF16)
            table[side, at, width:] = ((sin0 * cos1 + cos0 * sin1) * -scale).astype(BF16)


def ident_rows(num_slot, num_off, rows, slot, off, src):
    top = iota((num_slot, slot.shape[1]), 0) == slot
    low = iota((rows - num_slot, slot.shape[1]), 0)
    low = (low == off) | (low == src + num_off)
    return jnp.concatenate([hot(top).astype(BF16), hot(low).astype(BF16)], axis=0)


def spectra_kernel(
    num_off, num_src, rcv_n, first, tile,
    x_hbm, slot_hbm, off_hbm, src_hbm, lists_hbm, offset_hbm, source_hbm, own_hbm,
    counts_hbm, base_hbm, turn_hbm, taper_hbm, pay_hbm, joint_hbm, extra_hbm,
    x, ids, lists, terms, own, counts, base, turn, taper, table, total, stage, sems, x_sems,
):
    slots, peers = lists.shape
    num_slot = peers * slots
    rows = total.shape[0]
    width = base.shape[2]
    half = x.shape[1] // 2
    lead = first == 0
    group = lax.axis_index("src")
    near = [
        pltpu.make_async_copy(base_hbm, base, sems.at[0]),
        pltpu.make_async_copy(turn_hbm, turn, sems.at[1]),
        pltpu.make_async_copy(taper_hbm, taper, sems.at[2]),
    ]
    far = [
        pltpu.make_async_copy(slot_hbm, ids.at[0], sems.at[3]),
        pltpu.make_async_copy(off_hbm, ids.at[1], sems.at[4]),
        pltpu.make_async_copy(src_hbm, ids.at[2], sems.at[5]),
        pltpu.make_async_copy(offset_hbm, terms.at[0:num_off], sems.at[6]),
        pltpu.make_async_copy(source_hbm, terms.at[num_off : num_off + num_src], sems.at[7]),
    ]
    if lead:
        far.append(pltpu.make_async_copy(lists_hbm, lists, sems.at[8]))
    else:
        far.append(pltpu.make_async_copy(own_hbm, own, sems.at[8]))
        far.append(pltpu.make_async_copy(counts_hbm, counts, sems.at[9]))
    tiles = [
        pltpu.make_async_copy(
            x_hbm.at[t * tile : (t + 1) * tile], x.at[t * tile : (t + 1) * tile], x_sems.at[t]
        )
        for t in range(x.shape[0] // tile)
    ]
    start(near + tiles[:1] + far + tiles[1:])
    spare = num_off + num_src
    terms[spare:, :] = jnp.zeros((terms.shape[0] - spare, terms.shape[1]), F32)
    total[...] = jnp.zeros_like(total)
    if lead:
        counts[...] = jnp.zeros_like(counts)
    wait(near)
    build_table(base, turn, taper, table)
    wait(far + tiles)

    def step(t, _):
        at = pl.ds(pl.multiple_of(t * tile, tile), tile)
        slot, off = ids[0, :, at], ids[1, :, at]
        src = ids[2, :, at] - group * num_src
        every = ident_rows(num_slot, num_off, rows, slot, off, src)
        if lead:
            col = iota((LANES, tile), 0)
            counts[...] += dot(
                every, hot((col == off) | (col == src + num_off)).astype(BF16), NT
            )
        lane = iota((tile, LANES), 1) % 2 == 0
        even = []
        odd = []
        for g in range(half // LANES):
            front = x[at, g * LANES : (g + 1) * LANES]
            back = x[at, half + g * LANES : half + (g + 1) * LANES]
            back = pltpu.roll(back.astype(F32), 1, 1).astype(BF16)
            even.append(jnp.where(lane, front, back))
            odd.append(jnp.where(lane, back, front))
        even = dot(jnp.concatenate(even, axis=1), table[0])
        odd = dot(jnp.concatenate(odd, axis=1), table[1])
        ec, es = even[:, :width], even[:, width:]
        oc, os = odd[:, :width], odd[:, width:]
        re_low, im_low = ec + oc, es + os
        re_high, im_high = ec - oc, es - os
        if lead:
            zero = iota((tile, width), 1) == 0
            im_low = jnp.where(zero, 0.0, im_low)
            re_high = jnp.where(zero, es, re_high)
            im_high = jnp.where(zero, os, im_high)
        for k, (re, im) in enumerate(((re_low, im_low), (re_high, im_high))):
            amp = 0.5 * jnp.log(re * re + im * im + 0.01)
            upper = amp.astype(BF16)
            lower = (amp - upper.astype(F32)).astype(BF16)
            total[:, k * width : (k + 1) * width] += dot(every, upper) + dot(every, lower)
        return 0

    lax.fori_loop(0, x.shape[0] // tile, step, 0)
    known = exact(counts[...], part_of(terms[...], first, width))
    stage[:, :width] = total[:, :width] - known[:, :width]
    stage[:, width : 2 * width] = ascend(total[:, width:], lead) - known[:, width:]
    out = [
        pltpu.make_async_copy(
            stage.at[:num_slot, : 2 * width], pay_hbm.at[:, : 2 * width], sems.at[0]
        ),
        pltpu.make_async_copy(stage.at[num_slot:, : 2 * width], joint_hbm, sems.at[1]),
    ]
    start(out)
    if lead:
        part = counts[:num_slot]
        whole = jnp.sum(part, axis=0, keepdims=True)
        row = iota((num_slot, LANES), 0)
        col = iota((num_slot, LANES), 1)
        peer = row // slots
        inner = row % slots
        off_rows = num_off // (peers // rcv_n)
        is_off = (col == peer // rcv_n * off_rows + inner) & (inner < off_rows)
        is_src = (col == num_off + inner) & (peer // rcv_n == group) & (inner < num_src)
        num_o = jnp.sum(jnp.where(is_off, whole, 0.0), axis=1, keepdims=True)
        num_s = jnp.sum(jnp.where(is_src, whole, 0.0), axis=1, keepdims=True)
        spread = hot(iota((num_slot, peers), 0) // slots == iota((num_slot, peers), 1))
        listed = dot(spread.astype(BF16), lists[...].astype(F32).astype(BF16), NT)
        mine = iota((num_slot, slots), 0) % slots == iota((num_slot, slots), 1)
        asked = jnp.sum(jnp.where(mine, listed, 0.0), axis=1, keepdims=True)
        part = jnp.where(col == spare, asked, part)
        part = jnp.where(col == spare + 1, num_o, part)
        stage[:num_slot, 2 * width :] = jnp.where(col == spare + 2, num_s, part)
        last = [
            pltpu.make_async_copy(
                stage.at[:num_slot, 2 * width :], pay_hbm.at[:, 2 * width :], sems.at[2]
            ),
            pltpu.make_async_copy(counts, extra_hbm, sems.at[3]),
        ]
    else:
        kept = own[...]
        own[:, : 2 * first] = part_of(kept, 0, first)
        own[:, 2 * first :] = part_of(kept, first, width)
        last = [pltpu.make_async_copy(own, extra_hbm, sems.at[2])]
    start(last)
    wait(out + last)


def owner_hot(sent, base, owned):
    col = iota(sent.shape, 1)
    asked = jnp.sum(jnp.where(col == base, sent, 0.0), axis=1, keepdims=True).astype(jnp.int32)
    return hot(iota((sent.shape[0], owned), 1) == asked)


def pack_kernel(
    num_off, num_src, slots, src_n, rcv_n, got_hbm, joint0_hbm, joint1_hbm, own_hbm, _, out_hbm,
    got, joint, own, out, sems,
):
    edge = joint0_hbm.shape[1]
    rest = joint1_hbm.shape[1]
    freq = edge + rest
    copies = [
        pltpu.make_async_copy(got_hbm.at[:, edge:], got, sems.at[0]),
        pltpu.make_async_copy(joint0_hbm, joint.at[:, :edge], sems.at[1]),
        pltpu.make_async_copy(joint1_hbm, joint.at[:, edge:], sems.at[2]),
        pltpu.make_async_copy(own_hbm, own, sems.at[3]),
    ]
    start(copies)
    wait(copies)
    num = got.shape[0]
    group = lax.axis_index("src")
    sent = got[...]
    chosen = owner_hot(sent, num_off + num_src, own.shape[0])
    every_src = src_n * num_src
    col = iota((LANES, every_src), 0)
    pick = hot(col == num_off + iota((LANES, every_src), 1) % num_src)
    by_src = exact(sent, pick)
    from_group = iota((num, every_src), 0) // (slots * rcv_n)
    by_src = jnp.where(from_group == iota((num, every_src), 1) // num_src, by_src, 0.0)
    off_of = exact(chosen, sent, TN)[:, :num_off]
    src_of = exact(chosen, by_src, TN)
    off_sum = joint[:num_off, :] - exact(off_of, own[...], TN)
    src_sum = -exact(src_of, own[...], TN)
    mine = joint[num_off : num_off + num_src, :]
    off_rows = num_off // src_n
    piece = freq // rcv_n
    pad = [] if off_rows == slots else [jnp.zeros((slots - off_rows, piece), F32)]
    for i in range(src_n):
        source = src_sum[i * num_src : (i + 1) * num_src] + jnp.where(group == i, mine, 0.0)
        for m in range(rcv_n):
            to = slice((i * rcv_n + m) * slots, (i * rcv_n + m + 1) * slots)
            at = slice(m * piece, (m + 1) * piece)
            block = off_sum[i * off_rows : (i + 1) * off_rows, at]
            if pad:
                block = jnp.concatenate([block] + pad, axis=0)
            out[to, :piece] = block
            out[to, piece:] = source[:, at]
    copy = pltpu.make_async_copy(out, out_hbm.at[:, rest:], sems.at[0])
    copy.start()
    copy.wait()


def shares_kernel(num_off, num_src, slots, got_hbm, sums_hbm, off_out, src_out, sent, tail, sems):
    piece = src_out.shape[1]
    edge = got_hbm.shape[1] - LANES
    rest = sums_hbm.shape[1] - 2 * piece
    copies = [
        pltpu.make_async_copy(got_hbm.at[:, edge:], sent, sems.at[0]),
        pltpu.make_async_copy(sums_hbm.at[:, rest:], tail, sems.at[1]),
    ]
    start(copies)
    wait(copies)
    peers = sent.shape[0] // slots
    base = num_off + num_src
    both = sent[0:slots]
    value = tail[0:slots]
    for d in range(1, peers):
        both = both + sent[d * slots : (d + 1) * slots]
        value = value + tail[d * slots : (d + 1) * slots]
    col = iota(both.shape, 1)
    num_o = jnp.sum(jnp.where(col == base + 1, both, 0.0), axis=1, keepdims=True)
    num_s = jnp.sum(jnp.where(col == base + 2, both, 0.0), axis=1, keepdims=True)
    off_new = value[:, :piece] / (num_o + 1.0)
    src_out[...] = value[:, piece:] / (num_s + 1.0)
    for d in range(peers):
        off_out[d * slots : (d + 1) * slots, :] = off_new


def receiver_kernel(num_off, num_src, got_hbm, sums_hbm, terms_hbm, out, got, sums, terms, sems):
    edge = got.shape[1] - LANES
    rest = sums.shape[1]
    copies = [
        pltpu.make_async_copy(got_hbm, got, sems.at[0]),
        pltpu.make_async_copy(sums_hbm.at[:, :rest], sums, sems.at[1]),
        pltpu.make_async_copy(terms_hbm, terms, sems.at[2]),
    ]
    start(copies)
    wait(copies)
    sent = got[:, edge:]
    value = terms[...]
    chosen = owner_hot(sent, num_off + num_src, value.shape[0])
    per_slot = jnp.where(iota(sent.shape, 1) < num_off, sent, 0.0)
    num = jnp.sum(exact(chosen, per_slot, TN), axis=1, keepdims=True)
    one = exact(chosen, got[:, :edge], TN)
    two = exact(chosen, sums[...], TN)
    edge //= 2
    rest //= 2
    total = join(one[:, :edge], one[:, edge:], two[:, :rest], two[:, rest:])
    out[...] = value + (total - num * value) / (num + 1.0)


def final_kernel(src_n, rcv_n, off_rows, slots, edge, every_hbm, source, offset, *refs):
    src_out, off_out, every, rest, sems = refs[rcv_n:]
    copies = [pltpu.make_async_copy(refs[k], rest.at[k], sems.at[k]) for k in range(rcv_n)]
    copy = pltpu.make_async_copy(every_hbm, every, sems.at[rcv_n])
    start([copy] + copies)
    wait(copies)
    piece = every.shape[1]
    here = lax.axis_index("rcv")
    parts = []
    for j in range(rcv_n):
        value = jnp.zeros(rest.shape[1:], F32)
        for k in range(rcv_n):
            value = value + jnp.where((here + rcv_n - k) % rcv_n == j, rest[k], 0.0)
        parts.append(value)

    def columns(parts):
        whole = jnp.concatenate(parts, axis=1)
        rest = 2 * edge + (whole.shape[1] - 2 * edge) // 2
        return join(
            whole[:, :edge], whole[:, edge : 2 * edge], whole[:, 2 * edge : rest], whole[:, rest:]
        )

    src_out[...] = source[...] + columns(parts)
    copy.wait()
    parts = []
    for m in range(rcv_n):
        at = [(i * rcv_n + m) * slots for i in range(src_n)]
        parts.append(jnp.concatenate([every[a : a + off_rows, :] for a in at], axis=0))
    off_out[...] = offset[...] + columns(parts)


def swap(value, slots):
    shape = value.shape
    value = value.reshape(shape[0] // slots, slots, shape[1])
    value = lax.all_to_all(value, AXES, split_axis=0, concat_axis=0, tiled=True)
    return value.reshape(shape)


def local(
    traces,
    trace_source,
    trace_offset,
    trace_slot,
    request_list,
    source_terms,
    receiver_terms,
    offset_terms,
):
    src_n = lax.axis_size("src")
    rcv_n = lax.axis_size("rcv")
    peers = src_n * rcv_n
    slots = request_list.shape[2]
    num_tr, samples = traces.shape
    owned, freq = receiver_terms.shape
    num_src = source_terms.shape[0]
    num_off = offset_terms.shape[0]
    num_slot = peers * slots
    joint = -(-(num_off + num_src) // 16) * 16
    rows = num_slot + joint
    half = freq // 2
    edge = LANES
    rest = half - edge
    piece = freq // rcv_n
    off_rows = num_off // src_n
    tile = min(512, num_tr)
    assert slots == num_src and off_rows <= slots and num_off + num_src + 3 <= LANES
    assert samples == 2 * freq and freq % (4 * LANES) == 0 and owned <= 256
    ids = [v.reshape(1, num_tr) for v in (trace_slot, trace_offset, trace_source)]
    lists = jnp.swapaxes(request_list, 1, 2).reshape(slots, peers)
    vmem = pl.BlockSpec(memory_space=pltpu.VMEM)
    hbm = pl.BlockSpec(memory_space=pltpu.HBM)
    anywhere = pl.BlockSpec(memory_space=pl.ANY)

    def static(kernel, *args):
        return lambda *refs: kernel(*args, *refs)

    def shape(*dims):
        return jax.ShapeDtypeStruct(dims, F32)

    def spectra(first, width, counts):
        consts = [jnp.asarray(v) for v in twiddles(samples, first, first + width)]
        lead = first == 0
        return pl.pallas_call(
            static(spectra_kernel, num_off, num_src, rcv_n, first, tile),
            out_shape=(
                shape(num_slot, 2 * width + (LANES if lead else 2 * piece)),
                shape(joint, 2 * width),
                shape(rows, LANES) if lead else shape(owned, freq),
            ),
            in_specs=[hbm] * 12,
            out_specs=(hbm, hbm, hbm),
            scratch_shapes=[
                pltpu.VMEM((num_tr, samples), BF16),
                pltpu.VMEM((3, 1, num_tr), jnp.int32),
                pltpu.VMEM((slots, peers), jnp.int32),
                pltpu.VMEM((LANES, freq), F32),
                pltpu.VMEM((owned, freq), F32),
                pltpu.VMEM((rows, LANES), F32),
                pltpu.VMEM(consts[0].shape, F32),
                pltpu.VMEM(consts[1].shape, F32),
                pltpu.VMEM(consts[2].shape, F32),
                pltpu.VMEM((2, freq, 2 * width), BF16),
                pltpu.VMEM((rows, 2 * width), F32),
                pltpu.VMEM((rows, 2 * width + LANES), F32),
                pltpu.SemaphoreType.DMA((10,)),
                pltpu.SemaphoreType.DMA((num_tr // tile,)),
            ],
            compiler_params=pltpu.CompilerParams(vmem_limit_bytes=56 * 2**20),
            name="spectra%d" % first,
        )(traces, *ids, lists, offset_terms, source_terms, receiver_terms, counts, *consts)

    pay, joint0, counts = spectra(0, edge, jnp.zeros((8, LANES), F32))
    got = swap(pay, slots)
    pay, joint1, own = spectra(edge, rest, counts)
    pay = pl.pallas_call(
        static(pack_kernel, num_off, num_src, slots, src_n, rcv_n),
        out_shape=shape(*pay.shape),
        in_specs=[anywhere] + [hbm] * 4,
        out_specs=hbm,
        scratch_shapes=[
            pltpu.VMEM((num_slot, LANES), F32),
            pltpu.VMEM((joint, freq), F32),
            pltpu.VMEM((owned, freq), F32),
            pltpu.VMEM((num_slot, 2 * piece), F32),
            pltpu.SemaphoreType.DMA((4,)),
        ],
        input_output_aliases={4: 0},
        name="pack",
    )(got, joint0, joint1, own, pay)
    sums = swap(pay, slots)

    off_new, src_new = pl.pallas_call(
        static(shares_kernel, num_off, num_src, slots),
        out_shape=(shape(num_slot, piece), shape(num_src, piece)),
        in_specs=[anywhere, anywhere],
        out_specs=(vmem, vmem),
        scratch_shapes=[
            pltpu.VMEM((num_slot, LANES), F32),
            pltpu.VMEM((num_slot, 2 * piece), F32),
            pltpu.SemaphoreType.DMA((2,)),
        ],
        name="shares",
    )(got, sums)
    every = swap(off_new, slots)
    parts = [src_new]
    for k in range(1, rcv_n):
        ring = [(j, (j + k) % rcv_n) for j in range(rcv_n)]
        parts.append(lax.ppermute(src_new, "rcv", ring))
    receiver_new = pl.pallas_call(
        static(receiver_kernel, num_off, num_src),
        out_shape=shape(owned, freq),
        in_specs=[anywhere, anywhere, hbm],
        out_specs=vmem,
        scratch_shapes=[
            pltpu.VMEM((num_slot, 2 * edge + LANES), F32),
            pltpu.VMEM((num_slot, 2 * rest), F32),
            pltpu.VMEM((owned, freq), F32),
            pltpu.SemaphoreType.DMA((3,)),
        ],
        name="receiver",
    )(got, sums, receiver_terms)
    source_new, offset_new = pl.pallas_call(
        static(final_kernel, src_n, rcv_n, off_rows, slots, edge),
        out_shape=(shape(num_src, freq), shape(num_off, freq)),
        in_specs=[anywhere, vmem, vmem] + [anywhere] * rcv_n,
        out_specs=(vmem, vmem),
        scratch_shapes=[
            pltpu.VMEM((num_slot, piece), F32),
            pltpu.VMEM((rcv_n, num_src, piece), F32),
            pltpu.SemaphoreType.DMA((rcv_n + 1,)),
        ],
        name="final",
    )(every, source_terms, offset_terms, *parts)
    return (source_new, receiver_new, offset_new)


def solution(mesh):
    return jax.shard_map(
        local,
        mesh=mesh,
        in_specs=(
            P(AXES, None),
            P(AXES),
            P(AXES),
            P(AXES),
            P(AXES, None, None),
            P("src", None),
            P(AXES, None),
            P(),
        ),
        out_specs=(P("src", None), P(AXES, None), P()),
        check_vma=False,
    )
```

```python
import math

import jax
import jax.numpy as jnp
import numpy as np
from jax import lax
from jax.experimental import pallas as pl
from jax.experimental.pallas import tpu as pltpu
from jax.sharding import PartitionSpec as P

AXES = ("src", "rcv")
LANES = 128
F32 = jnp.float32
BF16 = jnp.bfloat16
NT = (((1,), (1,)), ((), ()))
TN = (((0,), (0,)), ((), ()))
NN = (((1,), (0,)), ((), ()))


def twiddles(samples, first, last):
    half = samples // 2
    quarter = samples // 4
    lane = np.arange(LANES)
    even = np.where(lane % 2 == 0, lane, half - 1 + lane)
    odd = np.where(lane % 2 == 1, lane, half - 1 + lane + np.where(lane == 0, LANES, 0))
    freq = np.arange(quarter)
    groups = half // LANES
    unit = 2.0 * math.pi / samples
    base = []
    taper = []
    for rows, fold in ((even, -np.cos(even * quarter * unit)), (odd, np.sin(odd * quarter * unit))):
        phase = (rows[:, None] * freq[None, :] % samples) * unit
        sine = np.sin(phase)
        sine[:, 0] = np.round(fold)
        base += [np.cos(phase), sine]
        at = rows[:, None] + LANES * np.arange(groups)[None, :]
        taper.append((0.5 - 0.5 * np.cos((at + 0.5) * unit)) / math.sqrt(samples))
    turn = (LANES * np.arange(groups)[:, None] * freq[None, :] % samples) * unit
    turn = np.stack([np.cos(turn), np.sin(turn)])
    return (
        np.stack(base)[:, :, first:last].astype(np.float32),
        turn[:, :, first:last].astype(np.float32),
        np.stack(taper).astype(np.float32),
    )


def dot(a, b, dims=NN):
    return lax.dot_general(a, b, dims, preferred_element_type=F32)


def exact(a, b, dims=NN):
    return lax.dot_general(
        a, b, dims, precision=lax.Precision.HIGHEST, preferred_element_type=F32
    )


def pieces(value):
    one = value.astype(BF16)
    rest = value - one.astype(F32)
    two = rest.astype(BF16)
    return one, two, (rest - two.astype(F32)).astype(BF16)


def count_dot(counts, terms):
    upper = counts.astype(BF16)
    lower = (counts - upper.astype(F32)).astype(BF16)
    counts = jnp.concatenate([upper, lower], axis=1)
    one, two, three = (jnp.concatenate([v, v], axis=0) for v in pieces(terms))
    return dot(counts, one) + dot(counts, two) + dot(counts, three)


def iota(shape, axis):
    return lax.broadcasted_iota(jnp.int32, shape, axis)


def hot(mask):
    return jnp.where(mask, 1.0, 0.0).astype(F32)


def ascend(value, lead):
    width = value.shape[1]
    row = iota((width, width), 0)
    col = iota((width, width), 1)
    if lead:
        pick = row == jnp.where(col == 0, 0, width - col)
    else:
        pick = row == width - 1 - col
    pick = hot(pick).astype(BF16)
    one, two, three = pieces(value)
    return dot(one, pick) + dot(two, pick) + dot(three, pick)


def join(low0, high0, low1, high1):
    edge = high1.shape[1]
    whole = jnp.concatenate([high1, high0], axis=1)
    col = iota(whole.shape, 1)
    shifted = pltpu.roll(whole, 1, 1)
    high = jnp.where(col <= edge, shifted, whole)
    high = jnp.where(col == 0, high0[:, :1], high)
    return jnp.concatenate([low0, low1, high], axis=1)


def part_of(value, first, width):
    half = value.shape[1] // 2
    high = value[:, half:]
    if first == 0:
        tail = high[:, half - width :]
        tail = jnp.where(iota(tail.shape, 1) == 0, high[:, :1], tail)
    else:
        tail = pltpu.roll(high, half - 1, 1)[:, :width]
    return jnp.concatenate([value[:, first : first + width], tail], axis=1)


def start(copies):
    for copy in copies:
        copy.start()


def wait(copies):
    for copy in copies:
        copy.wait()


def build_table(base, turn, taper, table):
    groups = taper.shape[2]
    width = base.shape[2]
    for side in range(2):
        for g in range(groups):
            cos0 = base[2 * side]
            sin0 = base[2 * side + 1]
            cos1 = turn[0, g : g + 1, :]
            sin1 = turn[1, g : g + 1, :]
            scale = taper[side, :, g : g + 1]
            at = slice(g * LANES, (g + 1) * LANES)
            table[side, at, :width] = ((cos0 * cos1 - sin0 * sin1) * scale).astype(BF16)
            table[side, at, width:] = ((sin0 * cos1 + cos0 * sin1) * -scale).astype(BF16)


def ident_rows(num_slot, num_off, rows, slot, off, src):
    top = iota((num_slot, slot.shape[1]), 0) == slot
    low = iota((rows - num_slot, slot.shape[1]), 0)
    low = (low == off) | (low == src + num_off)
    return jnp.concatenate([hot(top).astype(BF16), hot(low).astype(BF16)], axis=0)


def spectra_kernel(
    num_off, num_src, rcv_n, first, tile,
    x_hbm, slot_hbm, off_hbm, src_hbm, lists_hbm, offset_hbm, source_hbm, own_hbm,
    counts_hbm, base_hbm, turn_hbm, taper_hbm, pay_hbm, joint_hbm, extra_hbm,
    x, ids, lists, terms, own, counts, base, turn, taper, table, total, stage, spectrum, sems, x_sems,
):
    slots, peers = lists.shape
    num_slot = peers * slots
    rows = total.shape[0]
    width = base.shape[2]
    half = x.shape[1] // 2
    lead = first == 0
    group = lax.axis_index("src")
    near = [
        pltpu.make_async_copy(base_hbm, base, sems.at[0]),
        pltpu.make_async_copy(turn_hbm, turn, sems.at[1]),
        pltpu.make_async_copy(taper_hbm, taper, sems.at[2]),
    ]
    far = [
        pltpu.make_async_copy(slot_hbm, ids.at[0], sems.at[3]),
        pltpu.make_async_copy(off_hbm, ids.at[1], sems.at[4]),
        pltpu.make_async_copy(src_hbm, ids.at[2], sems.at[5]),
        pltpu.make_async_copy(offset_hbm, terms.at[0:num_off], sems.at[6]),
        pltpu.make_async_copy(source_hbm, terms.at[num_off : num_off + num_src], sems.at[7]),
    ]
    if lead:
        far.append(pltpu.make_async_copy(lists_hbm, lists, sems.at[8]))
    else:
        far.append(pltpu.make_async_copy(own_hbm, own, sems.at[8]))
        far.append(pltpu.make_async_copy(counts_hbm, counts, sems.at[9]))
    tiles = [
        pltpu.make_async_copy(
            x_hbm.at[t * tile : (t + 1) * tile], x.at[t * tile : (t + 1) * tile], x_sems.at[t]
        )
        for t in range(x.shape[0] // tile)
    ]
    start(near + tiles[:1] + far + tiles[1:])
    spare = num_off + num_src
    terms[spare:, :] = jnp.zeros((terms.shape[0] - spare, terms.shape[1]), F32)
    total[...] = jnp.zeros_like(total)
    if lead:
        counts[...] = jnp.zeros_like(counts)
    wait(near)
    build_table(base, turn, taper, table)
    wait(far)
    if lead:
        spread = hot(iota((num_slot, peers), 0) // slots == iota((num_slot, peers), 1))
        listed = dot(spread.astype(BF16), lists[...].astype(F32).astype(BF16), NT)
        mine = iota((num_slot, slots), 0) % slots == iota((num_slot, slots), 1)
        asked = jnp.sum(jnp.where(mine, listed, 0.0), axis=1, keepdims=True)
        stage[:num_slot, 2 * width : 2 * width + 1] = asked

    def transform(t):
        tiles[t].wait()
        lane = iota((tile, LANES), 1) % 2 == 0
        even = []
        odd = []
        for g in range(half // LANES):
            front = x[t * tile : (t + 1) * tile, g * LANES : (g + 1) * LANES]
            back = x[t * tile : (t + 1) * tile, half + g * LANES : half + (g + 1) * LANES]
            back = pltpu.roll(back.astype(F32), 1, 1).astype(BF16)
            even.append(jnp.where(lane, front, back))
            odd.append(jnp.where(lane, back, front))
        spectrum[t % 2, :, : 2 * width] = dot(jnp.concatenate(even, axis=1), table[0])
        spectrum[t % 2, :, 2 * width :] = dot(jnp.concatenate(odd, axis=1), table[1])

    def collect(t):
        at = slice(t * tile, (t + 1) * tile)
        slot, off = ids[0, :, at], ids[1, :, at]
        src = ids[2, :, at] - group * num_src
        every = ident_rows(num_slot, num_off, rows, slot, off, src)
        if lead:
            col = iota((LANES, tile), 0)
            counts[...] += dot(
                every, hot((col == off) | (col == src + num_off)).astype(BF16), NT
            )
        ec, es, oc, os = (
            spectrum[t % 2, :, k * width : (k + 1) * width] for k in range(4)
        )
        re_low, im_low = ec + oc, es + os
        re_high, im_high = ec - oc, es - os
        if lead:
            zero = iota((tile, width), 1) == 0
            im_low = jnp.where(zero, 0.0, im_low)
            re_high = jnp.where(zero, es, re_high)
            im_high = jnp.where(zero, os, im_high)
        power = jnp.concatenate(
            [re_low * re_low + im_low * im_low, re_high * re_high + im_high * im_high], axis=1
        )
        amp = 0.5 * jnp.log(power + 0.01)
        upper = amp.astype(BF16)
        lower = (amp - upper.astype(F32)).astype(BF16)
        total[...] += dot(every, upper) + dot(every, lower)

    transform(0)
    for t in range(1, len(tiles)):
        transform(t)
        collect(t - 1)
    collect(len(tiles) - 1)
    known = count_dot(counts[...], part_of(terms[...], first, width))
    stage[:, :width] = total[:, :width] - known[:, :width]
    stage[:, width : 2 * width] = ascend(total[:, width:], lead) - known[:, width:]
    out = [
        pltpu.make_async_copy(
            stage.at[:num_slot, : 2 * width], pay_hbm.at[:, : 2 * width], sems.at[0]
        ),
        pltpu.make_async_copy(stage.at[num_slot:, : 2 * width], joint_hbm, sems.at[1]),
    ]
    start(out)
    if lead:
        part = counts[:num_slot]
        whole = jnp.sum(part, axis=0, keepdims=True)
        row = iota((num_slot, LANES), 0)
        col = iota((num_slot, LANES), 1)
        peer = row // slots
        inner = row % slots
        off_rows = num_off // (peers // rcv_n)
        is_off = (col == peer // rcv_n * off_rows + inner) & (inner < off_rows)
        is_src = (col == num_off + inner) & (peer // rcv_n == group) & (inner < num_src)
        num_o = jnp.sum(jnp.where(is_off, whole, 0.0), axis=1, keepdims=True)
        num_s = jnp.sum(jnp.where(is_src, whole, 0.0), axis=1, keepdims=True)
        asked = stage[:num_slot, 2 * width : 2 * width + 1]
        part = jnp.where(col == spare, asked, part)
        part = jnp.where(col == spare + 1, num_o, part)
        stage[:num_slot, 2 * width :] = jnp.where(col == spare + 2, num_s, part)
        last = [
            pltpu.make_async_copy(
                stage.at[:num_slot, 2 * width :], pay_hbm.at[:, 2 * width :], sems.at[2]
            ),
            pltpu.make_async_copy(counts, extra_hbm, sems.at[3]),
        ]
    else:
        kept = own[...]
        own[:, : 2 * first] = part_of(kept, 0, first)
        own[:, 2 * first :] = part_of(kept, first, width)
        last = [pltpu.make_async_copy(own, extra_hbm, sems.at[2])]
    start(last)
    wait(out + last)


def owner_hot(sent, base, owned):
    col = iota(sent.shape, 1)
    asked = jnp.sum(jnp.where(col == base, sent, 0.0), axis=1, keepdims=True).astype(jnp.int32)
    return hot(iota((sent.shape[0], owned), 1) == asked)


def pack_kernel(
    num_off, num_src, slots, src_n, rcv_n, got_hbm, joint0_hbm, joint1_hbm, own_hbm, _, out_hbm,
    got, joint, own, out, sems,
):
    edge = joint0_hbm.shape[1]
    rest = joint1_hbm.shape[1]
    freq = edge + rest
    copies = [
        pltpu.make_async_copy(got_hbm.at[:, edge:], got, sems.at[0]),
        pltpu.make_async_copy(joint0_hbm, joint.at[:, :edge], sems.at[1]),
        pltpu.make_async_copy(joint1_hbm, joint.at[:, edge:], sems.at[2]),
        pltpu.make_async_copy(own_hbm, own, sems.at[3]),
    ]
    start(copies)
    wait(copies)
    num = got.shape[0]
    group = lax.axis_index("src")
    sent = got[...]
    chosen = owner_hot(sent, num_off + num_src, own.shape[0])
    every_src = src_n * num_src
    col = iota((LANES, every_src), 0)
    pick = hot(col == num_off + iota((LANES, every_src), 1) % num_src)
    by_src = exact(sent, pick)
    from_group = iota((num, every_src), 0) // (slots * rcv_n)
    by_src = jnp.where(from_group == iota((num, every_src), 1) // num_src, by_src, 0.0)
    off_of = exact(chosen, sent, TN)[:, :num_off]
    src_of = exact(chosen, by_src, TN)
    off_sum = joint[:num_off, :] - exact(off_of, own[...], TN)
    src_sum = -exact(src_of, own[...], TN)
    mine = joint[num_off : num_off + num_src, :]
    off_rows = num_off // src_n
    piece = freq // rcv_n
    pad = [] if off_rows == slots else [jnp.zeros((slots - off_rows, piece), F32)]
    for i in range(src_n):
        source = src_sum[i * num_src : (i + 1) * num_src] + jnp.where(group == i, mine, 0.0)
        for m in range(rcv_n):
            to = slice((i * rcv_n + m) * slots, (i * rcv_n + m + 1) * slots)
            at = slice(m * piece, (m + 1) * piece)
            block = off_sum[i * off_rows : (i + 1) * off_rows, at]
            if pad:
                block = jnp.concatenate([block] + pad, axis=0)
            out[to, :piece] = block
            out[to, piece:] = source[:, at]
    copy = pltpu.make_async_copy(out, out_hbm.at[:, rest:], sems.at[0])
    copy.start()
    copy.wait()


def shares_kernel(num_off, num_src, slots, got_hbm, sums_hbm, off_out, src_out, sent, tail, sems):
    piece = src_out.shape[1]
    edge = got_hbm.shape[1] - LANES
    rest = sums_hbm.shape[1] - 2 * piece
    copies = [
        pltpu.make_async_copy(got_hbm.at[:, edge:], sent, sems.at[0]),
        pltpu.make_async_copy(sums_hbm.at[:, rest:], tail, sems.at[1]),
    ]
    start(copies)
    wait(copies)
    peers = sent.shape[0] // slots
    base = num_off + num_src
    both = sent[0:slots]
    value = tail[0:slots]
    for d in range(1, peers):
        both = both + sent[d * slots : (d + 1) * slots]
        value = value + tail[d * slots : (d + 1) * slots]
    col = iota(both.shape, 1)
    num_o = jnp.sum(jnp.where(col == base + 1, both, 0.0), axis=1, keepdims=True)
    num_s = jnp.sum(jnp.where(col == base + 2, both, 0.0), axis=1, keepdims=True)
    off_new = value[:, :piece] / (num_o + 1.0)
    src_out[...] = value[:, piece:] / (num_s + 1.0)
    for d in range(peers):
        off_out[d * slots : (d + 1) * slots, :] = off_new


def receiver_kernel(num_off, num_src, got_hbm, sums_hbm, terms_hbm, out, got, sums, terms, sems):
    edge = got.shape[1] - LANES
    rest = sums.shape[1]
    copies = [
        pltpu.make_async_copy(got_hbm, got, sems.at[0]),
        pltpu.make_async_copy(sums_hbm.at[:, :rest], sums, sems.at[1]),
        pltpu.make_async_copy(terms_hbm, terms, sems.at[2]),
    ]
    start(copies)
    wait(copies)
    sent = got[:, edge:]
    value = terms[...]
    chosen = owner_hot(sent, num_off + num_src, value.shape[0])
    per_slot = jnp.where(iota(sent.shape, 1) < num_off, sent, 0.0)
    num = jnp.sum(exact(chosen, per_slot, TN), axis=1, keepdims=True)
    one = exact(chosen, got[:, :edge], TN)
    two = exact(chosen, sums[...], TN)
    edge //= 2
    rest //= 2
    total = join(one[:, :edge], one[:, edge:], two[:, :rest], two[:, rest:])
    out[...] = value + (total - num * value) / (num + 1.0)


def final_kernel(src_n, rcv_n, off_rows, slots, edge, every_hbm, source, offset, *refs):
    src_out, off_out, every, rest, sems = refs[rcv_n:]
    copies = [pltpu.make_async_copy(refs[k], rest.at[k], sems.at[k]) for k in range(rcv_n)]
    copy = pltpu.make_async_copy(every_hbm, every, sems.at[rcv_n])
    start([copy] + copies)
    wait(copies)
    piece = every.shape[1]
    here = lax.axis_index("rcv")
    parts = []
    for j in range(rcv_n):
        value = jnp.zeros(rest.shape[1:], F32)
        for k in range(rcv_n):
            value = value + jnp.where((here + rcv_n - k) % rcv_n == j, rest[k], 0.0)
        parts.append(value)

    def columns(parts):
        whole = jnp.concatenate(parts, axis=1)
        rest = 2 * edge + (whole.shape[1] - 2 * edge) // 2
        return join(
            whole[:, :edge], whole[:, edge : 2 * edge], whole[:, 2 * edge : rest], whole[:, rest:]
        )

    src_out[...] = source[...] + columns(parts)
    copy.wait()
    parts = []
    for m in range(rcv_n):
        at = [(i * rcv_n + m) * slots for i in range(src_n)]
        parts.append(jnp.concatenate([every[a : a + off_rows, :] for a in at], axis=0))
    off_out[...] = offset[...] + columns(parts)


def swap(value, slots):
    shape = value.shape
    value = value.reshape(shape[0] // slots, slots, shape[1])
    value = lax.all_to_all(value, AXES, split_axis=0, concat_axis=0, tiled=True)
    return value.reshape(shape)


def local(
    traces,
    trace_source,
    trace_offset,
    trace_slot,
    request_list,
    source_terms,
    receiver_terms,
    offset_terms,
):
    src_n = lax.axis_size("src")
    rcv_n = lax.axis_size("rcv")
    peers = src_n * rcv_n
    slots = request_list.shape[2]
    num_tr, samples = traces.shape
    owned, freq = receiver_terms.shape
    num_src = source_terms.shape[0]
    num_off = offset_terms.shape[0]
    num_slot = peers * slots
    joint = -(-(num_off + num_src) // 16) * 16
    rows = num_slot + joint
    half = freq // 2
    edge = half // 2
    rest = half - edge
    piece = freq // rcv_n
    off_rows = num_off // src_n
    tile = min(512, num_tr)
    assert slots == num_src and off_rows <= slots and num_off + num_src + 3 <= LANES
    assert samples == 2 * freq and freq % (4 * LANES) == 0 and owned <= 256
    ids = [v.reshape(1, num_tr) for v in (trace_slot, trace_offset, trace_source)]
    lists = jnp.swapaxes(request_list, 1, 2).reshape(slots, peers)
    vmem = pl.BlockSpec(memory_space=pltpu.VMEM)
    hbm = pl.BlockSpec(memory_space=pltpu.HBM)
    anywhere = pl.BlockSpec(memory_space=pl.ANY)

    def static(kernel, *args):
        return lambda *refs: kernel(*args, *refs)

    def shape(*dims):
        return jax.ShapeDtypeStruct(dims, F32)

    def spectra(first, width, counts):
        consts = [jnp.asarray(v) for v in twiddles(samples, first, first + width)]
        lead = first == 0
        return pl.pallas_call(
            static(spectra_kernel, num_off, num_src, rcv_n, first, tile),
            out_shape=(
                shape(num_slot, 2 * width + (LANES if lead else 2 * piece)),
                shape(joint, 2 * width),
                shape(rows, LANES) if lead else shape(owned, freq),
            ),
            in_specs=[hbm] * 12,
            out_specs=(hbm, hbm, hbm),
            scratch_shapes=[
                pltpu.VMEM((num_tr, samples), BF16),
                pltpu.VMEM((3, 1, num_tr), jnp.int32),
                pltpu.VMEM((slots, peers), jnp.int32),
                pltpu.VMEM((LANES, freq), F32),
                pltpu.VMEM((owned, freq), F32),
                pltpu.VMEM((rows, LANES), F32),
                pltpu.VMEM(consts[0].shape, F32),
                pltpu.VMEM(consts[1].shape, F32),
                pltpu.VMEM(consts[2].shape, F32),
                pltpu.VMEM((2, freq, 2 * width), BF16),
                pltpu.VMEM((rows, 2 * width), F32),
                pltpu.VMEM((rows, 2 * width + LANES), F32),
                pltpu.VMEM((2, tile, 4 * width), F32),
                pltpu.SemaphoreType.DMA((10,)),
                pltpu.SemaphoreType.DMA((num_tr // tile,)),
            ],
            compiler_params=pltpu.CompilerParams(vmem_limit_bytes=56 * 2**20),
            name="spectra%d" % first,
        )(traces, *ids, lists, offset_terms, source_terms, receiver_terms, counts, *consts)

    pay, joint0, counts = spectra(0, edge, offset_terms)
    got = swap(pay, slots)
    pay, joint1, own = spectra(edge, rest, counts)
    pay = pl.pallas_call(
        static(pack_kernel, num_off, num_src, slots, src_n, rcv_n),
        out_shape=shape(*pay.shape),
        in_specs=[anywhere] + [hbm] * 4,
        out_specs=hbm,
        scratch_shapes=[
            pltpu.VMEM((num_slot, LANES), F32),
            pltpu.VMEM((joint, freq), F32),
            pltpu.VMEM((owned, freq), F32),
            pltpu.VMEM((num_slot, 2 * piece), F32),
            pltpu.SemaphoreType.DMA((4,)),
        ],
        input_output_aliases={4: 0},
        name="pack",
    )(got, joint0, joint1, own, pay)
    sums = swap(pay, slots)

    off_new, src_new = pl.pallas_call(
        static(shares_kernel, num_off, num_src, slots),
        out_shape=(shape(num_slot, piece), shape(num_src, piece)),
        in_specs=[anywhere, anywhere],
        out_specs=(vmem, vmem),
        scratch_shapes=[
            pltpu.VMEM((num_slot, LANES), F32),
            pltpu.VMEM((num_slot, 2 * piece), F32),
            pltpu.SemaphoreType.DMA((2,)),
        ],
        name="shares",
    )(got, sums)
    every = swap(off_new, slots)
    parts = [src_new]
    for k in range(1, rcv_n):
        ring = [(j, (j + k) % rcv_n) for j in range(rcv_n)]
        parts.append(lax.ppermute(src_new, "rcv", ring))
    receiver_new = pl.pallas_call(
        static(receiver_kernel, num_off, num_src),
        out_shape=shape(owned, freq),
        in_specs=[anywhere, anywhere, hbm],
        out_specs=vmem,
        scratch_shapes=[
            pltpu.VMEM((num_slot, 2 * edge + LANES), F32),
            pltpu.VMEM((num_slot, 2 * rest), F32),
            pltpu.VMEM((owned, freq), F32),
            pltpu.SemaphoreType.DMA((3,)),
        ],
        name="receiver",
    )(got, sums, receiver_terms)
    source_new, offset_new = pl.pallas_call(
        static(final_kernel, src_n, rcv_n, off_rows, slots, edge),
        out_shape=(shape(num_src, freq), shape(num_off, freq)),
        in_specs=[anywhere, vmem, vmem] + [anywhere] * rcv_n,
        out_specs=(vmem, vmem),
        scratch_shapes=[
            pltpu.VMEM((num_slot, piece), F32),
            pltpu.VMEM((rcv_n, num_src, piece), F32),
            pltpu.SemaphoreType.DMA((rcv_n + 1,)),
        ],
        name="final",
    )(every, source_terms, offset_terms, *parts)
    return (source_new, receiver_new, offset_new)


def solution(mesh):
    return jax.shard_map(
        local,
        mesh=mesh,
        in_specs=(
            P(AXES, None),
            P(AXES),
            P(AXES),
            P(AXES),
            P(AXES, None, None),
            P("src", None),
            P(AXES, None),
            P(),
        ),
        out_specs=(P("src", None), P(AXES, None), P()),
        check_vma=False,
    )
```

```python
import math

import jax
import jax.numpy as jnp
import numpy as np
from jax import lax
from jax.experimental import pallas as pl
from jax.experimental.pallas import tpu as pltpu
from jax.sharding import PartitionSpec as P

AXES = ("src", "rcv")
LANES = 128
F32 = jnp.float32
BF16 = jnp.bfloat16
NT = (((1,), (1,)), ((), ()))
TN = (((0,), (0,)), ((), ()))
NN = (((1,), (0,)), ((), ()))


def twiddles(samples, first, last):
    half = samples // 2
    quarter = samples // 4
    lane = np.arange(LANES)
    even = np.where(lane % 2 == 0, lane, half - 1 + lane)
    odd = np.where(lane % 2 == 1, lane, half - 1 + lane + np.where(lane == 0, LANES, 0))
    freq = np.arange(quarter)
    groups = half // LANES
    unit = 2.0 * math.pi / samples
    base = []
    taper = []
    for rows, fold in ((even, -np.cos(even * quarter * unit)), (odd, np.sin(odd * quarter * unit))):
        phase = (rows[:, None] * freq[None, :] % samples) * unit
        sine = np.sin(phase)
        sine[:, 0] = np.round(fold)
        base += [np.cos(phase), sine]
        at = rows[:, None] + LANES * np.arange(groups)[None, :]
        taper.append((0.5 - 0.5 * np.cos((at + 0.5) * unit)) / math.sqrt(samples))
    turn = (LANES * np.arange(groups)[:, None] * freq[None, :] % samples) * unit
    turn = np.stack([np.cos(turn), np.sin(turn)])
    return (
        np.stack(base)[:, :, first:last].astype(np.float32),
        turn[:, :, first:last].astype(np.float32),
        np.stack(taper).astype(np.float32),
    )


def dot(a, b, dims=NN):
    return lax.dot_general(a, b, dims, preferred_element_type=F32)


def exact(a, b, dims=NN):
    return lax.dot_general(
        a, b, dims, precision=lax.Precision.HIGHEST, preferred_element_type=F32
    )


def pieces(value):
    one = value.astype(BF16)
    rest = value - one.astype(F32)
    two = rest.astype(BF16)
    return one, two, (rest - two.astype(F32)).astype(BF16)


def count_dot(counts, terms):
    upper = counts.astype(BF16)
    lower = (counts - upper.astype(F32)).astype(BF16)
    counts = jnp.concatenate([upper, lower], axis=1)
    one, two, three = (jnp.concatenate([v, v], axis=0) for v in pieces(terms))
    return dot(counts, one) + dot(counts, two) + dot(counts, three)


def iota(shape, axis):
    return lax.broadcasted_iota(jnp.int32, shape, axis)


def hot(mask):
    return jnp.where(mask, 1.0, 0.0).astype(F32)


def ascend(value, lead):
    width = value.shape[1]
    row = iota((width, width), 0)
    col = iota((width, width), 1)
    if lead:
        pick = row == jnp.where(col == 0, 0, width - col)
    else:
        pick = row == width - 1 - col
    pick = hot(pick).astype(BF16)
    one, two, three = pieces(value)
    return dot(one, pick) + dot(two, pick) + dot(three, pick)


def join(low0, high0, low1, high1):
    edge = high1.shape[1]
    whole = jnp.concatenate([high1, high0], axis=1)
    col = iota(whole.shape, 1)
    shifted = pltpu.roll(whole, 1, 1)
    high = jnp.where(col <= edge, shifted, whole)
    high = jnp.where(col == 0, high0[:, :1], high)
    return jnp.concatenate([low0, low1, high], axis=1)


def part_of(value, first, width):
    half = value.shape[1] // 2
    high = value[:, half:]
    if first == 0:
        tail = high[:, half - width :]
        tail = jnp.where(iota(tail.shape, 1) == 0, high[:, :1], tail)
    else:
        tail = pltpu.roll(high, half - 1, 1)[:, :width]
    return jnp.concatenate([value[:, first : first + width], tail], axis=1)


def start(copies):
    for copy in copies:
        copy.start()


def wait(copies):
    for copy in copies:
        copy.wait()


def build_table(base, turn, taper, table):
    groups = taper.shape[2]
    width = base.shape[2]
    for side in range(2):
        for g in range(groups):
            cos0 = base[2 * side]
            sin0 = base[2 * side + 1]
            cos1 = turn[0, g : g + 1, :]
            sin1 = turn[1, g : g + 1, :]
            scale = taper[side, :, g : g + 1]
            at = slice(g * LANES, (g + 1) * LANES)
            table[side, at, :width] = ((cos0 * cos1 - sin0 * sin1) * scale).astype(BF16)
            table[side, at, width:] = ((sin0 * cos1 + cos0 * sin1) * -scale).astype(BF16)


def ident_rows(num_slot, num_off, rows, slot, off, src):
    top = iota((num_slot, slot.shape[1]), 0) == slot
    low = iota((rows - num_slot, slot.shape[1]), 0)
    low = (low == off) | (low == src + num_off)
    return jnp.concatenate([hot(top).astype(BF16), hot(low).astype(BF16)], axis=0)


def spectra_kernel(
    num_off, num_src, rcv_n, first, tile,
    x_hbm, slot_hbm, off_hbm, src_hbm, lists_hbm, offset_hbm, source_hbm, own_hbm,
    counts_hbm, base_hbm, turn_hbm, taper_hbm, pay_hbm, joint_hbm, extra_hbm,
    x, ids, lists, terms, own, counts, base, turn, taper, table, total, stage, spectrum, sems, x_sems,
):
    slots, peers = lists.shape
    num_slot = peers * slots
    rows = total.shape[0]
    width = base.shape[2]
    half = x.shape[1] // 2
    lead = first == 0
    group = lax.axis_index("src")
    near = [
        pltpu.make_async_copy(base_hbm, base, sems.at[0]),
        pltpu.make_async_copy(turn_hbm, turn, sems.at[1]),
        pltpu.make_async_copy(taper_hbm, taper, sems.at[2]),
    ]
    far = [
        pltpu.make_async_copy(slot_hbm, ids.at[0], sems.at[3]),
        pltpu.make_async_copy(off_hbm, ids.at[1], sems.at[4]),
        pltpu.make_async_copy(src_hbm, ids.at[2], sems.at[5]),
        pltpu.make_async_copy(offset_hbm, terms.at[0:num_off], sems.at[6]),
        pltpu.make_async_copy(source_hbm, terms.at[num_off : num_off + num_src], sems.at[7]),
    ]
    if lead:
        far.append(pltpu.make_async_copy(lists_hbm, lists, sems.at[8]))
    else:
        far.append(pltpu.make_async_copy(own_hbm, own, sems.at[8]))
        far.append(pltpu.make_async_copy(counts_hbm, counts, sems.at[9]))
    tiles = [
        pltpu.make_async_copy(
            x_hbm.at[t * tile : (t + 1) * tile], x.at[t * tile : (t + 1) * tile], x_sems.at[t]
        )
        for t in range(x.shape[0] // tile)
    ]
    start(near + tiles[:1] + far + tiles[1:])
    spare = num_off + num_src
    terms[spare:, :] = jnp.zeros((terms.shape[0] - spare, terms.shape[1]), F32)
    total[...] = jnp.zeros_like(total)
    if lead:
        counts[...] = jnp.zeros_like(counts)
    wait(near)
    build_table(base, turn, taper, table)
    wait(far)
    if lead:
        spread = hot(iota((num_slot, peers), 0) // slots == iota((num_slot, peers), 1))
        listed = dot(spread.astype(BF16), lists[...].astype(F32).astype(BF16), NT)
        mine = iota((num_slot, slots), 0) % slots == iota((num_slot, slots), 1)
        asked = jnp.sum(jnp.where(mine, listed, 0.0), axis=1, keepdims=True)
        stage[:num_slot, 2 * width : 2 * width + 1] = asked

    def transform(t):
        tiles[t].wait()
        lane = iota((tile, LANES), 1) % 2 == 0
        even = []
        odd = []
        for g in range(half // LANES):
            front = x[t * tile : (t + 1) * tile, g * LANES : (g + 1) * LANES]
            back = x[t * tile : (t + 1) * tile, half + g * LANES : half + (g + 1) * LANES]
            back = pltpu.roll(back, 1, 1)
            even.append(jnp.where(lane, front, back))
            odd.append(jnp.where(lane, back, front))
        spectrum[t % 2, :, : 2 * width] = dot(jnp.concatenate(even, axis=1), table[0])
        spectrum[t % 2, :, 2 * width :] = dot(jnp.concatenate(odd, axis=1), table[1])

    def collect(t):
        at = slice(t * tile, (t + 1) * tile)
        slot, off = ids[0, :, at], ids[1, :, at]
        src = ids[2, :, at] - group * num_src
        every = ident_rows(num_slot, num_off, rows, slot, off, src)
        if lead:
            col = iota((LANES, tile), 0)
            counts[...] += dot(
                every, hot((col == off) | (col == src + num_off)).astype(BF16), NT
            )
        ec, es, oc, os = (
            spectrum[t % 2, :, k * width : (k + 1) * width] for k in range(4)
        )
        re_low, im_low = ec + oc, es + os
        re_high, im_high = ec - oc, es - os
        if lead:
            zero = iota((tile, width), 1) == 0
            im_low = jnp.where(zero, 0.0, im_low)
            re_high = jnp.where(zero, es, re_high)
            im_high = jnp.where(zero, os, im_high)
        power = jnp.concatenate(
            [re_low * re_low + im_low * im_low, re_high * re_high + im_high * im_high], axis=1
        )
        amp = 0.5 * jnp.log(power + 0.01)
        upper = amp.astype(BF16)
        lower = (amp - upper.astype(F32)).astype(BF16)
        total[...] += dot(every, upper) + dot(every, lower)

    transform(0)
    for t in range(1, len(tiles)):
        transform(t)
        collect(t - 1)
    collect(len(tiles) - 1)
    known = count_dot(counts[...], part_of(terms[...], first, width))
    stage[:, :width] = total[:, :width] - known[:, :width]
    stage[:, width : 2 * width] = ascend(total[:, width:], lead) - known[:, width:]
    out = [
        pltpu.make_async_copy(
            stage.at[:num_slot, : 2 * width], pay_hbm.at[:, : 2 * width], sems.at[0]
        ),
        pltpu.make_async_copy(stage.at[num_slot:, : 2 * width], joint_hbm, sems.at[1]),
    ]
    start(out)
    if lead:
        part = counts[:num_slot]
        whole = jnp.sum(part, axis=0, keepdims=True)
        row = iota((num_slot, LANES), 0)
        col = iota((num_slot, LANES), 1)
        peer = row // slots
        inner = row % slots
        off_rows = max(1, num_off // peers)
        src_rows = num_src // rcv_n
        is_off = (col == peer * off_rows + inner) & (inner < off_rows) & (col < num_off)
        is_src = (col == num_off + peer % rcv_n * src_rows + inner) & (inner < src_rows)
        is_src = is_src & (peer // rcv_n == group)
        num_o = jnp.sum(jnp.where(is_off, whole, 0.0), axis=1, keepdims=True)
        num_s = jnp.sum(jnp.where(is_src, whole, 0.0), axis=1, keepdims=True)
        asked = stage[:num_slot, 2 * width : 2 * width + 1]
        part = jnp.where(col == spare, asked, part)
        part = jnp.where(col == spare + 1, num_o, part)
        stage[:num_slot, 2 * width :] = jnp.where(col == spare + 2, num_s, part)
        last = [
            pltpu.make_async_copy(
                stage.at[:num_slot, 2 * width :], pay_hbm.at[:, 2 * width :], sems.at[2]
            ),
            pltpu.make_async_copy(counts, extra_hbm, sems.at[3]),
        ]
    else:
        kept = own[...]
        own[:, : 2 * first] = part_of(kept, 0, first)
        own[:, 2 * first :] = part_of(kept, first, width)
        last = [pltpu.make_async_copy(own, extra_hbm, sems.at[2])]
    start(last)
    wait(out + last)


def owner_hot(sent, base, owned):
    col = iota(sent.shape, 1)
    asked = jnp.sum(jnp.where(col == base, sent, 0.0), axis=1, keepdims=True).astype(jnp.int32)
    return hot(iota((sent.shape[0], owned), 1) == asked)


def pack_kernel(
    num_off, num_src, slots, src_n, rcv_n, got_hbm, joint0_hbm, joint1_hbm, own_hbm, _, out_hbm,
    got, joint, own, out, sems,
):
    edge = joint0_hbm.shape[1]
    rest = joint1_hbm.shape[1]
    freq = edge + rest
    copies = [
        pltpu.make_async_copy(got_hbm, got, sems.at[0]),
        pltpu.make_async_copy(joint0_hbm, joint.at[:, :edge], sems.at[1]),
        pltpu.make_async_copy(joint1_hbm, joint.at[:, edge:], sems.at[2]),
        pltpu.make_async_copy(own_hbm, own, sems.at[3]),
    ]
    start(copies)
    wait(copies)
    num = got.shape[0]
    group = lax.axis_index("src")
    sent = got[...]
    chosen = owner_hot(sent, num_off + num_src, own.shape[0])
    every_src = src_n * num_src
    col = iota((LANES, every_src), 0)
    pick = hot(col == num_off + iota((LANES, every_src), 1) % num_src)
    by_src = exact(sent, pick)
    from_group = iota((num, every_src), 0) // (slots * rcv_n)
    by_src = jnp.where(from_group == iota((num, every_src), 1) // num_src, by_src, 0.0)
    off_of = exact(chosen, sent, TN)[:, :num_off]
    src_of = exact(chosen, by_src, TN)
    off_sum = joint[:num_off, :] - exact(off_of, own[...], TN)
    src_sum = -exact(src_of, own[...], TN)
    mine = joint[num_off : num_off + num_src, :]
    piece = freq // rcv_n
    per_off = slots // max(1, num_off // (src_n * rcv_n))
    per_src = slots // (num_src // rcv_n)
    if num_off * per_off < num or per_off > rcv_n:
        out[...] = jnp.zeros_like(out)
    each = piece // LANES
    for m in range(rcv_n):
        for h in range(each):
            at = slice(m * piece + h * LANES, m * piece + (h + 1) * LANES)
            out[h, pl.ds(m, num_off, stride=per_off), :] = off_sum[:, at]
            for i in range(src_n):
                to = pl.ds(i * num_src * per_src + m, num_src, stride=per_src)
                source = src_sum[i * num_src : (i + 1) * num_src, at]
                out[each + h, to, :] = source + jnp.where(group == i, mine[:, at], 0.0)
    copies = [
        pltpu.make_async_copy(
            out.at[h], out_hbm.at[:, rest + h * LANES : rest + (h + 1) * LANES], sems.at[h]
        )
        for h in range(2 * each)
    ]
    start(copies)
    wait(copies)


def shares_kernel(
    num_off, num_src, slots, edge, got_hbm, sums_hbm, offset_hbm, source_hbm,
    off_out, src_out, sent, tail, offset, source, rows, block, sems,
):
    rcv_n = lax.axis_size("rcv")
    piece = src_out.shape[1]
    rest = sums_hbm.shape[1] - 2 * piece
    copies = [
        pltpu.make_async_copy(got_hbm, sent, sems.at[0]),
        pltpu.make_async_copy(sums_hbm.at[:, rest:], tail, sems.at[1]),
        pltpu.make_async_copy(offset_hbm, offset, sems.at[2]),
        pltpu.make_async_copy(source_hbm, source, sems.at[3]),
    ]
    start(copies)
    wait(copies)
    peers = sent.shape[0] // slots
    base = num_off + num_src
    both = sent[0:slots]
    value = tail[0:slots]
    for d in range(1, peers):
        both = both + sent[d * slots : (d + 1) * slots]
        value = value + tail[d * slots : (d + 1) * slots]
    rows[...] = value
    col = iota(both.shape, 1)
    num_o = jnp.sum(jnp.where(col == base + 1, both, 0.0), axis=1, keepdims=True)
    num_s = jnp.sum(jnp.where(col == base + 2, both, 0.0), axis=1, keepdims=True)
    here = lax.axis_index("rcv")
    off_rows = max(1, num_off // peers)
    src_rows = num_src // rcv_n
    at_off = (lax.axis_index("src") * rcv_n + here) * off_rows
    for count, num, at, first, terms in (
        (off_rows, num_o, slice(0, piece), at_off, offset),
        (src_rows, num_s, slice(piece, 2 * piece), here * src_rows, source),
    ):
        last = terms.shape[0] - 1
        parts = [
            jnp.concatenate(
                [rows[j * (slots // count) + m : j * (slots // count) + m + 1, at] for j in range(count)],
                axis=0,
            )
            for m in range(rcv_n)
        ]
        whole = jnp.concatenate(parts, axis=1)
        e, r = edge // 2, (whole.shape[1] - edge) // 2
        whole = join(
            whole[:, :e], whole[:, e:edge], whole[:, edge : edge + r], whole[:, edge + r :]
        )
        old = jnp.concatenate(
            [terms[pl.ds(jnp.minimum(first + j, last), 1), :] for j in range(count)], axis=0
        )
        new = old + whole / (num[:count] + 1.0)
        block[:, at] = jnp.zeros((slots, piece), F32)
        for j in range(count):
            for m in range(rcv_n):
                to = j * (slots // count) + m
                block[to : to + 1, at] = new[j : j + 1, m * piece : (m + 1) * piece]
    src_out[...] = block[:, piece:]
    done = block[:, :piece]
    for d in range(peers):
        off_out[d * slots : (d + 1) * slots, :] = done


def receiver_kernel(num_off, num_src, got_hbm, sums_hbm, terms_hbm, out, got, sums, terms, sems):
    edge = got.shape[1] - LANES
    rest = sums.shape[1]
    copies = [
        pltpu.make_async_copy(got_hbm, got, sems.at[0]),
        pltpu.make_async_copy(sums_hbm.at[:, :rest], sums, sems.at[1]),
        pltpu.make_async_copy(terms_hbm, terms, sems.at[2]),
    ]
    start(copies)
    wait(copies)
    sent = got[:, edge:]
    value = terms[...]
    chosen = owner_hot(sent, num_off + num_src, value.shape[0])
    per_slot = jnp.where(iota(sent.shape, 1) < num_off, sent, 0.0)
    num = jnp.sum(exact(chosen, per_slot, TN), axis=1, keepdims=True)
    one = exact(chosen, got[:, :edge], TN)
    two = exact(chosen, sums[...], TN)
    edge //= 2
    rest //= 2
    total = join(one[:, :edge], one[:, edge:], two[:, :rest], two[:, rest:])
    out[...] = value + (total - num * value) / (num + 1.0)


def source_kernel(rcv_n, *refs):
    src_out, rest, sems = refs[rcv_n:]
    copies = [pltpu.make_async_copy(refs[k], rest.at[k], sems.at[k]) for k in range(rcv_n)]
    start(copies)
    wait(copies)
    slots, piece = rest.shape[1:]
    count = src_out.shape[0] // rcv_n
    here = lax.axis_index("rcv")
    for j in range(rcv_n):
        value = jnp.zeros((slots, piece), F32)
        for k in range(rcv_n):
            value = value + jnp.where((here + rcv_n - k) % rcv_n == j, rest[k], 0.0)
        for i in range(count):
            for m in range(rcv_n):
                row = i * (slots // count) + m
                src_out[j * count + i : j * count + i + 1, m * piece : (m + 1) * piece] = (
                    value[row : row + 1]
                )


def swap(value, slots):
    shape = value.shape
    value = value.reshape(shape[0] // slots, slots, shape[1])
    value = lax.all_to_all(value, AXES, split_axis=0, concat_axis=0, tiled=True)
    return value.reshape(shape)


def local(
    traces,
    trace_source,
    trace_offset,
    trace_slot,
    request_list,
    source_terms,
    receiver_terms,
    offset_terms,
):
    src_n = lax.axis_size("src")
    rcv_n = lax.axis_size("rcv")
    peers = src_n * rcv_n
    slots = request_list.shape[2]
    num_tr, samples = traces.shape
    owned, freq = receiver_terms.shape
    num_src = source_terms.shape[0]
    num_off = offset_terms.shape[0]
    num_slot = peers * slots
    joint = -(-(num_off + num_src) // 16) * 16
    rows = num_slot + joint
    half = freq // 2
    edge = half // 2
    rest = half - edge
    piece = freq // rcv_n
    off_rows = max(1, num_off // peers)
    tile = min(512, num_tr)
    assert slots == num_src and off_rows * rcv_n <= slots and num_off + num_src + 3 <= LANES
    assert samples == 2 * freq and freq % (4 * LANES) == 0 and owned <= 256
    ids = [v.reshape(1, num_tr) for v in (trace_slot, trace_offset, trace_source)]
    lists = jnp.swapaxes(request_list, 1, 2).reshape(slots, peers)
    vmem = pl.BlockSpec(memory_space=pltpu.VMEM)
    hbm = pl.BlockSpec(memory_space=pltpu.HBM)
    anywhere = pl.BlockSpec(memory_space=pl.ANY)

    def static(kernel, *args):
        return lambda *refs: kernel(*args, *refs)

    def shape(*dims):
        return jax.ShapeDtypeStruct(dims, F32)

    def spectra(first, width, counts):
        consts = [jnp.asarray(v) for v in twiddles(samples, first, first + width)]
        lead = first == 0
        return pl.pallas_call(
            static(spectra_kernel, num_off, num_src, rcv_n, first, tile),
            out_shape=(
                shape(num_slot, 2 * width + (LANES if lead else 2 * piece)),
                shape(joint, 2 * width),
                shape(rows, LANES) if lead else shape(owned, freq),
            ),
            in_specs=[hbm] * 12,
            out_specs=(hbm, hbm, hbm),
            scratch_shapes=[
                pltpu.VMEM((num_tr, samples), BF16),
                pltpu.VMEM((3, 1, num_tr), jnp.int32),
                pltpu.VMEM((slots, peers), jnp.int32),
                pltpu.VMEM((LANES, freq), F32),
                pltpu.VMEM((owned, freq), F32),
                pltpu.VMEM((rows, LANES), F32),
                pltpu.VMEM(consts[0].shape, F32),
                pltpu.VMEM(consts[1].shape, F32),
                pltpu.VMEM(consts[2].shape, F32),
                pltpu.VMEM((2, freq, 2 * width), BF16),
                pltpu.VMEM((rows, 2 * width), F32),
                pltpu.VMEM((rows, 2 * width + LANES), F32),
                pltpu.VMEM((2, tile, 4 * width), F32),
                pltpu.SemaphoreType.DMA((10,)),
                pltpu.SemaphoreType.DMA((num_tr // tile,)),
            ],
            compiler_params=pltpu.CompilerParams(vmem_limit_bytes=56 * 2**20),
            name="spectra%d" % first,
        )(traces, *ids, lists, offset_terms, source_terms, receiver_terms, counts, *consts)

    pay, joint0, counts = spectra(0, edge, offset_terms)
    got = swap(pay, slots)
    sent = got[:, 2 * edge :]
    pay, joint1, own = spectra(edge, rest, counts)
    pay = pl.pallas_call(
        static(pack_kernel, num_off, num_src, slots, src_n, rcv_n),
        out_shape=shape(*pay.shape),
        in_specs=[anywhere] + [hbm] * 4,
        out_specs=hbm,
        scratch_shapes=[
            pltpu.VMEM((num_slot, LANES), F32),
            pltpu.VMEM((joint, freq), F32),
            pltpu.VMEM((owned, freq), F32),
            pltpu.VMEM((2 * piece // LANES, num_slot, LANES), F32),
            pltpu.SemaphoreType.DMA((max(4, 2 * piece // LANES),)),
        ],
        input_output_aliases={4: 0},
        name="pack",
    )(sent, joint0, joint1, own, pay)
    sums = swap(pay, slots)

    off_new, src_new = pl.pallas_call(
        static(shares_kernel, num_off, num_src, slots, 2 * edge),
        out_shape=(shape(num_slot, piece), shape(slots, piece)),
        in_specs=[anywhere, anywhere, hbm, hbm],
        out_specs=(vmem, vmem),
        scratch_shapes=[
            pltpu.VMEM((num_slot, LANES), F32),
            pltpu.VMEM((num_slot, 2 * piece), F32),
            pltpu.VMEM((num_off, freq), F32),
            pltpu.VMEM((num_src, freq), F32),
            pltpu.VMEM((slots, 2 * piece), F32),
            pltpu.VMEM((slots, 2 * piece), F32),
            pltpu.SemaphoreType.DMA((4,)),
        ],
        name="shares",
    )(sent, sums, offset_terms, source_terms)
    every = swap(off_new, slots)
    parts = [src_new]
    for k in range(1, rcv_n):
        ring = [(j, (j + k) % rcv_n) for j in range(rcv_n)]
        parts.append(lax.ppermute(src_new, "rcv", ring))
    receiver_new = pl.pallas_call(
        static(receiver_kernel, num_off, num_src),
        out_shape=shape(owned, freq),
        in_specs=[anywhere, anywhere, hbm],
        out_specs=vmem,
        scratch_shapes=[
            pltpu.VMEM((num_slot, 2 * edge + LANES), F32),
            pltpu.VMEM((num_slot, 2 * rest), F32),
            pltpu.VMEM((owned, freq), F32),
            pltpu.SemaphoreType.DMA((3,)),
        ],
        name="receiver",
    )(got, sums, receiver_terms)
    source_new = pl.pallas_call(
        static(source_kernel, rcv_n),
        out_shape=shape(num_src, freq),
        in_specs=[anywhere] * rcv_n,
        out_specs=vmem,
        scratch_shapes=[
            pltpu.VMEM((rcv_n, slots, piece), F32),
            pltpu.SemaphoreType.DMA((rcv_n,)),
        ],
        name="source",
    )(*parts)
    every = every.reshape(peers, off_rows, slots // off_rows, piece)[:, :, :rcv_n]
    offset_new = every.reshape(peers * off_rows, freq)[:num_off]
    return (source_new, receiver_new, offset_new)


def solution(mesh):
    return jax.shard_map(
        local,
        mesh=mesh,
        in_specs=(
            P(AXES, None),
            P(AXES),
            P(AXES),
            P(AXES),
            P(AXES, None, None),
            P("src", None),
            P(AXES, None),
            P(),
        ),
        out_specs=(P("src", None), P(AXES, None), P()),
        check_vma=False,
    )
```

```python
import math

import jax
import jax.numpy as jnp
import numpy as np
from jax import lax
from jax.experimental import pallas as pl
from jax.experimental.pallas import tpu as pltpu
from jax.sharding import PartitionSpec as P

AXES = ("src", "rcv")
LANES = 128
F32 = jnp.float32
BF16 = jnp.bfloat16
NT = (((1,), (1,)), ((), ()))
TN = (((0,), (0,)), ((), ()))
NN = (((1,), (0,)), ((), ()))


def twiddles(samples, first, last):
    half = samples // 2
    quarter = samples // 4
    lane = np.arange(LANES)
    even = np.where(lane % 2 == 0, lane, half - 1 + lane)
    odd = np.where(lane % 2 == 1, lane, half - 1 + lane + np.where(lane == 0, LANES, 0))
    freq = np.arange(quarter)
    groups = half // LANES
    unit = 2.0 * math.pi / samples
    base = []
    taper = []
    for rows, fold in ((even, -np.cos(even * quarter * unit)), (odd, np.sin(odd * quarter * unit))):
        phase = (rows[:, None] * freq[None, :] % samples) * unit
        sine = np.sin(phase)
        sine[:, 0] = np.round(fold)
        base += [np.cos(phase), sine]
        at = rows[:, None] + LANES * np.arange(groups)[None, :]
        taper.append((0.5 - 0.5 * np.cos((at + 0.5) * unit)) / math.sqrt(samples))
    turn = (LANES * np.arange(groups)[:, None] * freq[None, :] % samples) * unit
    turn = np.stack([np.cos(turn), np.sin(turn)])
    return (
        np.stack(base)[:, :, first:last].astype(np.float32),
        turn[:, :, first:last].astype(np.float32),
        np.stack(taper).astype(np.float32),
    )


def dot(a, b, dims=NN):
    return lax.dot_general(a, b, dims, preferred_element_type=F32)


def exact(a, b, dims=NN):
    return lax.dot_general(
        a, b, dims, precision=lax.Precision.HIGHEST, preferred_element_type=F32
    )


def pieces(value):
    one = value.astype(BF16)
    rest = value - one.astype(F32)
    two = rest.astype(BF16)
    return one, two, (rest - two.astype(F32)).astype(BF16)


def count_dot(counts, terms):
    counts = jnp.concatenate(halves(counts), axis=1)
    one, two, three = (jnp.concatenate([v, v], axis=0) for v in pieces(terms))
    return dot(counts, one) + dot(counts, two) + dot(counts, three)


def halves(counts):
    upper = counts.astype(BF16)
    return upper, (counts - upper.astype(F32)).astype(BF16)


def count_dot_tn(counts, terms):
    counts = jnp.concatenate(halves(counts), axis=0)
    one, two, three = (jnp.concatenate([v, v], axis=0) for v in pieces(terms))
    return dot(counts, one, TN) + dot(counts, two, TN) + dot(counts, three, TN)


def chosen_sum(chosen, value):
    one, two, three = pieces(value)
    return dot(chosen, one, TN) + dot(chosen, two, TN) + dot(chosen, three, TN)


def iota(shape, axis):
    return lax.broadcasted_iota(jnp.int32, shape, axis)


def hot(mask):
    return jnp.where(mask, 1.0, 0.0).astype(F32)


def ascend(value, lead):
    width = value.shape[1]
    row = iota((width, width), 0)
    col = iota((width, width), 1)
    if lead:
        pick = row == jnp.where(col == 0, 0, width - col)
    else:
        pick = row == width - 1 - col
    pick = hot(pick).astype(BF16)
    one, two, three = pieces(value)
    return dot(one, pick) + dot(two, pick) + dot(three, pick)


def join(low0, high0, low1, high1):
    edge = high1.shape[1]
    whole = jnp.concatenate([high1, high0], axis=1)
    col = iota(whole.shape, 1)
    shifted = pltpu.roll(whole, 1, 1)
    high = jnp.where(col <= edge, shifted, whole)
    high = jnp.where(col == 0, high0[:, :1], high)
    return jnp.concatenate([low0, low1, high], axis=1)


def part_of(value, first, width):
    half = value.shape[1] // 2
    high = value[:, half:]
    if first == 0:
        tail = high[:, half - width :]
        tail = jnp.where(iota(tail.shape, 1) == 0, high[:, :1], tail)
    else:
        tail = pltpu.roll(high, half - 1, 1)[:, :width]
    return jnp.concatenate([value[:, first : first + width], tail], axis=1)


def start(copies):
    for copy in copies:
        copy.start()


def wait(copies):
    for copy in copies:
        copy.wait()


def build_table(base, turn, taper, table):
    groups = taper.shape[2]
    width = base.shape[2]
    for side in range(2):
        for g in range(groups):
            cos0 = base[2 * side]
            sin0 = base[2 * side + 1]
            cos1 = turn[0, g : g + 1, :]
            sin1 = turn[1, g : g + 1, :]
            scale = taper[side, :, g : g + 1]
            at = slice(g * LANES, (g + 1) * LANES)
            table[side, at, :width] = ((cos0 * cos1 - sin0 * sin1) * scale).astype(BF16)
            table[side, at, width:] = ((sin0 * cos1 + cos0 * sin1) * -scale).astype(BF16)


def ident_rows(num_slot, num_off, rows, slot, off, src):
    top = iota((num_slot, slot.shape[1]), 0) == slot
    low = iota((rows - num_slot, slot.shape[1]), 0)
    low = (low == off) | (low == src + num_off)
    return jnp.concatenate([hot(top).astype(BF16), hot(low).astype(BF16)], axis=0)


def spectra_kernel(
    num_off, num_src, rcv_n, head, lead, tile,
    x_hbm, slot_hbm, off_hbm, src_hbm, lists_hbm, offset_hbm, source_hbm, own_hbm,
    counts_hbm, base_hbm, turn_hbm, taper_hbm, pay_hbm, joint_hbm, extra_hbm,
    x, ids, lists, terms, own, counts, extra, base, turn, taper, table, every, total, stage, spectrum, sems, x_sems,
):
    slots, peers = lists.shape
    num_slot = peers * slots
    rows = total.shape[0]
    width = base.shape[2]
    half = x.shape[1] // 2
    first = 0 if lead else width
    group = lax.axis_index("src")
    near = [
        pltpu.make_async_copy(base_hbm, base, sems.at[0]),
        pltpu.make_async_copy(turn_hbm, turn, sems.at[1]),
        pltpu.make_async_copy(taper_hbm, taper, sems.at[2]),
    ]
    far = [
        pltpu.make_async_copy(slot_hbm, ids.at[0], sems.at[3]),
        pltpu.make_async_copy(off_hbm, ids.at[1], sems.at[4]),
        pltpu.make_async_copy(src_hbm, ids.at[2], sems.at[5]),
        pltpu.make_async_copy(offset_hbm, terms.at[0:num_off], sems.at[6]),
        pltpu.make_async_copy(source_hbm, terms.at[num_off : num_off + num_src], sems.at[7]),
    ]
    if head:
        far.append(pltpu.make_async_copy(lists_hbm, lists, sems.at[8]))
    else:
        far.append(pltpu.make_async_copy(own_hbm, own, sems.at[8]))
        far.append(pltpu.make_async_copy(counts_hbm, counts, sems.at[9]))
    tiles = [
        pltpu.make_async_copy(
            x_hbm.at[t * tile : (t + 1) * tile], x.at[t * tile : (t + 1) * tile], x_sems.at[t]
        )
        for t in range(x.shape[0] // tile)
    ]
    start(far + near + tiles)
    spare = num_off + num_src
    terms[spare:, :] = jnp.zeros((terms.shape[0] - spare, terms.shape[1]), F32)
    total[...] = jnp.zeros_like(total)
    wait(far)
    src = ids[2] - group * num_src
    every[...] = ident_rows(num_slot, num_off, rows, ids[0], ids[1], src)
    last = []
    if head:
        at = iota((LANES, x.shape[0]), 0)
        joint = hot((at == ids[1]) | (at == src + num_off)).astype(BF16)
        counts[...] = dot(every[...], joint, NT)
        part = counts[:num_slot]
        whole = jnp.sum(part, axis=0, keepdims=True)
        row = iota((num_slot, LANES), 0)
        col = iota((num_slot, LANES), 1)
        peer = row // slots
        inner = row % slots
        off_rows = max(1, num_off // peers)
        src_rows = num_src // rcv_n
        is_off = (col == peer * off_rows + inner) & (inner < off_rows) & (col < num_off)
        is_src = (col == num_off + peer % rcv_n * src_rows + inner) & (inner < src_rows)
        is_src = is_src & (peer // rcv_n == group)
        num_o = jnp.sum(jnp.where(is_off, whole, 0.0), axis=1, keepdims=True)
        num_s = jnp.sum(jnp.where(is_src, whole, 0.0), axis=1, keepdims=True)
        spread = hot(iota((num_slot, peers), 0) // slots == iota((num_slot, peers), 1))
        listed = dot(spread.astype(BF16), lists[...].astype(F32).astype(BF16), NT)
        mine = iota((num_slot, slots), 0) % slots == iota((num_slot, slots), 1)
        asked = jnp.sum(jnp.where(mine, listed, 0.0), axis=1, keepdims=True)
        part = jnp.where(col == spare, asked, part)
        part = jnp.where(col == spare + 1, num_o, part)
        extra[...] = jnp.where(col == spare + 2, num_s, part)
        last.append(pltpu.make_async_copy(extra, pay_hbm.at[:, 2 * width :], sems.at[6]))
        last.append(pltpu.make_async_copy(counts, extra_hbm, sems.at[7]))
    else:
        kept = own[...]
        own[:, : 2 * width] = part_of(kept, width, width)
        own[:, 2 * width :] = part_of(kept, 0, width)
        last.append(pltpu.make_async_copy(own, extra_hbm, sems.at[6]))
    start(last)
    stage[...] = count_dot(counts[...], part_of(terms[...], first, width))
    wait(near)
    build_table(base, turn, taper, table)

    def transform(t):
        tiles[t].wait()
        lane = iota((tile, LANES), 1) % 2 == 0
        even = []
        odd = []
        for g in range(half // LANES):
            front = x[t * tile : (t + 1) * tile, g * LANES : (g + 1) * LANES]
            back = x[t * tile : (t + 1) * tile, half + g * LANES : half + (g + 1) * LANES]
            back = pltpu.roll(back, 1, 1)
            even.append(jnp.where(lane, front, back))
            odd.append(jnp.where(lane, back, front))
        spectrum[t % 2, :, : 2 * width] = dot(jnp.concatenate(even, axis=1), table[0])
        spectrum[t % 2, :, 2 * width :] = dot(jnp.concatenate(odd, axis=1), table[1])

    def collect(t):
        ec, es, oc, os = (
            spectrum[t % 2, :, k * width : (k + 1) * width] for k in range(4)
        )
        re_low, im_low = ec + oc, es + os
        re_high, im_high = ec - oc, es - os
        if lead:
            zero = iota((tile, width), 1) == 0
            im_low = jnp.where(zero, 0.0, im_low)
            re_high = jnp.where(zero, es, re_high)
            im_high = jnp.where(zero, os, im_high)
        power = jnp.concatenate(
            [re_low * re_low + im_low * im_low, re_high * re_high + im_high * im_high], axis=1
        )
        amp = 0.5 * jnp.log(power + 0.01)
        upper = amp.astype(BF16)
        lower = (amp - upper.astype(F32)).astype(BF16)
        ids_t = every[:, t * tile : (t + 1) * tile]
        total[...] += dot(ids_t, upper) + dot(ids_t, lower)

    transform(0)
    for t in range(1, len(tiles)):
        transform(t)
        collect(t - 1)
    collect(len(tiles) - 1)
    stage[:, :width] = total[:, :width] - stage[:, :width]
    stage[:, width:] = ascend(total[:, width:], lead) - stage[:, width:]
    out = [
        pltpu.make_async_copy(stage.at[:num_slot], pay_hbm.at[:, : 2 * width], sems.at[0]),
        pltpu.make_async_copy(stage.at[num_slot:], joint_hbm, sems.at[1]),
    ]
    start(out)
    wait(last + out)


def owner_hot(sent, base, owned):
    col = iota(sent.shape, 1)
    asked = jnp.sum(jnp.where(col == base, sent, 0.0), axis=1, keepdims=True).astype(jnp.int32)
    return hot(iota((sent.shape[0], owned), 1) == asked)


def pack_kernel(
    num_off, num_src, slots, src_n, rcv_n, got_hbm, joint0_hbm, joint1_hbm, own_hbm, _, out_hbm,
    got, joint, own, out, sems,
):
    edge = joint0_hbm.shape[1]
    rest = joint1_hbm.shape[1]
    freq = edge + rest
    copies = [
        pltpu.make_async_copy(got_hbm, got, sems.at[0]),
        pltpu.make_async_copy(joint0_hbm, joint.at[:, :edge], sems.at[1]),
        pltpu.make_async_copy(joint1_hbm, joint.at[:, edge:], sems.at[2]),
        pltpu.make_async_copy(own_hbm, own, sems.at[3]),
    ]
    start(copies)
    copies[0].wait()
    num = got.shape[0]
    group = lax.axis_index("src")
    sent = got[...]
    chosen = owner_hot(sent, num_off + num_src, own.shape[0]).astype(BF16)
    every_src = src_n * num_src
    col = iota((LANES, every_src), 0)
    pick = hot(col == num_off + iota((LANES, every_src), 1) % num_src).astype(BF16)
    from_group = iota((num, every_src), 0) // (slots * rcv_n)
    from_group = from_group == iota((num, every_src), 1) // num_src
    upper, lower = halves(sent)
    by_src = [jnp.where(from_group, dot(v, pick), 0.0).astype(BF16) for v in (upper, lower)]
    off_of = (dot(chosen, upper, TN) + dot(chosen, lower, TN))[:, :num_off]
    src_of = dot(chosen, by_src[0], TN) + dot(chosen, by_src[1], TN)
    wait(copies[1:])
    off_sum = joint[:num_off, :] - count_dot_tn(off_of, own[...])
    src_sum = -count_dot_tn(src_of, own[...])
    mine = joint[num_off : num_off + num_src, :]
    piece = freq // rcv_n
    per_off = slots // max(1, num_off // (src_n * rcv_n))
    per_src = slots // (num_src // rcv_n)
    if num_off * per_off < num or per_off > rcv_n:
        out[...] = jnp.zeros_like(out)
    each = piece // LANES
    copies = [
        pltpu.make_async_copy(
            out.at[h], out_hbm.at[:, rest + h * LANES : rest + (h + 1) * LANES], sems.at[h]
        )
        for h in range(2 * each)
    ]
    for h in range(each):
        for m in range(rcv_n):
            at = slice(m * piece + h * LANES, m * piece + (h + 1) * LANES)
            out[h, pl.ds(m, num_off, stride=per_off), :] = off_sum[:, at]
        copies[h].start()
    for h in range(each):
        for m in range(rcv_n):
            at = slice(m * piece + h * LANES, m * piece + (h + 1) * LANES)
            for i in range(src_n):
                to = pl.ds(i * num_src * per_src + m, num_src, stride=per_src)
                source = src_sum[i * num_src : (i + 1) * num_src, at]
                out[each + h, to, :] = source + jnp.where(group == i, mine[:, at], 0.0)
        copies[each + h].start()
    wait(copies)


def shares_kernel(
    num_off, num_src, slots, edge, got_hbm, sums_hbm, offset_hbm, source_hbm,
    off_out, src_out, sent, tail, offset, source, rows, block, sems,
):
    rcv_n = lax.axis_size("rcv")
    piece = src_out.shape[1]
    rest = sums_hbm.shape[1] - 2 * piece
    copies = [
        pltpu.make_async_copy(got_hbm, sent, sems.at[0]),
        pltpu.make_async_copy(sums_hbm.at[:, rest:], tail, sems.at[1]),
        pltpu.make_async_copy(offset_hbm, offset, sems.at[2]),
        pltpu.make_async_copy(source_hbm, source, sems.at[3]),
    ]
    start(copies)
    wait(copies)
    peers = sent.shape[0] // slots
    base = num_off + num_src
    both = sent[0:slots]
    value = tail[0:slots]
    for d in range(1, peers):
        both = both + sent[d * slots : (d + 1) * slots]
        value = value + tail[d * slots : (d + 1) * slots]
    rows[...] = value
    col = iota(both.shape, 1)
    num_o = jnp.sum(jnp.where(col == base + 1, both, 0.0), axis=1, keepdims=True)
    num_s = jnp.sum(jnp.where(col == base + 2, both, 0.0), axis=1, keepdims=True)
    here = lax.axis_index("rcv")
    off_rows = max(1, num_off // peers)
    src_rows = num_src // rcv_n
    at_off = (lax.axis_index("src") * rcv_n + here) * off_rows
    for count, num, at, first, terms in (
        (off_rows, num_o, slice(0, piece), at_off, offset),
        (src_rows, num_s, slice(piece, 2 * piece), here * src_rows, source),
    ):
        last = terms.shape[0] - 1
        parts = [
            jnp.concatenate(
                [rows[j * (slots // count) + m : j * (slots // count) + m + 1, at] for j in range(count)],
                axis=0,
            )
            for m in range(rcv_n)
        ]
        whole = jnp.concatenate(parts, axis=1)
        e, r = edge // 2, (whole.shape[1] - edge) // 2
        whole = join(
            whole[:, edge : edge + r], whole[:, edge + r :], whole[:, :e], whole[:, e:edge]
        )
        old = jnp.concatenate(
            [terms[pl.ds(jnp.minimum(first + j, last), 1), :] for j in range(count)], axis=0
        )
        new = old + whole / (num[:count] + 1.0)
        block[:, at] = jnp.zeros((slots, piece), F32)
        for j in range(count):
            for m in range(rcv_n):
                to = j * (slots // count) + m
                block[to : to + 1, at] = new[j : j + 1, m * piece : (m + 1) * piece]
    src_out[...] = block[:, piece:]
    done = block[:, :piece]
    for d in range(peers):
        off_out[d * slots : (d + 1) * slots, :] = done


def receiver_kernel(num_off, num_src, got_hbm, sums_hbm, terms_hbm, out, got, sums, terms, sems):
    edge = got.shape[1] - LANES
    rest = sums.shape[1]
    copies = [
        pltpu.make_async_copy(got_hbm, got, sems.at[0]),
        pltpu.make_async_copy(sums_hbm.at[:, :rest], sums, sems.at[1]),
        pltpu.make_async_copy(terms_hbm, terms, sems.at[2]),
    ]
    start(copies)
    wait(copies)
    sent = got[:, edge:]
    value = terms[...]
    chosen = owner_hot(sent, num_off + num_src, value.shape[0]).astype(BF16)
    per_slot = jnp.where(iota(sent.shape, 1) < num_off, sent, 0.0)
    num = jnp.sum(chosen_sum(chosen, per_slot), axis=1, keepdims=True)
    one = chosen_sum(chosen, got[:, :edge])
    two = chosen_sum(chosen, sums[...])
    edge //= 2
    rest //= 2
    total = join(two[:, :rest], two[:, rest:], one[:, :edge], one[:, edge:])
    out[...] = value + (total - num * value) / (num + 1.0)


def source_kernel(rcv_n, *refs):
    src_out, rest, sems = refs[rcv_n:]
    copies = [pltpu.make_async_copy(refs[k], rest.at[k], sems.at[k]) for k in range(rcv_n)]
    start(copies)
    wait(copies)
    slots, piece = rest.shape[1:]
    count = src_out.shape[0] // rcv_n
    here = lax.axis_index("rcv")
    for j in range(rcv_n):
        value = jnp.zeros((slots, piece), F32)
        for k in range(rcv_n):
            value = value + jnp.where((here + rcv_n - k) % rcv_n == j, rest[k], 0.0)
        for i in range(count):
            for m in range(rcv_n):
                row = i * (slots // count) + m
                src_out[j * count + i : j * count + i + 1, m * piece : (m + 1) * piece] = (
                    value[row : row + 1]
                )


def swap(value, slots):
    shape = value.shape
    value = value.reshape(shape[0] // slots, slots, shape[1])
    value = lax.all_to_all(value, AXES, split_axis=0, concat_axis=0, tiled=True)
    return value.reshape(shape)


def local(
    traces,
    trace_source,
    trace_offset,
    trace_slot,
    request_list,
    source_terms,
    receiver_terms,
    offset_terms,
):
    src_n = lax.axis_size("src")
    rcv_n = lax.axis_size("rcv")
    peers = src_n * rcv_n
    slots = request_list.shape[2]
    num_tr, samples = traces.shape
    owned, freq = receiver_terms.shape
    num_src = source_terms.shape[0]
    num_off = offset_terms.shape[0]
    num_slot = peers * slots
    joint = -(-(num_off + num_src) // 16) * 16
    rows = num_slot + joint
    half = freq // 2
    edge = half // 2
    rest = half - edge
    piece = freq // rcv_n
    off_rows = max(1, num_off // peers)
    tile = min(512, num_tr)
    assert slots == num_src and off_rows * rcv_n <= slots and num_off + num_src + 3 <= LANES
    assert samples == 2 * freq and freq % (4 * LANES) == 0 and owned <= 256
    ids = [v.reshape(1, num_tr) for v in (trace_slot, trace_offset, trace_source)]
    lists = jnp.swapaxes(request_list, 1, 2).reshape(slots, peers)
    vmem = pl.BlockSpec(memory_space=pltpu.VMEM)
    hbm = pl.BlockSpec(memory_space=pltpu.HBM)
    anywhere = pl.BlockSpec(memory_space=pl.ANY)

    def static(kernel, *args):
        return lambda *refs: kernel(*args, *refs)

    def shape(*dims):
        return jax.ShapeDtypeStruct(dims, F32)

    def spectra(head, width, counts):
        lead = not head
        first = 0 if lead else half - width
        consts = [jnp.asarray(v) for v in twiddles(samples, first, first + width)]
        return pl.pallas_call(
            static(spectra_kernel, num_off, num_src, rcv_n, head, lead, tile),
            out_shape=(
                shape(num_slot, 2 * width + (LANES if head else 2 * piece)),
                shape(joint, 2 * width),
                shape(rows, LANES) if head else shape(owned, freq),
            ),
            in_specs=[hbm] * 12,
            out_specs=(hbm, hbm, hbm),
            scratch_shapes=[
                pltpu.VMEM((num_tr, samples), BF16),
                pltpu.VMEM((3, 1, num_tr), jnp.int32),
                pltpu.VMEM((slots, peers), jnp.int32),
                pltpu.VMEM((LANES, freq), F32),
                pltpu.VMEM((owned, freq), F32),
                pltpu.VMEM((rows, LANES), F32),
                pltpu.VMEM((num_slot, LANES), F32),
                pltpu.VMEM(consts[0].shape, F32),
                pltpu.VMEM(consts[1].shape, F32),
                pltpu.VMEM(consts[2].shape, F32),
                pltpu.VMEM((2, freq, 2 * width), BF16),
                pltpu.VMEM((rows, num_tr), BF16),
                pltpu.VMEM((rows, 2 * width), F32),
                pltpu.VMEM((rows, 2 * width), F32),
                pltpu.VMEM((2, tile, 4 * width), F32),
                pltpu.SemaphoreType.DMA((10,)),
                pltpu.SemaphoreType.DMA((num_tr // tile,)),
            ],
            compiler_params=pltpu.CompilerParams(vmem_limit_bytes=56 * 2**20),
            name="spectra%d" % head,
        )(traces, *ids, lists, offset_terms, source_terms, receiver_terms, counts, *consts)

    pay, joint0, counts = spectra(True, edge, offset_terms)
    got = swap(pay, slots)
    sent = got[:, 2 * edge :]
    pay, joint1, own = spectra(False, rest, counts)
    pay = pl.pallas_call(
        static(pack_kernel, num_off, num_src, slots, src_n, rcv_n),
        out_shape=shape(*pay.shape),
        in_specs=[anywhere] + [hbm] * 4,
        out_specs=hbm,
        scratch_shapes=[
            pltpu.VMEM((num_slot, LANES), F32),
            pltpu.VMEM((joint, freq), F32),
            pltpu.VMEM((owned, freq), F32),
            pltpu.VMEM((2 * piece // LANES, num_slot, LANES), F32),
            pltpu.SemaphoreType.DMA((max(4, 2 * piece // LANES),)),
        ],
        input_output_aliases={4: 0},
        name="pack",
    )(sent, joint0, joint1, own, pay)
    sums = swap(pay, slots)

    off_new, src_new = pl.pallas_call(
        static(shares_kernel, num_off, num_src, slots, 2 * edge),
        out_shape=(shape(num_slot, piece), shape(slots, piece)),
        in_specs=[anywhere, anywhere, hbm, hbm],
        out_specs=(vmem, vmem),
        scratch_shapes=[
            pltpu.VMEM((num_slot, LANES), F32),
            pltpu.VMEM((num_slot, 2 * piece), F32),
            pltpu.VMEM((num_off, freq), F32),
            pltpu.VMEM((num_src, freq), F32),
            pltpu.VMEM((slots, 2 * piece), F32),
            pltpu.VMEM((slots, 2 * piece), F32),
            pltpu.SemaphoreType.DMA((4,)),
        ],
        name="shares",
    )(sent, sums, offset_terms, source_terms)
    every = swap(off_new, slots)
    parts = [src_new]
    for k in range(1, rcv_n):
        ring = [(j, (j + k) % rcv_n) for j in range(rcv_n)]
        parts.append(lax.ppermute(src_new, "rcv", ring))
    receiver_new = pl.pallas_call(
        static(receiver_kernel, num_off, num_src),
        out_shape=shape(owned, freq),
        in_specs=[anywhere, anywhere, hbm],
        out_specs=vmem,
        scratch_shapes=[
            pltpu.VMEM((num_slot, 2 * edge + LANES), F32),
            pltpu.VMEM((num_slot, 2 * rest), F32),
            pltpu.VMEM((owned, freq), F32),
            pltpu.SemaphoreType.DMA((3,)),
        ],
        name="receiver",
    )(got, sums, receiver_terms)
    source_new = pl.pallas_call(
        static(source_kernel, rcv_n),
        out_shape=shape(num_src, freq),
        in_specs=[anywhere] * rcv_n,
        out_specs=vmem,
        scratch_shapes=[
            pltpu.VMEM((rcv_n, slots, piece), F32),
            pltpu.SemaphoreType.DMA((rcv_n,)),
        ],
        name="source",
    )(*parts)
    every = every.reshape(peers, off_rows, slots // off_rows, piece)[:, :, :rcv_n]
    offset_new = every.reshape(peers * off_rows, freq)[:num_off]
    return (source_new, receiver_new, offset_new)


def solution(mesh):
    return jax.shard_map(
        local,
        mesh=mesh,
        in_specs=(
            P(AXES, None),
            P(AXES),
            P(AXES),
            P(AXES),
            P(AXES, None, None),
            P("src", None),
            P(AXES, None),
            P(),
        ),
        out_specs=(P("src", None), P(AXES, None), P()),
        check_vma=False,
    )
```

```python
import math

import jax
import jax.numpy as jnp
import numpy as np
from jax import lax
from jax.experimental import pallas as pl
from jax.experimental.pallas import tpu as pltpu
from jax.sharding import PartitionSpec as P

AXES = ("src", "rcv")
LANES = 128
F32 = jnp.float32
BF16 = jnp.bfloat16
NT = (((1,), (1,)), ((), ()))
TN = (((0,), (0,)), ((), ()))
NN = (((1,), (0,)), ((), ()))


def twiddles(samples, first, last):
    half = samples // 2
    quarter = samples // 4
    lane = np.arange(LANES)
    even = np.where(lane % 2 == 0, lane, half - 1 + lane)
    odd = np.where(lane % 2 == 1, lane, half - 1 + lane + np.where(lane == 0, LANES, 0))
    freq = np.arange(quarter)
    groups = half // LANES
    unit = 2.0 * math.pi / samples
    base = []
    taper = []
    for rows, fold in ((even, -np.cos(even * quarter * unit)), (odd, np.sin(odd * quarter * unit))):
        phase = (rows[:, None] * freq[None, :] % samples) * unit
        sine = np.sin(phase)
        sine[:, 0] = np.round(fold)
        base += [np.cos(phase), sine]
        at = rows[:, None] + LANES * np.arange(groups)[None, :]
        taper.append((0.5 - 0.5 * np.cos((at + 0.5) * unit)) / math.sqrt(samples))
    turn = (LANES * np.arange(groups)[:, None] * freq[None, :] % samples) * unit
    turn = np.stack([np.cos(turn), np.sin(turn)])
    return (
        np.stack(base)[:, :, first:last].astype(np.float32),
        turn[:, :, first:last].astype(np.float32),
        np.stack(taper).astype(np.float32),
    )


def dot(a, b, dims=NN):
    return lax.dot_general(a, b, dims, preferred_element_type=F32)


def exact(a, b, dims=NN):
    return lax.dot_general(
        a, b, dims, precision=lax.Precision.HIGHEST, preferred_element_type=F32
    )


def pieces(value):
    one = value.astype(BF16)
    rest = value - one.astype(F32)
    two = rest.astype(BF16)
    return one, two, (rest - two.astype(F32)).astype(BF16)


def count_dot(counts, terms):
    counts = jnp.concatenate(halves(counts), axis=1)
    one, two, three = (jnp.concatenate([v, v], axis=0) for v in pieces(terms))
    return dot(counts, one) + dot(counts, two) + dot(counts, three)


def halves(counts):
    upper = counts.astype(BF16)
    return upper, (counts - upper.astype(F32)).astype(BF16)


def count_dot_tn(counts, terms):
    counts = jnp.concatenate(halves(counts), axis=0)
    one, two, three = (jnp.concatenate([v, v], axis=0) for v in pieces(terms))
    return dot(counts, one, TN) + dot(counts, two, TN) + dot(counts, three, TN)


def chosen_sum(chosen, value):
    one, two, three = pieces(value)
    return dot(chosen, one, TN) + dot(chosen, two, TN) + dot(chosen, three, TN)


def iota(shape, axis):
    return lax.broadcasted_iota(jnp.int32, shape, axis)


def hot(mask):
    return jnp.where(mask, 1.0, 0.0).astype(F32)


def ascend(value, lead):
    width = value.shape[1]
    row = iota((width, width), 0)
    col = iota((width, width), 1)
    if lead:
        pick = row == jnp.where(col == 0, 0, width - col)
    else:
        pick = row == width - 1 - col
    pick = hot(pick).astype(BF16)
    one, two, three = pieces(value)
    return dot(one, pick) + dot(two, pick) + dot(three, pick)


def join(low0, high0, low1, high1):
    edge = high1.shape[1]
    whole = jnp.concatenate([high1, high0], axis=1)
    col = iota(whole.shape, 1)
    shifted = pltpu.roll(whole, 1, 1)
    high = jnp.where(col <= edge, shifted, whole)
    high = jnp.where(col == 0, high0[:, :1], high)
    return jnp.concatenate([low0, low1, high], axis=1)


def part_of(value, first, width):
    half = value.shape[1] // 2
    high = value[:, half:]
    if first == 0:
        tail = high[:, half - width :]
        tail = jnp.where(iota(tail.shape, 1) == 0, high[:, :1], tail)
    else:
        tail = pltpu.roll(high, half - 1, 1)[:, :width]
    return jnp.concatenate([value[:, first : first + width], tail], axis=1)


def joint_rows(num_off, num_src):
    return -(-(num_off + num_src) // 16) * 16


def start(copies):
    for copy in copies:
        copy.start()


def wait(copies):
    for copy in copies:
        copy.wait()


def build_table(base, turn, taper, table):
    groups = taper.shape[2]
    width = base.shape[2]
    for side in range(2):
        for g in range(groups):
            cos0 = base[2 * side]
            sin0 = base[2 * side + 1]
            cos1 = turn[0, g : g + 1, :]
            sin1 = turn[1, g : g + 1, :]
            scale = taper[side, :, g : g + 1]
            at = slice(g * LANES, (g + 1) * LANES)
            table[side, at, :width] = ((cos0 * cos1 - sin0 * sin1) * scale).astype(BF16)
            table[side, at, width:] = ((sin0 * cos1 + cos0 * sin1) * -scale).astype(BF16)


def ident_rows(num_slot, num_off, rows, slot, off, src):
    top = iota((num_slot, slot.shape[1]), 0) == slot
    low = iota((rows - num_slot, slot.shape[1]), 0)
    low = (low == off) | (low == src + num_off)
    return jnp.concatenate([hot(top).astype(BF16), hot(low).astype(BF16)], axis=0)


def spectra_kernel(
    num_off, num_src, rcv_n, head, lead, tile,
    x_hbm, slot_hbm, off_hbm, src_hbm, lists_hbm, offset_hbm, source_hbm, own_hbm,
    counts_hbm, joint0_hbm, base_hbm, turn_hbm, taper_hbm, pay_hbm, joint_hbm, extra_hbm,
    joint0, swapped, x, ids, lists, terms, own, counts, extra, base, turn, taper, table, every, total, stage, spectrum, sems, x_sems,
):
    slots, peers = lists.shape
    num_slot = peers * slots
    rows = total.shape[0]
    width = base.shape[2]
    half = x.shape[1] // 2
    first = 0 if lead else width
    group = lax.axis_index("src")
    near = [
        pltpu.make_async_copy(base_hbm, base, sems.at[0]),
        pltpu.make_async_copy(turn_hbm, turn, sems.at[1]),
        pltpu.make_async_copy(taper_hbm, taper, sems.at[2]),
    ]
    far = [
        pltpu.make_async_copy(slot_hbm, ids.at[0], sems.at[3]),
        pltpu.make_async_copy(off_hbm, ids.at[1], sems.at[4]),
        pltpu.make_async_copy(src_hbm, ids.at[2], sems.at[5]),
        pltpu.make_async_copy(offset_hbm, terms.at[0:num_off], sems.at[6]),
        pltpu.make_async_copy(source_hbm, terms.at[num_off : num_off + num_src], sems.at[7]),
    ]
    if head:
        far.append(pltpu.make_async_copy(lists_hbm, lists, sems.at[8]))
    else:
        far.append(pltpu.make_async_copy(own_hbm, own, sems.at[8]))
        far.append(pltpu.make_async_copy(counts_hbm, counts, sems.at[9]))
        far.append(pltpu.make_async_copy(joint0_hbm, joint0, sems.at[10]))
    tiles = [
        pltpu.make_async_copy(
            x_hbm.at[t * tile : (t + 1) * tile], x.at[t * tile : (t + 1) * tile], x_sems.at[t]
        )
        for t in range(x.shape[0] // tile)
    ]
    start(far + near + tiles)
    spare = num_off + num_src
    terms[spare:, :] = jnp.zeros((terms.shape[0] - spare, terms.shape[1]), F32)
    total[...] = jnp.zeros_like(total)
    wait(far + near)
    src = ids[2] - group * num_src
    every[...] = ident_rows(num_slot, num_off, rows, ids[0], ids[1], src)
    last = []
    if head:
        at = iota((LANES, x.shape[0]), 0)
        joint = hot((at == ids[1]) | (at == src + num_off)).astype(BF16)
        counts[...] = dot(every[...], joint, NT)
        part = counts[:num_slot]
        whole = jnp.sum(part, axis=0, keepdims=True)
        row = iota((num_slot, LANES), 0)
        col = iota((num_slot, LANES), 1)
        peer = row // slots
        inner = row % slots
        off_rows = max(1, num_off // peers)
        src_rows = num_src // rcv_n
        is_off = (col == peer * off_rows + inner) & (inner < off_rows) & (col < num_off)
        is_src = (col == num_off + peer % rcv_n * src_rows + inner) & (inner < src_rows)
        is_src = is_src & (peer // rcv_n == group)
        num_o = jnp.sum(jnp.where(is_off, whole, 0.0), axis=1, keepdims=True)
        num_s = jnp.sum(jnp.where(is_src, whole, 0.0), axis=1, keepdims=True)
        spread = hot(iota((num_slot, peers), 0) // slots == iota((num_slot, peers), 1))
        listed = dot(spread.astype(BF16), lists[...].astype(F32).astype(BF16), NT)
        mine = iota((num_slot, slots), 0) % slots == iota((num_slot, slots), 1)
        asked = jnp.sum(jnp.where(mine, listed, 0.0), axis=1, keepdims=True)
        part = jnp.where(col == spare, asked, part)
        part = jnp.where(col == spare + 1, num_o, part)
        extra[:, :LANES] = jnp.where(col == spare + 2, num_s, part)
        for p in range(peers):
            mate = p ^ 1
            extra[p * slots : (p + 1) * slots, LANES:] = extra[
                mate * slots : (mate + 1) * slots, :LANES
            ]
        last.append(pltpu.make_async_copy(extra, pay_hbm.at[:, 2 * width :], sems.at[6]))
        last.append(pltpu.make_async_copy(counts, extra_hbm, sems.at[7]))
    else:
        kept = own[...]
        own[:, : 2 * width] = part_of(kept, width, width)
        own[:, 2 * width :] = part_of(kept, 0, width)
    start(last)
    stage[...] = count_dot(counts[...], part_of(terms[...], first, width))
    build_table(base, turn, taper, table)

    def transform(t):
        tiles[t].wait()
        lane = iota((tile, LANES), 1) % 2 == 0
        even = []
        odd = []
        for g in range(half // LANES):
            front = x[t * tile : (t + 1) * tile, g * LANES : (g + 1) * LANES]
            back = x[t * tile : (t + 1) * tile, half + g * LANES : half + (g + 1) * LANES]
            back = pltpu.roll(back, 1, 1)
            even.append(jnp.where(lane, front, back))
            odd.append(jnp.where(lane, back, front))
        spectrum[t % 2, :, : 2 * width] = dot(jnp.concatenate(even, axis=1), table[0])
        spectrum[t % 2, :, 2 * width :] = dot(jnp.concatenate(odd, axis=1), table[1])

    def collect(t):
        ec, es, oc, os = (
            spectrum[t % 2, :, k * width : (k + 1) * width] for k in range(4)
        )
        re_low, im_low = ec + oc, es + os
        re_high, im_high = ec - oc, es - os
        if lead:
            zero = iota((tile, width), 1) == 0
            im_low = jnp.where(zero, 0.0, im_low)
            re_high = jnp.where(zero, es, re_high)
            im_high = jnp.where(zero, os, im_high)
        power = jnp.concatenate(
            [re_low * re_low + im_low * im_low, re_high * re_high + im_high * im_high], axis=1
        )
        amp = 0.5 * jnp.log(power + 0.01)
        upper = amp.astype(BF16)
        lower = (amp - upper.astype(F32)).astype(BF16)
        ids_t = every[:, t * tile : (t + 1) * tile]
        total[...] += dot(ids_t, upper) + dot(ids_t, lower)

    transform(0)
    for t in range(1, len(tiles)):
        transform(t)
        collect(t - 1)
    collect(len(tiles) - 1)
    stage[:, :width] = total[:, :width] - stage[:, :width]
    stage[:, width:] = ascend(total[:, width:], lead) - stage[:, width:]
    out = [pltpu.make_async_copy(stage.at[:num_slot], pay_hbm.at[:, : 2 * width], sems.at[0])]
    if head:
        out.append(pltpu.make_async_copy(stage.at[num_slot:], joint_hbm, sems.at[1]))
    else:
        odd = lax.axis_index("rcv") % 2 == 1
        cut = rows - num_slot
        for m in range(2 * width // LANES):
            lo, hi = 2 * m * LANES, (2 * m + 1) * LANES
            if hi < 2 * width:
                sums = joint0[:, lo:hi], joint0[:, hi : hi + LANES]
            else:
                lo, hi = lo - 2 * width, hi - 2 * width
                sums = stage[num_slot:, lo:hi], stage[num_slot:, hi : hi + LANES]
            both = own[:, 2 * m * LANES : (2 * m + 1) * LANES], own[:, (2 * m + 1) * LANES : (2 * m + 2) * LANES]
            at = slice(m * LANES, (m + 1) * LANES)
            swapped[0, :cut, at] = jnp.where(odd, sums[1], sums[0])
            swapped[1, :cut, at] = jnp.where(odd, sums[0], sums[1])
            swapped[0, cut:, at] = jnp.where(odd, both[1], both[0])
            swapped[1, cut:, at] = jnp.where(odd, both[0], both[1])
        out.append(pltpu.make_async_copy(swapped.at[0], joint_hbm, sems.at[1]))
        out.append(pltpu.make_async_copy(swapped.at[1], extra_hbm, sems.at[2]))
    start(out)
    wait(last + out)


def owner_hot(sent, base, owned):
    col = iota(sent.shape, 1)
    asked = jnp.sum(jnp.where(col == base, sent, 0.0), axis=1, keepdims=True).astype(jnp.int32)
    return hot(iota((sent.shape[0], owned), 1) == asked)


def pack_kernel(
    num_off, num_src, slots, src_n, rcv_n, sent_hbm, keep_hbm, mate_hbm, _, out_hbm,
    sent, keep, mate, out, sems,
):
    half = keep.shape[1]
    owned = keep.shape[0] - joint_rows(num_off, num_src)
    copies = [
        pltpu.make_async_copy(sent_hbm, sent, sems.at[0]),
        pltpu.make_async_copy(keep_hbm, keep, sems.at[1]),
        pltpu.make_async_copy(mate_hbm, mate, sems.at[2]),
    ]
    start(copies)
    copies[0].wait()
    num = sent.shape[0]
    group = lax.axis_index("src")
    every_src = src_n * num_src
    col = iota((LANES, every_src), 0)
    pick = hot(col == num_off + iota((LANES, every_src), 1) % num_src).astype(BF16)
    from_group = iota((num, every_src), 0) // (slots * rcv_n)
    from_group = from_group == iota((num, every_src), 1) // num_src
    off_of = []
    src_of = []
    for k in range(2):
        part = sent[:, k * LANES : (k + 1) * LANES]
        chosen = owner_hot(part, num_off + num_src, owned).astype(BF16)
        upper, lower = halves(part)
        by_src = [jnp.where(from_group, dot(v, pick), 0.0).astype(BF16) for v in (upper, lower)]
        off_of.append((dot(chosen, upper, TN) + dot(chosen, lower, TN))[:, :num_off])
        src_of.append(dot(chosen, by_src[0], TN) + dot(chosen, by_src[1], TN))
    wait(copies[1:])
    cut = keep.shape[0] - owned
    terms = jnp.concatenate([keep[cut:, :], mate[cut:, :]], axis=0)
    sums = keep[:cut, :] + mate[:cut, :]
    off_sum = sums[:num_off] - count_dot_tn(jnp.concatenate(off_of, axis=0), terms)
    src_sum = -count_dot_tn(jnp.concatenate(src_of, axis=0), terms)
    mine = sums[num_off : num_off + num_src]
    per_off = slots // max(1, num_off // (src_n * rcv_n))
    per_src = slots // (num_src // rcv_n)
    if num_off * per_off < num or per_off > rcv_n:
        out[...] = jnp.zeros_like(out)
    copies = [
        pltpu.make_async_copy(
            out.at[h], out_hbm.at[:, half + h * LANES : half + (h + 1) * LANES], sems.at[h]
        )
        for h in range(2)
    ]
    for m in range(rcv_n):
        at = slice(m * LANES, (m + 1) * LANES)
        out[0, pl.ds(m, num_off, stride=per_off), :] = off_sum[:, at]
    copies[0].start()
    for m in range(rcv_n):
        at = slice(m * LANES, (m + 1) * LANES)
        for i in range(src_n):
            to = pl.ds(i * num_src * per_src + m, num_src, stride=per_src)
            source = src_sum[i * num_src : (i + 1) * num_src, at]
            out[1, to, :] = source + jnp.where(group == i, mine[:, at], 0.0)
    copies[1].start()
    wait(copies)


def shares_kernel(
    num_off, num_src, slots, edge, got_hbm, sums_hbm, offset_hbm, source_hbm,
    off_out, src_out, sent, tail, offset, source, rows, block, sems,
):
    rcv_n = lax.axis_size("rcv")
    piece = src_out.shape[1]
    rest = sums_hbm.shape[1] - piece
    copies = [
        pltpu.make_async_copy(got_hbm.at[:, :LANES], sent, sems.at[0]),
        pltpu.make_async_copy(sums_hbm.at[:, rest:], tail, sems.at[1]),
        pltpu.make_async_copy(offset_hbm, offset, sems.at[2]),
        pltpu.make_async_copy(source_hbm, source, sems.at[3]),
    ]
    start(copies)
    wait(copies)
    peers = sent.shape[0] // slots
    base = num_off + num_src
    both = sent[0:slots]
    for d in range(1, peers):
        both = both + sent[d * slots : (d + 1) * slots]
    for k in range(2):
        value = tail[k * slots : (k + 1) * slots]
        for d in range(k + 2, peers, 2):
            value = value + tail[d * slots : (d + 1) * slots]
        rows[:, k * LANES : (k + 1) * LANES] = value[:, :LANES]
        rows[:, piece + k * LANES : piece + (k + 1) * LANES] = value[:, LANES:]
    col = iota(both.shape, 1)
    num_o = jnp.sum(jnp.where(col == base + 1, both, 0.0), axis=1, keepdims=True)
    num_s = jnp.sum(jnp.where(col == base + 2, both, 0.0), axis=1, keepdims=True)
    here = lax.axis_index("rcv")
    off_rows = max(1, num_off // peers)
    src_rows = num_src // rcv_n
    at_off = (lax.axis_index("src") * rcv_n + here) * off_rows
    for count, num, at, first, terms in (
        (off_rows, num_o, slice(0, piece), at_off, offset),
        (src_rows, num_s, slice(piece, 2 * piece), here * src_rows, source),
    ):
        last = terms.shape[0] - 1
        parts = [
            jnp.concatenate(
                [rows[j * (slots // count) + m : j * (slots // count) + m + 1, at] for j in range(count)],
                axis=0,
            )
            for m in range(rcv_n)
        ]
        whole = jnp.concatenate(parts, axis=1)
        e, r = edge // 2, (whole.shape[1] - edge) // 2
        whole = join(
            whole[:, edge : edge + r], whole[:, edge + r :], whole[:, :e], whole[:, e:edge]
        )
        old = jnp.concatenate(
            [terms[pl.ds(jnp.minimum(first + j, last), 1), :] for j in range(count)], axis=0
        )
        new = old + whole / (num[:count] + 1.0)
        block[:, at] = jnp.zeros((slots, piece), F32)
        for j in range(count):
            for m in range(rcv_n):
                to = j * (slots // count) + m
                block[to : to + 1, at] = new[j : j + 1, m * piece : (m + 1) * piece]
    src_out[...] = block[:, piece:]
    done = block[:, :piece]
    for d in range(peers):
        off_out[d * slots : (d + 1) * slots, :] = done


def receiver_kernel(num_off, num_src, got_hbm, sums_hbm, terms_hbm, out, got, sums, terms, sems):
    edge = got.shape[1] - LANES
    rest = sums.shape[1]
    copies = [
        pltpu.make_async_copy(got_hbm.at[:, : edge + LANES], got, sems.at[0]),
        pltpu.make_async_copy(sums_hbm.at[:, :rest], sums, sems.at[1]),
        pltpu.make_async_copy(terms_hbm, terms, sems.at[2]),
    ]
    start(copies)
    wait(copies)
    sent = got[:, edge:]
    value = terms[...]
    chosen = owner_hot(sent, num_off + num_src, value.shape[0]).astype(BF16)
    per_slot = jnp.where(iota(sent.shape, 1) < num_off, sent, 0.0)
    num = jnp.sum(chosen_sum(chosen, per_slot), axis=1, keepdims=True)
    one = chosen_sum(chosen, got[:, :edge])
    two = chosen_sum(chosen, sums[...])
    edge //= 2
    rest //= 2
    total = join(two[:, :rest], two[:, rest:], one[:, :edge], one[:, edge:])
    out[...] = value + (total - num * value) / (num + 1.0)


def source_kernel(rcv_n, *refs):
    src_out, rest, sems = refs[rcv_n:]
    copies = [pltpu.make_async_copy(refs[k], rest.at[k], sems.at[k]) for k in range(rcv_n)]
    start(copies)
    wait(copies)
    slots, piece = rest.shape[1:]
    count = src_out.shape[0] // rcv_n
    here = lax.axis_index("rcv")
    for j in range(rcv_n):
        value = jnp.zeros((slots, piece), F32)
        for k in range(rcv_n):
            value = value + jnp.where((here + rcv_n - k) % rcv_n == j, rest[k], 0.0)
        for i in range(count):
            for m in range(rcv_n):
                row = i * (slots // count) + m
                src_out[j * count + i : j * count + i + 1, m * piece : (m + 1) * piece] = (
                    value[row : row + 1]
                )


def swap(value, slots):
    shape = value.shape
    value = value.reshape(shape[0] // slots, slots, shape[1])
    value = lax.all_to_all(value, AXES, split_axis=0, concat_axis=0, tiled=True)
    return value.reshape(shape)


def local(
    traces,
    trace_source,
    trace_offset,
    trace_slot,
    request_list,
    source_terms,
    receiver_terms,
    offset_terms,
):
    src_n = lax.axis_size("src")
    rcv_n = lax.axis_size("rcv")
    peers = src_n * rcv_n
    slots = request_list.shape[2]
    num_tr, samples = traces.shape
    owned, freq = receiver_terms.shape
    num_src = source_terms.shape[0]
    num_off = offset_terms.shape[0]
    num_slot = peers * slots
    joint = joint_rows(num_off, num_src)
    rows = num_slot + joint
    half = freq // 2
    edge = half // 2
    rest = half - edge
    piece = freq // rcv_n
    off_rows = max(1, num_off // peers)
    tile = min(512, num_tr)
    assert slots == num_src and off_rows * rcv_n <= slots and num_off + num_src + 3 <= LANES
    assert samples == 2 * freq and freq % (4 * LANES) == 0 and owned <= 256
    assert rcv_n % 2 == 0 and piece == 2 * LANES and edge == rest
    ids = [v.reshape(1, num_tr) for v in (trace_slot, trace_offset, trace_source)]
    lists = jnp.swapaxes(request_list, 1, 2).reshape(slots, peers)
    vmem = pl.BlockSpec(memory_space=pltpu.VMEM)
    hbm = pl.BlockSpec(memory_space=pltpu.HBM)
    anywhere = pl.BlockSpec(memory_space=pl.ANY)

    def static(kernel, *args):
        return lambda *refs: kernel(*args, *refs)

    def shape(*dims):
        return jax.ShapeDtypeStruct(dims, F32)

    def spectra(head, width, counts, joint0):
        lead = not head
        first = 0 if lead else half - width
        consts = [jnp.asarray(v) for v in twiddles(samples, first, first + width)]
        return pl.pallas_call(
            static(spectra_kernel, num_off, num_src, rcv_n, head, lead, tile),
            out_shape=(
                shape(num_slot, 2 * width + (2 * LANES if head else piece)),
                shape(joint, 2 * width) if head else shape(joint + owned, half),
                shape(rows, LANES) if head else shape(joint + owned, half),
            ),
            in_specs=[hbm] * 13,
            out_specs=(hbm, hbm, hbm),
            scratch_shapes=[
                pltpu.VMEM((joint, half), F32),
                pltpu.VMEM((2, joint + owned, half), F32),
                pltpu.VMEM((num_tr, samples), BF16),
                pltpu.VMEM((3, 1, num_tr), jnp.int32),
                pltpu.VMEM((slots, peers), jnp.int32),
                pltpu.VMEM((LANES, freq), F32),
                pltpu.VMEM((owned, freq), F32),
                pltpu.VMEM((rows, LANES), F32),
                pltpu.VMEM((num_slot, 2 * LANES), F32),
                pltpu.VMEM(consts[0].shape, F32),
                pltpu.VMEM(consts[1].shape, F32),
                pltpu.VMEM(consts[2].shape, F32),
                pltpu.VMEM((2, freq, 2 * width), BF16),
                pltpu.VMEM((rows, num_tr), BF16),
                pltpu.VMEM((rows, 2 * width), F32),
                pltpu.VMEM((rows, 2 * width), F32),
                pltpu.VMEM((2, tile, 4 * width), F32),
                pltpu.SemaphoreType.DMA((11,)),
                pltpu.SemaphoreType.DMA((num_tr // tile,)),
            ],
            compiler_params=pltpu.CompilerParams(vmem_limit_bytes=56 * 2**20),
            name="spectra%d" % head,
        )(traces, *ids, lists, offset_terms, source_terms, receiver_terms, counts, joint0, *consts)

    pay, joint0, counts = spectra(True, edge, offset_terms, source_terms)
    got = swap(pay, slots)
    sent = got[:, 2 * edge :]
    pay, keep, mate = spectra(False, rest, counts, joint0)
    mate = lax.ppermute(mate, "rcv", [(j, j ^ 1) for j in range(rcv_n)])
    pay = pl.pallas_call(
        static(pack_kernel, num_off, num_src, slots, src_n, rcv_n),
        out_shape=shape(*pay.shape),
        in_specs=[anywhere, hbm, anywhere, hbm],
        out_specs=hbm,
        scratch_shapes=[
            pltpu.VMEM((num_slot, 2 * LANES), F32),
            pltpu.VMEM((joint + owned, half), F32),
            pltpu.VMEM((joint + owned, half), F32),
            pltpu.VMEM((2, num_slot, LANES), F32),
            pltpu.SemaphoreType.DMA((3,)),
        ],
        input_output_aliases={3: 0},
        name="pack",
    )(sent, keep, mate, pay)
    sums = swap(pay, slots)

    off_new, src_new = pl.pallas_call(
        static(shares_kernel, num_off, num_src, slots, 2 * edge),
        out_shape=(shape(num_slot, piece), shape(slots, piece)),
        in_specs=[anywhere, anywhere, hbm, hbm],
        out_specs=(vmem, vmem),
        scratch_shapes=[
            pltpu.VMEM((num_slot, LANES), F32),
            pltpu.VMEM((num_slot, piece), F32),
            pltpu.VMEM((num_off, freq), F32),
            pltpu.VMEM((num_src, freq), F32),
            pltpu.VMEM((slots, 2 * piece), F32),
            pltpu.VMEM((slots, 2 * piece), F32),
            pltpu.SemaphoreType.DMA((4,)),
        ],
        name="shares",
    )(sent, sums, offset_terms, source_terms)
    every = swap(off_new, slots)
    parts = [src_new]
    for k in range(1, rcv_n):
        ring = [(j, (j + k) % rcv_n) for j in range(rcv_n)]
        parts.append(lax.ppermute(src_new, "rcv", ring))
    receiver_new = pl.pallas_call(
        static(receiver_kernel, num_off, num_src),
        out_shape=shape(owned, freq),
        in_specs=[anywhere, anywhere, hbm],
        out_specs=vmem,
        scratch_shapes=[
            pltpu.VMEM((num_slot, 2 * edge + LANES), F32),
            pltpu.VMEM((num_slot, 2 * rest), F32),
            pltpu.VMEM((owned, freq), F32),
            pltpu.SemaphoreType.DMA((3,)),
        ],
        name="receiver",
    )(got, sums, receiver_terms)
    source_new = pl.pallas_call(
        static(source_kernel, rcv_n),
        out_shape=shape(num_src, freq),
        in_specs=[anywhere] * rcv_n,
        out_specs=vmem,
        scratch_shapes=[
            pltpu.VMEM((rcv_n, slots, piece), F32),
            pltpu.SemaphoreType.DMA((rcv_n,)),
        ],
        name="source",
    )(*parts)
    every = every.reshape(peers, off_rows, slots // off_rows, piece)[:, :, :rcv_n]
    offset_new = every.reshape(peers * off_rows, freq)[:num_off]
    return (source_new, receiver_new, offset_new)


def solution(mesh):
    return jax.shard_map(
        local,
        mesh=mesh,
        in_specs=(
            P(AXES, None),
            P(AXES),
            P(AXES),
            P(AXES),
            P(AXES, None, None),
            P("src", None),
            P(AXES, None),
            P(),
        ),
        out_specs=(P("src", None), P(AXES, None), P()),
        check_vma=False,
    )
```

```python
import math

import jax
import jax.numpy as jnp
import numpy as np
from jax import lax
from jax.experimental import pallas as pl
from jax.experimental.pallas import tpu as pltpu
from jax.sharding import PartitionSpec as P

AXES = ("src", "rcv")
LANES = 128
F32 = jnp.float32
BF16 = jnp.bfloat16
NT = (((1,), (1,)), ((), ()))
TN = (((0,), (0,)), ((), ()))
NN = (((1,), (0,)), ((), ()))


def twiddles(samples, first, last):
    half = samples // 2
    quarter = samples // 4
    lane = np.arange(LANES)
    even = np.where(lane % 2 == 0, lane, half - 1 + lane)
    odd = np.where(lane % 2 == 1, lane, half - 1 + lane + np.where(lane == 0, LANES, 0))
    freq = np.arange(quarter)
    groups = half // LANES
    unit = 2.0 * math.pi / samples
    base = []
    taper = []
    for rows, fold in ((even, -np.cos(even * quarter * unit)), (odd, np.sin(odd * quarter * unit))):
        phase = (rows[:, None] * freq[None, :] % samples) * unit
        sine = np.sin(phase)
        sine[:, 0] = np.round(fold)
        base += [np.cos(phase), sine]
        at = rows[:, None] + LANES * np.arange(groups)[None, :]
        taper.append((0.5 - 0.5 * np.cos((at + 0.5) * unit)) / math.sqrt(samples))
    turn = (LANES * np.arange(groups)[:, None] * freq[None, :] % samples) * unit
    turn = np.stack([np.cos(turn), np.sin(turn)])
    return (
        np.stack(base)[:, :, first:last].astype(np.float32),
        turn[:, :, first:last].astype(np.float32),
        np.stack(taper).astype(np.float32),
    )


def dot(a, b, dims=NN):
    return lax.dot_general(a, b, dims, preferred_element_type=F32)


def exact(a, b, dims=NN):
    return lax.dot_general(
        a, b, dims, precision=lax.Precision.HIGHEST, preferred_element_type=F32
    )


def pieces(value):
    one = value.astype(BF16)
    rest = value - one.astype(F32)
    two = rest.astype(BF16)
    return one, two, (rest - two.astype(F32)).astype(BF16)


def count_dot(counts, terms):
    counts = jnp.concatenate(halves(counts), axis=1)
    one, two, three = (jnp.concatenate([v, v], axis=0) for v in pieces(terms))
    return dot(counts, one) + dot(counts, two) + dot(counts, three)


def halves(counts):
    upper = counts.astype(BF16)
    return upper, (counts - upper.astype(F32)).astype(BF16)


def count_dot_tn(counts, terms):
    counts = jnp.concatenate(halves(counts), axis=0)
    one, two, three = (jnp.concatenate([v, v], axis=0) for v in pieces(terms))
    return dot(counts, one, TN) + dot(counts, two, TN) + dot(counts, three, TN)


def chosen_sum(chosen, value):
    one, two, three = pieces(value)
    return dot(chosen, one, TN) + dot(chosen, two, TN) + dot(chosen, three, TN)


def iota(shape, axis):
    return lax.broadcasted_iota(jnp.int32, shape, axis)


def hot(mask):
    return jnp.where(mask, 1.0, 0.0).astype(F32)


def ascend(value, lead):
    width = value.shape[1]
    row = iota((width, width), 0)
    col = iota((width, width), 1)
    if lead:
        pick = row == jnp.where(col == 0, 0, width - col)
    else:
        pick = row == width - 1 - col
    pick = hot(pick).astype(BF16)
    one, two, three = pieces(value)
    return dot(one, pick) + dot(two, pick) + dot(three, pick)


def join(low0, high0, low1, high1):
    edge = high1.shape[1]
    whole = jnp.concatenate([high1, high0], axis=1)
    col = iota(whole.shape, 1)
    shifted = pltpu.roll(whole, 1, 1)
    high = jnp.where(col <= edge, shifted, whole)
    high = jnp.where(col == 0, high0[:, :1], high)
    return jnp.concatenate([low0, low1, high], axis=1)


def part_of(value, first, width):
    half = value.shape[1] // 2
    high = value[:, half:]
    if first == 0:
        tail = high[:, half - width :]
        tail = jnp.where(iota(tail.shape, 1) == 0, high[:, :1], tail)
    else:
        tail = pltpu.roll(high, half - 1, 1)[:, :width]
    return jnp.concatenate([value[:, first : first + width], tail], axis=1)


def joint_rows(num_off, num_src):
    return -(-(num_off + num_src) // 16) * 16


def start(copies):
    for copy in copies:
        copy.start()


def wait(copies):
    for copy in copies:
        copy.wait()


def build_table(base, turn, taper, table):
    groups = taper.shape[2]
    width = base.shape[2]
    for side in range(2):
        for g in range(groups):
            cos0 = base[2 * side]
            sin0 = base[2 * side + 1]
            cos1 = turn[0, g : g + 1, :]
            sin1 = turn[1, g : g + 1, :]
            scale = taper[side, :, g : g + 1]
            at = slice(g * LANES, (g + 1) * LANES)
            table[side, at, :width] = ((cos0 * cos1 - sin0 * sin1) * scale).astype(BF16)
            table[side, at, width:] = ((sin0 * cos1 + cos0 * sin1) * -scale).astype(BF16)


def ident_rows(num_slot, num_off, rows, slot, off, src):
    top = iota((num_slot, slot.shape[1]), 0) == slot
    low = iota((rows - num_slot, slot.shape[1]), 0)
    low = (low == off) | (low == src + num_off)
    return jnp.concatenate([hot(top).astype(BF16), hot(low).astype(BF16)], axis=0)


def spectra_kernel(
    num_off, num_src, rcv_n, head, lead, tile,
    x_hbm, slot_hbm, off_hbm, src_hbm, lists_hbm, offset_hbm, source_hbm, own_hbm,
    counts_hbm, joint0_hbm, base_hbm, turn_hbm, taper_hbm, pay_hbm, joint_hbm, extra_hbm,
    joint0, swapped, x, ids, lists, terms, own, counts, extra, base, turn, taper, table, every, total, stage, spectrum, sems, x_sems,
):
    slots, peers = lists.shape
    num_slot = peers * slots
    rows = total.shape[0]
    width = base.shape[2]
    half = x.shape[1] // 2
    first = 0 if lead else width
    group = lax.axis_index("src")
    near = [
        pltpu.make_async_copy(base_hbm, base, sems.at[0]),
        pltpu.make_async_copy(turn_hbm, turn, sems.at[1]),
        pltpu.make_async_copy(taper_hbm, taper, sems.at[2]),
    ]
    far = [
        pltpu.make_async_copy(slot_hbm, ids.at[0], sems.at[3]),
        pltpu.make_async_copy(off_hbm, ids.at[1], sems.at[4]),
        pltpu.make_async_copy(src_hbm, ids.at[2], sems.at[5]),
        pltpu.make_async_copy(offset_hbm, terms.at[0:num_off], sems.at[6]),
        pltpu.make_async_copy(source_hbm, terms.at[num_off : num_off + num_src], sems.at[7]),
    ]
    if head:
        far.append(pltpu.make_async_copy(lists_hbm, lists, sems.at[8]))
    else:
        far.append(pltpu.make_async_copy(own_hbm, own, sems.at[8]))
        far.append(pltpu.make_async_copy(counts_hbm, counts, sems.at[9]))
        far.append(pltpu.make_async_copy(joint0_hbm, joint0, sems.at[10]))
    tiles = [
        pltpu.make_async_copy(
            x_hbm.at[t * tile : (t + 1) * tile], x.at[t * tile : (t + 1) * tile], x_sems.at[t]
        )
        for t in range(x.shape[0] // tile)
    ]
    start(far + near)
    spare = num_off + num_src
    terms[spare:, :] = jnp.zeros((terms.shape[0] - spare, terms.shape[1]), F32)
    total[...] = jnp.zeros_like(total)
    wait(far + near)
    start(tiles)
    src = ids[2] - group * num_src
    every[...] = ident_rows(num_slot, num_off, rows, ids[0], ids[1], src)
    last = []
    if head:
        at = iota((LANES, x.shape[0]), 0)
        joint = hot((at == ids[1]) | (at == src + num_off)).astype(BF16)
        counts[...] = dot(every[...], joint, NT)
        part = counts[:num_slot]
        whole = jnp.sum(part, axis=0, keepdims=True)
        row = iota((num_slot, LANES), 0)
        col = iota((num_slot, LANES), 1)
        peer = row // slots
        inner = row % slots
        off_rows = max(1, num_off // peers)
        src_rows = num_src // rcv_n
        is_off = (col == peer * off_rows + inner) & (inner < off_rows) & (col < num_off)
        is_src = (col == num_off + peer % rcv_n * src_rows + inner) & (inner < src_rows)
        is_src = is_src & (peer // rcv_n == group)
        num_o = jnp.sum(jnp.where(is_off, whole, 0.0), axis=1, keepdims=True)
        num_s = jnp.sum(jnp.where(is_src, whole, 0.0), axis=1, keepdims=True)
        spread = hot(iota((num_slot, peers), 0) // slots == iota((num_slot, peers), 1))
        listed = dot(spread.astype(BF16), lists[...].astype(F32).astype(BF16), NT)
        mine = iota((num_slot, slots), 0) % slots == iota((num_slot, slots), 1)
        asked = jnp.sum(jnp.where(mine, listed, 0.0), axis=1, keepdims=True)
        part = jnp.where(col == spare, asked, part)
        part = jnp.where(col == spare + 1, num_o, part)
        extra[:, :LANES] = jnp.where(col == spare + 2, num_s, part)
        for p in range(peers):
            mate = p ^ 1
            extra[p * slots : (p + 1) * slots, LANES:] = extra[
                mate * slots : (mate + 1) * slots, :LANES
            ]
        last.append(pltpu.make_async_copy(extra, pay_hbm.at[:, 2 * width :], sems.at[6]))
        last.append(pltpu.make_async_copy(counts, extra_hbm, sems.at[7]))
    else:
        kept = own[...]
        own[:, : 2 * width] = part_of(kept, width, width)
        own[:, 2 * width :] = part_of(kept, 0, width)
    start(last)
    stage[...] = count_dot(counts[...], part_of(terms[...], first, width))
    build_table(base, turn, taper, table)

    def transform(t):
        tiles[t].wait()
        lane = iota((tile, LANES), 1) % 2 == 0
        even = []
        odd = []
        for g in range(half // LANES):
            front = x[t * tile : (t + 1) * tile, g * LANES : (g + 1) * LANES]
            back = x[t * tile : (t + 1) * tile, half + g * LANES : half + (g + 1) * LANES]
            back = pltpu.roll(back, 1, 1)
            even.append(jnp.where(lane, front, back))
            odd.append(jnp.where(lane, back, front))
        spectrum[t % 2, :, : 2 * width] = dot(jnp.concatenate(even, axis=1), table[0])
        spectrum[t % 2, :, 2 * width :] = dot(jnp.concatenate(odd, axis=1), table[1])

    def collect(t):
        ec, es, oc, os = (
            spectrum[t % 2, :, k * width : (k + 1) * width] for k in range(4)
        )
        re_low, im_low = ec + oc, es + os
        re_high, im_high = ec - oc, es - os
        if lead:
            zero = iota((tile, width), 1) == 0
            im_low = jnp.where(zero, 0.0, im_low)
            re_high = jnp.where(zero, es, re_high)
            im_high = jnp.where(zero, os, im_high)
        power = jnp.concatenate(
            [re_low * re_low + im_low * im_low, re_high * re_high + im_high * im_high], axis=1
        )
        amp = 0.5 * jnp.log(power + 0.01)
        upper = amp.astype(BF16)
        lower = (amp - upper.astype(F32)).astype(BF16)
        ids_t = every[:, t * tile : (t + 1) * tile]
        total[...] += dot(ids_t, upper) + dot(ids_t, lower)

    transform(0)
    for t in range(1, len(tiles)):
        transform(t)
        collect(t - 1)
    collect(len(tiles) - 1)
    stage[:, :width] = total[:, :width] - stage[:, :width]
    stage[:, width:] = ascend(total[:, width:], lead) - stage[:, width:]
    out = [pltpu.make_async_copy(stage.at[:num_slot], pay_hbm.at[:, : 2 * width], sems.at[0])]
    if head:
        out.append(pltpu.make_async_copy(stage.at[num_slot:], joint_hbm, sems.at[1]))
    else:
        odd = lax.axis_index("rcv") % 2 == 1
        cut = rows - num_slot
        for m in range(2 * width // LANES):
            lo, hi = 2 * m * LANES, (2 * m + 1) * LANES
            if hi < 2 * width:
                sums = joint0[:, lo:hi], joint0[:, hi : hi + LANES]
            else:
                lo, hi = lo - 2 * width, hi - 2 * width
                sums = stage[num_slot:, lo:hi], stage[num_slot:, hi : hi + LANES]
            both = own[:, 2 * m * LANES : (2 * m + 1) * LANES], own[:, (2 * m + 1) * LANES : (2 * m + 2) * LANES]
            at = slice(m * LANES, (m + 1) * LANES)
            swapped[0, :cut, at] = jnp.where(odd, sums[1], sums[0])
            swapped[1, :cut, at] = jnp.where(odd, sums[0], sums[1])
            swapped[0, cut:, at] = jnp.where(odd, both[1], both[0])
            swapped[1, cut:, at] = jnp.where(odd, both[0], both[1])
        out.append(pltpu.make_async_copy(swapped.at[0], joint_hbm, sems.at[1]))
        out.append(pltpu.make_async_copy(swapped.at[1], extra_hbm, sems.at[2]))
    start(out)
    wait(last + out)


def owner_hot(sent, base, owned):
    col = iota(sent.shape, 1)
    asked = jnp.sum(jnp.where(col == base, sent, 0.0), axis=1, keepdims=True).astype(jnp.int32)
    return hot(iota((sent.shape[0], owned), 1) == asked)


def pack_kernel(
    num_off, num_src, slots, src_n, rcv_n, sent_hbm, pair_hbm, _, out_hbm,
    sent, pair, out, sems,
):
    half = pair.shape[1]
    cut = joint_rows(num_off, num_src)
    owned = (pair.shape[0] - cut) // 2
    copies = [
        pltpu.make_async_copy(sent_hbm, sent, sems.at[0]),
        pltpu.make_async_copy(pair_hbm, pair, sems.at[1]),
    ]
    start(copies)
    copies[0].wait()
    num = sent.shape[0]
    group = lax.axis_index("src")
    every_src = src_n * num_src
    col = iota((LANES, every_src), 0)
    pick = hot(col == num_off + iota((LANES, every_src), 1) % num_src).astype(BF16)
    from_group = iota((num, every_src), 0) // (slots * rcv_n)
    from_group = from_group == iota((num, every_src), 1) // num_src
    off_of = []
    src_of = []
    for k in range(2):
        part = sent[:, k * LANES : (k + 1) * LANES]
        chosen = owner_hot(part, num_off + num_src, owned).astype(BF16)
        upper, lower = halves(part)
        by_src = [jnp.where(from_group, dot(v, pick), 0.0).astype(BF16) for v in (upper, lower)]
        off_of.append((dot(chosen, upper, TN) + dot(chosen, lower, TN))[:, :num_off])
        src_of.append(dot(chosen, by_src[0], TN) + dot(chosen, by_src[1], TN))
    wait(copies[1:])
    terms = pair[cut:, :]
    sums = pair[:cut, :]
    off_sum = sums[:num_off] - count_dot_tn(jnp.concatenate(off_of, axis=0), terms)
    src_sum = -count_dot_tn(jnp.concatenate(src_of, axis=0), terms)
    mine = sums[num_off : num_off + num_src]
    per_off = slots // max(1, num_off // (src_n * rcv_n))
    per_src = slots // (num_src // rcv_n)
    if num_off * per_off < num or per_off > rcv_n:
        out[...] = jnp.zeros_like(out)
    copies = [
        pltpu.make_async_copy(
            out.at[h], out_hbm.at[:, half + h * LANES : half + (h + 1) * LANES], sems.at[h]
        )
        for h in range(2)
    ]
    for m in range(rcv_n):
        at = slice(m * LANES, (m + 1) * LANES)
        out[0, pl.ds(m, num_off, stride=per_off), :] = off_sum[:, at]
    copies[0].start()
    for m in range(rcv_n):
        at = slice(m * LANES, (m + 1) * LANES)
        for i in range(src_n):
            to = pl.ds(i * num_src * per_src + m, num_src, stride=per_src)
            source = src_sum[i * num_src : (i + 1) * num_src, at]
            out[1, to, :] = source + jnp.where(group == i, mine[:, at], 0.0)
    copies[1].start()
    wait(copies)


def shares_kernel(
    num_off, num_src, slots, edge, got_hbm, sums_hbm, offset_hbm, source_hbm,
    off_out, src_out, sent, tail, offset, source, rows, block, sems,
):
    rcv_n = lax.axis_size("rcv")
    piece = src_out.shape[1]
    rest = sums_hbm.shape[1] - piece
    copies = [
        pltpu.make_async_copy(got_hbm.at[:, :LANES], sent, sems.at[0]),
        pltpu.make_async_copy(sums_hbm.at[:, rest:], tail, sems.at[1]),
        pltpu.make_async_copy(offset_hbm, offset, sems.at[2]),
        pltpu.make_async_copy(source_hbm, source, sems.at[3]),
    ]
    start(copies)
    wait(copies)
    peers = sent.shape[0] // slots
    base = num_off + num_src
    both = sent[0:slots]
    for d in range(1, peers):
        both = both + sent[d * slots : (d + 1) * slots]
    for k in range(2):
        value = tail[k * slots : (k + 1) * slots]
        for d in range(k + 2, peers, 2):
            value = value + tail[d * slots : (d + 1) * slots]
        rows[:, k * LANES : (k + 1) * LANES] = value[:, :LANES]
        rows[:, piece + k * LANES : piece + (k + 1) * LANES] = value[:, LANES:]
    col = iota(both.shape, 1)
    num_o = jnp.sum(jnp.where(col == base + 1, both, 0.0), axis=1, keepdims=True)
    num_s = jnp.sum(jnp.where(col == base + 2, both, 0.0), axis=1, keepdims=True)
    here = lax.axis_index("rcv")
    off_rows = max(1, num_off // peers)
    src_rows = num_src // rcv_n
    at_off = (lax.axis_index("src") * rcv_n + here) * off_rows
    for count, num, at, first, terms in (
        (off_rows, num_o, slice(0, piece), at_off, offset),
        (src_rows, num_s, slice(piece, 2 * piece), here * src_rows, source),
    ):
        last = terms.shape[0] - 1
        parts = [
            jnp.concatenate(
                [rows[j * (slots // count) + m : j * (slots // count) + m + 1, at] for j in range(count)],
                axis=0,
            )
            for m in range(rcv_n)
        ]
        whole = jnp.concatenate(parts, axis=1)
        e, r = edge // 2, (whole.shape[1] - edge) // 2
        whole = join(
            whole[:, edge : edge + r], whole[:, edge + r :], whole[:, :e], whole[:, e:edge]
        )
        old = jnp.concatenate(
            [terms[pl.ds(jnp.minimum(first + j, last), 1), :] for j in range(count)], axis=0
        )
        new = old + whole / (num[:count] + 1.0)
        block[:, at] = jnp.zeros((slots, piece), F32)
        for j in range(count):
            for m in range(rcv_n):
                to = j * (slots // count) + m
                block[to : to + 1, at] = new[j : j + 1, m * piece : (m + 1) * piece]
    src_out[...] = block[:, piece:]
    done = block[:, :piece]
    for d in range(peers):
        off_out[d * slots : (d + 1) * slots, :] = done


def receiver_kernel(num_off, num_src, got_hbm, sums_hbm, terms_hbm, out, got, sums, terms, sems):
    edge = got.shape[1] - LANES
    rest = sums.shape[1]
    copies = [
        pltpu.make_async_copy(got_hbm.at[:, : edge + LANES], got, sems.at[0]),
        pltpu.make_async_copy(sums_hbm.at[:, :rest], sums, sems.at[1]),
        pltpu.make_async_copy(terms_hbm, terms, sems.at[2]),
    ]
    start(copies)
    wait(copies)
    sent = got[:, edge:]
    value = terms[...]
    chosen = owner_hot(sent, num_off + num_src, value.shape[0]).astype(BF16)
    per_slot = jnp.where(iota(sent.shape, 1) < num_off, sent, 0.0)
    num = jnp.sum(chosen_sum(chosen, per_slot), axis=1, keepdims=True)
    one = chosen_sum(chosen, got[:, :edge])
    two = chosen_sum(chosen, sums[...])
    edge //= 2
    rest //= 2
    total = join(two[:, :rest], two[:, rest:], one[:, :edge], one[:, edge:])
    out[...] = value + (total - num * value) / (num + 1.0)


def source_kernel(rcv_n, *refs):
    src_out, rest, sems = refs[rcv_n:]
    copies = [pltpu.make_async_copy(refs[k], rest.at[k], sems.at[k]) for k in range(rcv_n)]
    start(copies)
    wait(copies)
    slots, piece = rest.shape[1:]
    count = src_out.shape[0] // rcv_n
    here = lax.axis_index("rcv")
    for j in range(rcv_n):
        value = jnp.zeros((slots, piece), F32)
        for k in range(rcv_n):
            value = value + jnp.where((here + rcv_n - k) % rcv_n == j, rest[k], 0.0)
        for i in range(count):
            for m in range(rcv_n):
                row = i * (slots // count) + m
                src_out[j * count + i : j * count + i + 1, m * piece : (m + 1) * piece] = (
                    value[row : row + 1]
                )


def swap(value, slots):
    shape = value.shape
    value = value.reshape(shape[0] // slots, slots, shape[1])
    value = lax.all_to_all(value, AXES, split_axis=0, concat_axis=0, tiled=True)
    return value.reshape(shape)


def local(
    traces,
    trace_source,
    trace_offset,
    trace_slot,
    request_list,
    source_terms,
    receiver_terms,
    offset_terms,
):
    src_n = lax.axis_size("src")
    rcv_n = lax.axis_size("rcv")
    peers = src_n * rcv_n
    slots = request_list.shape[2]
    num_tr, samples = traces.shape
    owned, freq = receiver_terms.shape
    num_src = source_terms.shape[0]
    num_off = offset_terms.shape[0]
    num_slot = peers * slots
    joint = joint_rows(num_off, num_src)
    rows = num_slot + joint
    half = freq // 2
    edge = half // 2
    rest = half - edge
    piece = freq // rcv_n
    off_rows = max(1, num_off // peers)
    tile = min(512, num_tr)
    assert slots == num_src and off_rows * rcv_n <= slots and num_off + num_src + 3 <= LANES
    assert samples == 2 * freq and freq % (4 * LANES) == 0 and owned <= 256
    assert rcv_n % 2 == 0 and piece == 2 * LANES and edge == rest
    ids = [v.reshape(1, num_tr) for v in (trace_slot, trace_offset, trace_source)]
    lists = jnp.swapaxes(request_list, 1, 2).reshape(slots, peers)
    vmem = pl.BlockSpec(memory_space=pltpu.VMEM)
    hbm = pl.BlockSpec(memory_space=pltpu.HBM)
    anywhere = pl.BlockSpec(memory_space=pl.ANY)

    def static(kernel, *args):
        return lambda *refs: kernel(*args, *refs)

    def shape(*dims):
        return jax.ShapeDtypeStruct(dims, F32)

    def spectra(head, width, counts, joint0):
        lead = not head
        first = 0 if lead else half - width
        consts = [jnp.asarray(v) for v in twiddles(samples, first, first + width)]
        return pl.pallas_call(
            static(spectra_kernel, num_off, num_src, rcv_n, head, lead, tile),
            out_shape=(
                shape(num_slot, 2 * width + (2 * LANES if head else piece)),
                shape(joint, 2 * width) if head else shape(joint + owned, half),
                shape(rows, LANES) if head else shape(joint + owned, half),
            ),
            in_specs=[hbm] * 13,
            out_specs=(hbm, hbm, hbm),
            scratch_shapes=[
                pltpu.VMEM((joint, half), F32),
                pltpu.VMEM((2, joint + owned, half), F32),
                pltpu.VMEM((num_tr, samples), BF16),
                pltpu.VMEM((3, 1, num_tr), jnp.int32),
                pltpu.VMEM((slots, peers), jnp.int32),
                pltpu.VMEM((LANES, freq), F32),
                pltpu.VMEM((owned, freq), F32),
                pltpu.VMEM((rows, LANES), F32),
                pltpu.VMEM((num_slot, 2 * LANES), F32),
                pltpu.VMEM(consts[0].shape, F32),
                pltpu.VMEM(consts[1].shape, F32),
                pltpu.VMEM(consts[2].shape, F32),
                pltpu.VMEM((2, freq, 2 * width), BF16),
                pltpu.VMEM((rows, num_tr), BF16),
                pltpu.VMEM((rows, 2 * width), F32),
                pltpu.VMEM((rows, 2 * width), F32),
                pltpu.VMEM((2, tile, 4 * width), F32),
                pltpu.SemaphoreType.DMA((11,)),
                pltpu.SemaphoreType.DMA((num_tr // tile,)),
            ],
            compiler_params=pltpu.CompilerParams(vmem_limit_bytes=56 * 2**20),
            name="spectra%d" % head,
        )(traces, *ids, lists, offset_terms, source_terms, receiver_terms, counts, joint0, *consts)

    pay, joint0, counts = spectra(True, edge, offset_terms, source_terms)
    got = swap(pay, slots)
    sent = got[:, 2 * edge :]
    pay, keep, mate = spectra(False, rest, counts, joint0)
    mate = lax.ppermute(mate, "rcv", [(j, j ^ 1) for j in range(rcv_n)])
    pair = jnp.concatenate([keep[:joint] + mate[:joint], keep[joint:], mate[joint:]], axis=0)
    pay = pl.pallas_call(
        static(pack_kernel, num_off, num_src, slots, src_n, rcv_n),
        out_shape=shape(*pay.shape),
        in_specs=[anywhere, hbm, hbm],
        out_specs=hbm,
        scratch_shapes=[
            pltpu.VMEM((num_slot, 2 * LANES), F32),
            pltpu.VMEM((joint + 2 * owned, half), F32),
            pltpu.VMEM((2, num_slot, LANES), F32),
            pltpu.SemaphoreType.DMA((2,)),
        ],
        input_output_aliases={2: 0},
        name="pack",
    )(sent, pair, pay)
    sums = swap(pay, slots)

    off_new, src_new = pl.pallas_call(
        static(shares_kernel, num_off, num_src, slots, 2 * edge),
        out_shape=(shape(num_slot, piece), shape(slots, piece)),
        in_specs=[anywhere, anywhere, hbm, hbm],
        out_specs=(vmem, vmem),
        scratch_shapes=[
            pltpu.VMEM((num_slot, LANES), F32),
            pltpu.VMEM((num_slot, piece), F32),
            pltpu.VMEM((num_off, freq), F32),
            pltpu.VMEM((num_src, freq), F32),
            pltpu.VMEM((slots, 2 * piece), F32),
            pltpu.VMEM((slots, 2 * piece), F32),
            pltpu.SemaphoreType.DMA((4,)),
        ],
        name="shares",
    )(sent, sums, offset_terms, source_terms)
    every = swap(off_new, slots)
    parts = [src_new]
    for k in range(1, rcv_n):
        ring = [(j, (j + k) % rcv_n) for j in range(rcv_n)]
        parts.append(lax.ppermute(src_new, "rcv", ring))
    receiver_new = pl.pallas_call(
        static(receiver_kernel, num_off, num_src),
        out_shape=shape(owned, freq),
        in_specs=[anywhere, anywhere, hbm],
        out_specs=vmem,
        scratch_shapes=[
            pltpu.VMEM((num_slot, 2 * edge + LANES), F32),
            pltpu.VMEM((num_slot, 2 * rest), F32),
            pltpu.VMEM((owned, freq), F32),
            pltpu.SemaphoreType.DMA((3,)),
        ],
        name="receiver",
    )(got, sums, receiver_terms)
    source_new = pl.pallas_call(
        static(source_kernel, rcv_n),
        out_shape=shape(num_src, freq),
        in_specs=[anywhere] * rcv_n,
        out_specs=vmem,
        scratch_shapes=[
            pltpu.VMEM((rcv_n, slots, piece), F32),
            pltpu.SemaphoreType.DMA((rcv_n,)),
        ],
        name="source",
    )(*parts)
    every = every.reshape(peers, off_rows, slots // off_rows, piece)[:, :, :rcv_n]
    offset_new = every.reshape(peers * off_rows, freq)[:num_off]
    return (source_new, receiver_new, offset_new)


def solution(mesh):
    return jax.shard_map(
        local,
        mesh=mesh,
        in_specs=(
            P(AXES, None),
            P(AXES),
            P(AXES),
            P(AXES),
            P(AXES, None, None),
            P("src", None),
            P(AXES, None),
            P(),
        ),
        out_specs=(P("src", None), P(AXES, None), P()),
        check_vma=False,
    )
```

```python
import math

import jax
import jax.numpy as jnp
import numpy as np
from jax import lax
from jax.experimental import pallas as pl
from jax.experimental.pallas import tpu as pltpu
from jax.sharding import PartitionSpec as P

AXES = ("src", "rcv")
LANES = 128
F32 = jnp.float32
BF16 = jnp.bfloat16
NT = (((1,), (1,)), ((), ()))
TN = (((0,), (0,)), ((), ()))
NN = (((1,), (0,)), ((), ()))


def twiddles(samples, first, last):
    half = samples // 2
    quarter = samples // 4
    lane = np.arange(LANES)
    even = np.where(lane % 2 == 0, lane, half - 1 + lane)
    odd = np.where(lane % 2 == 1, lane, half - 1 + lane + np.where(lane == 0, LANES, 0))
    freq = np.arange(quarter)
    groups = half // LANES
    unit = 2.0 * math.pi / samples
    base = []
    taper = []
    for rows, fold in ((even, -np.cos(even * quarter * unit)), (odd, np.sin(odd * quarter * unit))):
        phase = (rows[:, None] * freq[None, :] % samples) * unit
        sine = np.sin(phase)
        sine[:, 0] = np.round(fold)
        base += [np.cos(phase), sine]
        at = rows[:, None] + LANES * np.arange(groups)[None, :]
        taper.append((0.5 - 0.5 * np.cos((at + 0.5) * unit)) / math.sqrt(samples))
    turn = (LANES * np.arange(groups)[:, None] * freq[None, :] % samples) * unit
    turn = np.stack([np.cos(turn), np.sin(turn)])
    return (
        np.stack(base)[:, :, first:last].astype(np.float32),
        turn[:, :, first:last].astype(np.float32),
        np.stack(taper).astype(np.float32),
    )


def dot(a, b, dims=NN):
    return lax.dot_general(a, b, dims, preferred_element_type=F32)


def exact(a, b, dims=NN):
    return lax.dot_general(
        a, b, dims, precision=lax.Precision.HIGHEST, preferred_element_type=F32
    )


def pieces(value):
    one = value.astype(BF16)
    rest = value - one.astype(F32)
    two = rest.astype(BF16)
    return one, two, (rest - two.astype(F32)).astype(BF16)


def count_dot(counts, terms):
    counts = jnp.concatenate(halves(counts), axis=1)
    one, two, three = (jnp.concatenate([v, v], axis=0) for v in pieces(terms))
    return dot(counts, one) + dot(counts, two) + dot(counts, three)


def halves(counts):
    upper = counts.astype(BF16)
    return upper, (counts - upper.astype(F32)).astype(BF16)


def count_dot_tn(counts, terms):
    counts = jnp.concatenate(halves(counts), axis=0)
    one, two, three = (jnp.concatenate([v, v], axis=0) for v in pieces(terms))
    return dot(counts, one, TN) + dot(counts, two, TN) + dot(counts, three, TN)


def chosen_sum(chosen, value):
    one, two, three = pieces(value)
    return dot(chosen, one, TN) + dot(chosen, two, TN) + dot(chosen, three, TN)


def iota(shape, axis):
    return lax.broadcasted_iota(jnp.int32, shape, axis)


def hot(mask):
    return jnp.where(mask, 1.0, 0.0).astype(F32)


def ascend(value, lead):
    width = value.shape[1]
    row = iota((width, width), 0)
    col = iota((width, width), 1)
    if lead:
        pick = row == jnp.where(col == 0, 0, width - col)
    else:
        pick = row == width - 1 - col
    pick = hot(pick).astype(BF16)
    one, two, three = pieces(value)
    return dot(one, pick) + dot(two, pick) + dot(three, pick)


def join(low0, high0, low1, high1):
    edge = high1.shape[1]
    whole = jnp.concatenate([high1, high0], axis=1)
    col = iota(whole.shape, 1)
    shifted = pltpu.roll(whole, 1, 1)
    high = jnp.where(col <= edge, shifted, whole)
    high = jnp.where(col == 0, high0[:, :1], high)
    return jnp.concatenate([low0, low1, high], axis=1)


def part_of(value, first, width):
    half = value.shape[1] // 2
    high = value[:, half:]
    if first == 0:
        tail = high[:, half - width :]
        tail = jnp.where(iota(tail.shape, 1) == 0, high[:, :1], tail)
    else:
        tail = pltpu.roll(high, half - 1, 1)[:, :width]
    return jnp.concatenate([value[:, first : first + width], tail], axis=1)


def joint_rows(num_off, num_src):
    return -(-(num_off + num_src) // 16) * 16


def start(copies):
    for copy in copies:
        copy.start()


def wait(copies):
    for copy in copies:
        copy.wait()


def build_table(base, turn, taper, table):
    groups = taper.shape[2]
    width = base.shape[2]
    for side in range(2):
        for g in range(groups):
            cos0 = base[2 * side]
            sin0 = base[2 * side + 1]
            cos1 = turn[0, g : g + 1, :]
            sin1 = turn[1, g : g + 1, :]
            scale = taper[side, :, g : g + 1]
            at = slice(g * LANES, (g + 1) * LANES)
            table[side, at, :width] = ((cos0 * cos1 - sin0 * sin1) * scale).astype(BF16)
            table[side, at, width:] = ((sin0 * cos1 + cos0 * sin1) * -scale).astype(BF16)


def ident_rows(num_slot, num_off, rows, slot, off, src):
    top = iota((num_slot, slot.shape[1]), 0) == slot
    low = iota((rows - num_slot, slot.shape[1]), 0)
    low = (low == off) | (low == src + num_off)
    return jnp.concatenate([hot(top).astype(BF16), hot(low).astype(BF16)], axis=0)


def spectra_kernel(
    num_off, num_src, rcv_n, head, lead, tile,
    x_hbm, slot_hbm, off_hbm, src_hbm, lists_hbm, offset_hbm, source_hbm, own_hbm,
    counts_hbm, joint0_hbm, base_hbm, turn_hbm, taper_hbm, pay_hbm, joint_hbm, extra_hbm,
    joint0, swapped, x, ids, lists, terms, own, counts, extra, base, turn, taper, table, every, total, stage, spectrum, sems, x_sems,
):
    slots, peers = lists.shape
    num_slot = peers * slots
    rows = total.shape[0]
    width = base.shape[2]
    half = x.shape[1] // 2
    first = 0 if lead else width
    group = lax.axis_index("src")
    near = [
        pltpu.make_async_copy(base_hbm, base, sems.at[0]),
        pltpu.make_async_copy(turn_hbm, turn, sems.at[1]),
        pltpu.make_async_copy(taper_hbm, taper, sems.at[2]),
    ]
    far = [
        pltpu.make_async_copy(slot_hbm, ids.at[0], sems.at[3]),
        pltpu.make_async_copy(off_hbm, ids.at[1], sems.at[4]),
        pltpu.make_async_copy(src_hbm, ids.at[2], sems.at[5]),
    ]
    late = [
        pltpu.make_async_copy(offset_hbm, terms.at[0:num_off], sems.at[6]),
        pltpu.make_async_copy(source_hbm, terms.at[num_off : num_off + num_src], sems.at[7]),
    ]
    if head:
        far.append(pltpu.make_async_copy(lists_hbm, lists, sems.at[8]))
    else:
        late.append(pltpu.make_async_copy(own_hbm, own, sems.at[8]))
        late.append(pltpu.make_async_copy(counts_hbm, counts, sems.at[9]))
        late.append(pltpu.make_async_copy(joint0_hbm, joint0, sems.at[10]))
    tiles = [
        pltpu.make_async_copy(
            x_hbm.at[t * tile : (t + 1) * tile], x.at[t * tile : (t + 1) * tile], x_sems.at[t]
        )
        for t in range(x.shape[0] // tile)
    ]
    start(far + near)
    spare = num_off + num_src
    terms[spare:, :] = jnp.zeros((terms.shape[0] - spare, terms.shape[1]), F32)
    total[...] = jnp.zeros_like(total)
    wait(far + near)
    start(tiles[:1] + late + tiles[1:])
    src = ids[2] - group * num_src
    every[...] = ident_rows(num_slot, num_off, rows, ids[0], ids[1], src)
    last = []
    if head:
        counts[...] = jnp.zeros_like(counts)
        counts[:, : rows - num_slot] = dot(every[...], every[num_slot:, :], NT)
        part = counts[:num_slot]
        whole = jnp.sum(part, axis=0, keepdims=True)
        row = iota((num_slot, LANES), 0)
        col = iota((num_slot, LANES), 1)
        peer = row // slots
        inner = row % slots
        off_rows = max(1, num_off // peers)
        src_rows = num_src // rcv_n
        is_off = (col == peer * off_rows + inner) & (inner < off_rows) & (col < num_off)
        is_src = (col == num_off + peer % rcv_n * src_rows + inner) & (inner < src_rows)
        is_src = is_src & (peer // rcv_n == group)
        num_o = jnp.sum(jnp.where(is_off, whole, 0.0), axis=1, keepdims=True)
        num_s = jnp.sum(jnp.where(is_src, whole, 0.0), axis=1, keepdims=True)
        spread = hot(iota((num_slot, peers), 0) // slots == iota((num_slot, peers), 1))
        listed = dot(spread.astype(BF16), lists[...].astype(F32).astype(BF16), NT)
        mine = iota((num_slot, slots), 0) % slots == iota((num_slot, slots), 1)
        asked = jnp.sum(jnp.where(mine, listed, 0.0), axis=1, keepdims=True)
        part = jnp.where(col == spare, asked, part)
        part = jnp.where(col == spare + 1, num_o, part)
        extra[:, :LANES] = jnp.where(col == spare + 2, num_s, part)
        for p in range(peers):
            mate = p ^ 1
            extra[p * slots : (p + 1) * slots, LANES:] = extra[
                mate * slots : (mate + 1) * slots, :LANES
            ]
        last.append(pltpu.make_async_copy(extra, pay_hbm.at[:, 2 * width :], sems.at[9]))
        last.append(pltpu.make_async_copy(counts, extra_hbm, sems.at[10]))
    start(last)
    build_table(base, turn, taper, table)
    wait(late)
    if not head:
        kept = own[...]
        own[:, : 2 * width] = part_of(kept, width, width)
        own[:, 2 * width :] = part_of(kept, 0, width)
    stage[...] = count_dot(counts[...], part_of(terms[...], first, width))

    def transform(t):
        tiles[t].wait()
        lane = iota((tile, LANES), 1) % 2 == 0
        even = []
        odd = []
        for g in range(half // LANES):
            front = x[t * tile : (t + 1) * tile, g * LANES : (g + 1) * LANES]
            back = x[t * tile : (t + 1) * tile, half + g * LANES : half + (g + 1) * LANES]
            back = pltpu.roll(back, 1, 1)
            even.append(jnp.where(lane, front, back))
            odd.append(jnp.where(lane, back, front))
        spectrum[t % 2, :, : 2 * width] = dot(jnp.concatenate(even, axis=1), table[0])
        spectrum[t % 2, :, 2 * width :] = dot(jnp.concatenate(odd, axis=1), table[1])

    def collect(t):
        ec, es, oc, os = (
            spectrum[t % 2, :, k * width : (k + 1) * width] for k in range(4)
        )
        re_low, im_low = ec + oc, es + os
        re_high, im_high = ec - oc, es - os
        if lead:
            zero = iota((tile, width), 1) == 0
            im_low = jnp.where(zero, 0.0, im_low)
            re_high = jnp.where(zero, es, re_high)
            im_high = jnp.where(zero, os, im_high)
        power = jnp.concatenate(
            [re_low * re_low + im_low * im_low, re_high * re_high + im_high * im_high], axis=1
        )
        amp = 0.5 * jnp.log(power + 0.01)
        upper = amp.astype(BF16)
        lower = (amp - upper.astype(F32)).astype(BF16)
        ids_t = every[:, t * tile : (t + 1) * tile]
        total[...] += dot(ids_t, upper) + dot(ids_t, lower)

    transform(0)
    for t in range(1, len(tiles)):
        transform(t)
        collect(t - 1)
    collect(len(tiles) - 1)
    stage[:, :width] = total[:, :width] - stage[:, :width]
    stage[:, width:] = ascend(total[:, width:], lead) - stage[:, width:]
    out = [pltpu.make_async_copy(stage.at[:num_slot], pay_hbm.at[:, : 2 * width], sems.at[0])]
    if head:
        out.append(pltpu.make_async_copy(stage.at[num_slot:], joint_hbm, sems.at[1]))
    else:
        odd = lax.axis_index("rcv") % 2 == 1
        cut = rows - num_slot
        for m in range(2 * width // LANES):
            lo, hi = 2 * m * LANES, (2 * m + 1) * LANES
            if hi < 2 * width:
                sums = joint0[:, lo:hi], joint0[:, hi : hi + LANES]
            else:
                lo, hi = lo - 2 * width, hi - 2 * width
                sums = stage[num_slot:, lo:hi], stage[num_slot:, hi : hi + LANES]
            both = own[:, 2 * m * LANES : (2 * m + 1) * LANES], own[:, (2 * m + 1) * LANES : (2 * m + 2) * LANES]
            at = slice(m * LANES, (m + 1) * LANES)
            swapped[0, :cut, at] = jnp.where(odd, sums[1], sums[0])
            swapped[1, :cut, at] = jnp.where(odd, sums[0], sums[1])
            swapped[0, cut:, at] = jnp.where(odd, both[1], both[0])
            swapped[1, cut:, at] = jnp.where(odd, both[0], both[1])
        out.append(pltpu.make_async_copy(swapped.at[0], joint_hbm, sems.at[1]))
        out.append(pltpu.make_async_copy(swapped.at[1], extra_hbm, sems.at[2]))
    start(out)
    wait(last + out)


def owner_hot(sent, base, owned):
    col = iota(sent.shape, 1)
    asked = jnp.sum(jnp.where(col == base, sent, 0.0), axis=1, keepdims=True).astype(jnp.int32)
    return hot(iota((sent.shape[0], owned), 1) == asked)


def pack_kernel(
    num_off, num_src, slots, src_n, rcv_n, sent_hbm, pair_hbm, _, out_hbm,
    sent, pair, out, sems,
):
    half = pair.shape[1]
    cut = joint_rows(num_off, num_src)
    owned = (pair.shape[0] - cut) // 2
    copies = [
        pltpu.make_async_copy(sent_hbm, sent, sems.at[0]),
        pltpu.make_async_copy(pair_hbm, pair, sems.at[1]),
    ]
    start(copies)
    copies[0].wait()
    num = sent.shape[0]
    group = lax.axis_index("src")
    every_src = src_n * num_src
    col = iota((LANES, every_src), 0)
    pick = hot(col == num_off + iota((LANES, every_src), 1) % num_src).astype(BF16)
    from_group = iota((num, every_src), 0) // (slots * rcv_n)
    from_group = from_group == iota((num, every_src), 1) // num_src
    off_of = []
    src_of = []
    for k in range(2):
        part = sent[:, k * LANES : (k + 1) * LANES]
        chosen = owner_hot(part, num_off + num_src, owned).astype(BF16)
        upper, lower = halves(part)
        by_src = [jnp.where(from_group, dot(v, pick), 0.0).astype(BF16) for v in (upper, lower)]
        off_of.append((dot(chosen, upper, TN) + dot(chosen, lower, TN))[:, :num_off])
        src_of.append(dot(chosen, by_src[0], TN) + dot(chosen, by_src[1], TN))
    wait(copies[1:])
    terms = pair[cut:, :]
    sums = pair[:cut, :]
    off_sum = sums[:num_off] - count_dot_tn(jnp.concatenate(off_of, axis=0), terms)
    src_sum = -count_dot_tn(jnp.concatenate(src_of, axis=0), terms)
    mine = sums[num_off : num_off + num_src]
    per_off = slots // max(1, num_off // (src_n * rcv_n))
    per_src = slots // (num_src // rcv_n)
    if num_off * per_off < num or per_off > rcv_n:
        out[...] = jnp.zeros_like(out)
    copies = [
        pltpu.make_async_copy(
            out.at[h], out_hbm.at[:, half + h * LANES : half + (h + 1) * LANES], sems.at[h]
        )
        for h in range(2)
    ]
    for m in range(rcv_n):
        at = slice(m * LANES, (m + 1) * LANES)
        out[0, pl.ds(m, num_off, stride=per_off), :] = off_sum[:, at]
    copies[0].start()
    for m in range(rcv_n):
        at = slice(m * LANES, (m + 1) * LANES)
        for i in range(src_n):
            to = pl.ds(i * num_src * per_src + m, num_src, stride=per_src)
            source = src_sum[i * num_src : (i + 1) * num_src, at]
            out[1, to, :] = source + jnp.where(group == i, mine[:, at], 0.0)
    copies[1].start()
    wait(copies)


def shares_kernel(
    num_off, num_src, slots, edge, got_hbm, sums_hbm, offset_hbm, source_hbm,
    off_out, src_out, sent, tail, offset, source, rows, block, sems,
):
    rcv_n = lax.axis_size("rcv")
    piece = src_out.shape[1]
    rest = sums_hbm.shape[1] - piece
    copies = [
        pltpu.make_async_copy(got_hbm.at[:, :LANES], sent, sems.at[0]),
        pltpu.make_async_copy(sums_hbm.at[:, rest:], tail, sems.at[1]),
        pltpu.make_async_copy(offset_hbm, offset, sems.at[2]),
        pltpu.make_async_copy(source_hbm, source, sems.at[3]),
    ]
    start(copies)
    wait(copies)
    peers = sent.shape[0] // slots
    base = num_off + num_src
    both = sent[0:slots]
    for d in range(1, peers):
        both = both + sent[d * slots : (d + 1) * slots]
    for k in range(2):
        value = tail[k * slots : (k + 1) * slots]
        for d in range(k + 2, peers, 2):
            value = value + tail[d * slots : (d + 1) * slots]
        rows[:, k * LANES : (k + 1) * LANES] = value[:, :LANES]
        rows[:, piece + k * LANES : piece + (k + 1) * LANES] = value[:, LANES:]
    col = iota(both.shape, 1)
    num_o = jnp.sum(jnp.where(col == base + 1, both, 0.0), axis=1, keepdims=True)
    num_s = jnp.sum(jnp.where(col == base + 2, both, 0.0), axis=1, keepdims=True)
    here = lax.axis_index("rcv")
    off_rows = max(1, num_off // peers)
    src_rows = num_src // rcv_n
    at_off = (lax.axis_index("src") * rcv_n + here) * off_rows
    for count, num, at, first, terms in (
        (off_rows, num_o, slice(0, piece), at_off, offset),
        (src_rows, num_s, slice(piece, 2 * piece), here * src_rows, source),
    ):
        last = terms.shape[0] - 1
        parts = [
            jnp.concatenate(
                [rows[j * (slots // count) + m : j * (slots // count) + m + 1, at] for j in range(count)],
                axis=0,
            )
            for m in range(rcv_n)
        ]
        whole = jnp.concatenate(parts, axis=1)
        e, r = edge // 2, (whole.shape[1] - edge) // 2
        whole = join(
            whole[:, edge : edge + r], whole[:, edge + r :], whole[:, :e], whole[:, e:edge]
        )
        old = jnp.concatenate(
            [terms[pl.ds(jnp.minimum(first + j, last), 1), :] for j in range(count)], axis=0
        )
        new = old + whole / (num[:count] + 1.0)
        block[:, at] = jnp.zeros((slots, piece), F32)
        for j in range(count):
            for m in range(rcv_n):
                to = j * (slots // count) + m
                block[to : to + 1, at] = new[j : j + 1, m * piece : (m + 1) * piece]
    src_out[...] = block[:, piece:]
    done = block[:, :piece]
    for d in range(peers):
        off_out[d * slots : (d + 1) * slots, :] = done


def receiver_kernel(num_off, num_src, got_hbm, sums_hbm, terms_hbm, out, got, sums, terms, sems):
    edge = got.shape[1] - LANES
    rest = sums.shape[1]
    copies = [
        pltpu.make_async_copy(got_hbm.at[:, : edge + LANES], got, sems.at[0]),
        pltpu.make_async_copy(sums_hbm.at[:, :rest], sums, sems.at[1]),
        pltpu.make_async_copy(terms_hbm, terms, sems.at[2]),
    ]
    start(copies)
    wait(copies)
    sent = got[:, edge:]
    value = terms[...]
    chosen = owner_hot(sent, num_off + num_src, value.shape[0]).astype(BF16)
    per_slot = jnp.where(iota(sent.shape, 1) < num_off, sent, 0.0)
    num = jnp.sum(chosen_sum(chosen, per_slot), axis=1, keepdims=True)
    one = chosen_sum(chosen, got[:, :edge])
    two = chosen_sum(chosen, sums[...])
    edge //= 2
    rest //= 2
    total = join(two[:, :rest], two[:, rest:], one[:, :edge], one[:, edge:])
    out[...] = value + (total - num * value) / (num + 1.0)


def source_kernel(rcv_n, *refs):
    src_out, rest, sems = refs[rcv_n:]
    copies = [pltpu.make_async_copy(refs[k], rest.at[k], sems.at[k]) for k in range(rcv_n)]
    start(copies)
    wait(copies)
    slots, piece = rest.shape[1:]
    count = src_out.shape[0] // rcv_n
    here = lax.axis_index("rcv")
    for j in range(rcv_n):
        value = jnp.zeros((slots, piece), F32)
        for k in range(rcv_n):
            value = value + jnp.where((here + rcv_n - k) % rcv_n == j, rest[k], 0.0)
        for i in range(count):
            for m in range(rcv_n):
                row = i * (slots // count) + m
                src_out[j * count + i : j * count + i + 1, m * piece : (m + 1) * piece] = (
                    value[row : row + 1]
                )


def swap(value, slots):
    shape = value.shape
    value = value.reshape(shape[0] // slots, slots, shape[1])
    value = lax.all_to_all(value, AXES, split_axis=0, concat_axis=0, tiled=True)
    return value.reshape(shape)


def local(
    traces,
    trace_source,
    trace_offset,
    trace_slot,
    request_list,
    source_terms,
    receiver_terms,
    offset_terms,
):
    src_n = lax.axis_size("src")
    rcv_n = lax.axis_size("rcv")
    peers = src_n * rcv_n
    slots = request_list.shape[2]
    num_tr, samples = traces.shape
    owned, freq = receiver_terms.shape
    num_src = source_terms.shape[0]
    num_off = offset_terms.shape[0]
    num_slot = peers * slots
    joint = joint_rows(num_off, num_src)
    rows = num_slot + joint
    half = freq // 2
    edge = half // 2
    rest = half - edge
    piece = freq // rcv_n
    off_rows = max(1, num_off // peers)
    tile = min(512, num_tr)
    assert slots == num_src and off_rows * rcv_n <= slots and num_off + num_src + 3 <= LANES
    assert samples == 2 * freq and freq % (4 * LANES) == 0 and owned <= 256
    assert rcv_n % 2 == 0 and piece == 2 * LANES and edge == rest
    ids = [v.reshape(1, num_tr) for v in (trace_slot, trace_offset, trace_source)]
    lists = jnp.swapaxes(request_list, 1, 2).reshape(slots, peers)
    vmem = pl.BlockSpec(memory_space=pltpu.VMEM)
    hbm = pl.BlockSpec(memory_space=pltpu.HBM)
    anywhere = pl.BlockSpec(memory_space=pl.ANY)

    def static(kernel, *args):
        return lambda *refs: kernel(*args, *refs)

    def shape(*dims):
        return jax.ShapeDtypeStruct(dims, F32)

    def spectra(head, width, counts, joint0):
        lead = not head
        first = 0 if lead else half - width
        consts = [jnp.asarray(v) for v in twiddles(samples, first, first + width)]
        return pl.pallas_call(
            static(spectra_kernel, num_off, num_src, rcv_n, head, lead, tile),
            out_shape=(
                shape(num_slot, 2 * width + (2 * LANES if head else piece)),
                shape(joint, 2 * width) if head else shape(joint + owned, half),
                shape(rows, LANES) if head else shape(joint + owned, half),
            ),
            in_specs=[hbm] * 13,
            out_specs=(hbm, hbm, hbm),
            scratch_shapes=[
                pltpu.VMEM((joint, half), F32),
                pltpu.VMEM((2, joint + owned, half), F32),
                pltpu.VMEM((num_tr, samples), BF16),
                pltpu.VMEM((3, 1, num_tr), jnp.int32),
                pltpu.VMEM((slots, peers), jnp.int32),
                pltpu.VMEM((LANES, freq), F32),
                pltpu.VMEM((owned, freq), F32),
                pltpu.VMEM((rows, LANES), F32),
                pltpu.VMEM((num_slot, 2 * LANES), F32),
                pltpu.VMEM(consts[0].shape, F32),
                pltpu.VMEM(consts[1].shape, F32),
                pltpu.VMEM(consts[2].shape, F32),
                pltpu.VMEM((2, freq, 2 * width), BF16),
                pltpu.VMEM((rows, num_tr), BF16),
                pltpu.VMEM((rows, 2 * width), F32),
                pltpu.VMEM((rows, 2 * width), F32),
                pltpu.VMEM((2, tile, 4 * width), F32),
                pltpu.SemaphoreType.DMA((11,)),
                pltpu.SemaphoreType.DMA((num_tr // tile,)),
            ],
            compiler_params=pltpu.CompilerParams(vmem_limit_bytes=56 * 2**20),
            name="spectra%d" % head,
        )(traces, *ids, lists, offset_terms, source_terms, receiver_terms, counts, joint0, *consts)

    pay, joint0, counts = spectra(True, edge, offset_terms, source_terms)
    got = swap(pay, slots)
    sent = got[:, 2 * edge :]
    pay, keep, mate = spectra(False, rest, counts, joint0)
    mate = lax.ppermute(mate, "rcv", [(j, j ^ 1) for j in range(rcv_n)])
    pair = jnp.concatenate([keep[:joint] + mate[:joint], keep[joint:], mate[joint:]], axis=0)
    pay = pl.pallas_call(
        static(pack_kernel, num_off, num_src, slots, src_n, rcv_n),
        out_shape=shape(*pay.shape),
        in_specs=[anywhere, hbm, hbm],
        out_specs=hbm,
        scratch_shapes=[
            pltpu.VMEM((num_slot, 2 * LANES), F32),
            pltpu.VMEM((joint + 2 * owned, half), F32),
            pltpu.VMEM((2, num_slot, LANES), F32),
            pltpu.SemaphoreType.DMA((2,)),
        ],
        input_output_aliases={2: 0},
        name="pack",
    )(sent, pair, pay)
    sums = swap(pay, slots)

    off_new, src_new = pl.pallas_call(
        static(shares_kernel, num_off, num_src, slots, 2 * edge),
        out_shape=(shape(num_slot, piece), shape(slots, piece)),
        in_specs=[anywhere, anywhere, hbm, hbm],
        out_specs=(vmem, vmem),
        scratch_shapes=[
            pltpu.VMEM((num_slot, LANES), F32),
            pltpu.VMEM((num_slot, piece), F32),
            pltpu.VMEM((num_off, freq), F32),
            pltpu.VMEM((num_src, freq), F32),
            pltpu.VMEM((slots, 2 * piece), F32),
            pltpu.VMEM((slots, 2 * piece), F32),
            pltpu.SemaphoreType.DMA((4,)),
        ],
        name="shares",
    )(sent, sums, offset_terms, source_terms)
    every = swap(off_new, slots)
    parts = [src_new]
    for k in range(1, rcv_n):
        ring = [(j, (j + k) % rcv_n) for j in range(rcv_n)]
        parts.append(lax.ppermute(src_new, "rcv", ring))
    receiver_new = pl.pallas_call(
        static(receiver_kernel, num_off, num_src),
        out_shape=shape(owned, freq),
        in_specs=[anywhere, anywhere, hbm],
        out_specs=vmem,
        scratch_shapes=[
            pltpu.VMEM((num_slot, 2 * edge + LANES), F32),
            pltpu.VMEM((num_slot, 2 * rest), F32),
            pltpu.VMEM((owned, freq), F32),
            pltpu.SemaphoreType.DMA((3,)),
        ],
        name="receiver",
    )(got, sums, receiver_terms)
    source_new = pl.pallas_call(
        static(source_kernel, rcv_n),
        out_shape=shape(num_src, freq),
        in_specs=[anywhere] * rcv_n,
        out_specs=vmem,
        scratch_shapes=[
            pltpu.VMEM((rcv_n, slots, piece), F32),
            pltpu.SemaphoreType.DMA((rcv_n,)),
        ],
        name="source",
    )(*parts)
    every = every.reshape(peers, off_rows, slots // off_rows, piece)[:, :, :rcv_n]
    offset_new = every.reshape(peers * off_rows, freq)[:num_off]
    return (source_new, receiver_new, offset_new)


def solution(mesh):
    return jax.shard_map(
        local,
        mesh=mesh,
        in_specs=(
            P(AXES, None),
            P(AXES),
            P(AXES),
            P(AXES),
            P(AXES, None, None),
            P("src", None),
            P(AXES, None),
            P(),
        ),
        out_specs=(P("src", None), P(AXES, None), P()),
        check_vma=False,
    )
```

```python
import math

import jax
import jax.numpy as jnp
import numpy as np
from jax import lax
from jax.experimental import pallas as pl
from jax.experimental.pallas import tpu as pltpu
from jax.sharding import PartitionSpec as P

AXES = ("src", "rcv")
LANES = 128
F32 = jnp.float32
BF16 = jnp.bfloat16
NT = (((1,), (1,)), ((), ()))
TN = (((0,), (0,)), ((), ()))
NN = (((1,), (0,)), ((), ()))


def twiddles(samples, first, last):
    half = samples // 2
    quarter = samples // 4
    lane = np.arange(LANES)
    even = np.where(lane % 2 == 0, lane, half - 1 + lane)
    odd = np.where(lane % 2 == 1, lane, half - 1 + lane + np.where(lane == 0, LANES, 0))
    freq = np.arange(quarter)
    groups = half // LANES
    unit = 2.0 * math.pi / samples
    base = []
    taper = []
    for rows, fold in ((even, -np.cos(even * quarter * unit)), (odd, np.sin(odd * quarter * unit))):
        phase = (rows[:, None] * freq[None, :] % samples) * unit
        sine = np.sin(phase)
        sine[:, 0] = np.round(fold)
        base += [np.cos(phase), sine]
        at = rows[:, None] + LANES * np.arange(groups)[None, :]
        taper.append((0.5 - 0.5 * np.cos((at + 0.5) * unit)) / math.sqrt(samples))
    turn = (LANES * np.arange(groups)[:, None] * freq[None, :] % samples) * unit
    turn = np.stack([np.cos(turn), np.sin(turn)])
    return (
        np.stack(base)[:, :, first:last].astype(np.float32),
        turn[:, :, first:last].astype(np.float32),
        np.stack(taper).astype(np.float32),
    )


def dot(a, b, dims=NN):
    return lax.dot_general(a, b, dims, preferred_element_type=F32)


def exact(a, b, dims=NN):
    return lax.dot_general(
        a, b, dims, precision=lax.Precision.HIGHEST, preferred_element_type=F32
    )


def pieces(value):
    one = value.astype(BF16)
    rest = value - one.astype(F32)
    two = rest.astype(BF16)
    return one, two, (rest - two.astype(F32)).astype(BF16)


def count_dot(counts, terms):
    counts = jnp.concatenate(halves(counts), axis=1)
    one, two, three = (jnp.concatenate([v, v], axis=0) for v in pieces(terms))
    return dot(counts, one) + dot(counts, two) + dot(counts, three)


def halves(counts):
    upper = counts.astype(BF16)
    return upper, (counts - upper.astype(F32)).astype(BF16)


def count_dot_tn(counts, terms):
    counts = jnp.concatenate(halves(counts), axis=0)
    one, two, three = (jnp.concatenate([v, v], axis=0) for v in pieces(terms))
    return dot(counts, one, TN) + dot(counts, two, TN) + dot(counts, three, TN)


def chosen_sum(chosen, value):
    one, two, three = pieces(value)
    return dot(chosen, one, TN) + dot(chosen, two, TN) + dot(chosen, three, TN)


def iota(shape, axis):
    return lax.broadcasted_iota(jnp.int32, shape, axis)


def hot(mask):
    return jnp.where(mask, 1.0, 0.0).astype(F32)


def ascend(value, lead):
    width = value.shape[1]
    row = iota((width, width), 0)
    col = iota((width, width), 1)
    if lead:
        pick = row == jnp.where(col == 0, 0, width - col)
    else:
        pick = row == width - 1 - col
    pick = hot(pick).astype(BF16)
    one, two, three = pieces(value)
    return dot(one, pick) + dot(two, pick) + dot(three, pick)


def join(low0, high0, low1, high1):
    edge = high1.shape[1]
    whole = jnp.concatenate([high1, high0], axis=1)
    col = iota(whole.shape, 1)
    shifted = pltpu.roll(whole, 1, 1)
    high = jnp.where(col <= edge, shifted, whole)
    high = jnp.where(col == 0, high0[:, :1], high)
    return jnp.concatenate([low0, low1, high], axis=1)


def part_of(value, first, width):
    half = value.shape[1] // 2
    high = value[:, half:]
    if first == 0:
        tail = high[:, half - width :]
        tail = jnp.where(iota(tail.shape, 1) == 0, high[:, :1], tail)
    else:
        tail = pltpu.roll(high, half - 1, 1)[:, :width]
    return jnp.concatenate([value[:, first : first + width], tail], axis=1)


def joint_rows(num_off, num_src):
    return -(-(num_off + num_src) // 16) * 16


def start(copies):
    for copy in copies:
        copy.start()


def wait(copies):
    for copy in copies:
        copy.wait()


def build_table(base, turn, taper, table):
    groups = taper.shape[2]
    width = base.shape[2]
    for side in range(2):
        for g in range(groups):
            cos0 = base[2 * side]
            sin0 = base[2 * side + 1]
            cos1 = turn[0, g : g + 1, :]
            sin1 = turn[1, g : g + 1, :]
            scale = taper[side, :, g : g + 1]
            at = slice(g * LANES, (g + 1) * LANES)
            table[side, at, :width] = ((cos0 * cos1 - sin0 * sin1) * scale).astype(BF16)
            table[side, at, width:] = ((sin0 * cos1 + cos0 * sin1) * -scale).astype(BF16)


def ident_rows(num_slot, num_off, rows, slot, off, src):
    top = iota((num_slot, slot.shape[1]), 0) == slot
    low = iota((rows - num_slot, slot.shape[1]), 0)
    low = (low == off) | (low == src + num_off)
    return jnp.concatenate([hot(top).astype(BF16), hot(low).astype(BF16)], axis=0)


def spectra_kernel(
    num_off, num_src, rcv_n, head, lead, tile,
    x_hbm, slot_hbm, off_hbm, src_hbm, lists_hbm, offset_hbm, source_hbm, own_hbm,
    counts_hbm, joint0_hbm, base_hbm, turn_hbm, taper_hbm, pay_hbm, joint_hbm, extra_hbm,
    joint0, swapped, x, ids, lists, terms, own, counts, extra, base, turn, taper, table, every, total, stage, spectrum, sems, x_sems,
):
    slots, peers = lists.shape
    num_slot = peers * slots
    rows = total.shape[0]
    width = base.shape[2]
    half = x.shape[1] // 2
    first = 0 if lead else width
    group = lax.axis_index("src")
    near = [
        pltpu.make_async_copy(base_hbm, base, sems.at[0]),
        pltpu.make_async_copy(turn_hbm, turn, sems.at[1]),
        pltpu.make_async_copy(taper_hbm, taper, sems.at[2]),
    ]
    far = [
        pltpu.make_async_copy(slot_hbm, ids.at[0], sems.at[3]),
        pltpu.make_async_copy(off_hbm, ids.at[1], sems.at[4]),
        pltpu.make_async_copy(src_hbm, ids.at[2], sems.at[5]),
        pltpu.make_async_copy(offset_hbm, terms.at[0:num_off], sems.at[6]),
        pltpu.make_async_copy(source_hbm, terms.at[num_off : num_off + num_src], sems.at[7]),
    ]
    if head:
        far.append(pltpu.make_async_copy(lists_hbm, lists, sems.at[8]))
    else:
        far.append(pltpu.make_async_copy(own_hbm, own, sems.at[8]))
        far.append(pltpu.make_async_copy(counts_hbm, counts, sems.at[9]))
        far.append(pltpu.make_async_copy(joint0_hbm, joint0, sems.at[10]))
    tiles = [
        pltpu.make_async_copy(
            x_hbm.at[t * tile : (t + 1) * tile], x.at[t * tile : (t + 1) * tile], x_sems.at[t]
        )
        for t in range(x.shape[0] // tile)
    ]
    start(far + near)
    spare = num_off + num_src
    terms[spare:, :] = jnp.zeros((terms.shape[0] - spare, terms.shape[1]), F32)
    total[...] = jnp.zeros_like(total)
    wait(far + near)
    start(tiles[:2])
    src = ids[2] - group * num_src
    every[...] = ident_rows(num_slot, num_off, rows, ids[0], ids[1], src)
    last = []
    if head:
        counts[...] = jnp.zeros_like(counts)
        counts[:, : rows - num_slot] = dot(every[...], every[num_slot:, :], NT)
        part = counts[:num_slot]
        whole = jnp.sum(part, axis=0, keepdims=True)
        row = iota((num_slot, LANES), 0)
        col = iota((num_slot, LANES), 1)
        peer = row // slots
        inner = row % slots
        off_rows = max(1, num_off // peers)
        src_rows = num_src // rcv_n
        is_off = (col == peer * off_rows + inner) & (inner < off_rows) & (col < num_off)
        is_src = (col == num_off + peer % rcv_n * src_rows + inner) & (inner < src_rows)
        is_src = is_src & (peer // rcv_n == group)
        num_o = jnp.sum(jnp.where(is_off, whole, 0.0), axis=1, keepdims=True)
        num_s = jnp.sum(jnp.where(is_src, whole, 0.0), axis=1, keepdims=True)
        spread = hot(iota((num_slot, peers), 0) // slots == iota((num_slot, peers), 1))
        listed = dot(spread.astype(BF16), lists[...].astype(F32).astype(BF16), NT)
        mine = iota((num_slot, slots), 0) % slots == iota((num_slot, slots), 1)
        asked = jnp.sum(jnp.where(mine, listed, 0.0), axis=1, keepdims=True)
        part = jnp.where(col == spare, asked, part)
        part = jnp.where(col == spare + 1, num_o, part)
        extra[:, :LANES] = jnp.where(col == spare + 2, num_s, part)
        for p in range(peers):
            mate = p ^ 1
            extra[p * slots : (p + 1) * slots, LANES:] = extra[
                mate * slots : (mate + 1) * slots, :LANES
            ]
        last.append(pltpu.make_async_copy(extra, pay_hbm.at[:, 2 * width :], sems.at[6]))
        last.append(pltpu.make_async_copy(counts, extra_hbm, sems.at[7]))
    else:
        kept = own[...]
        own[:, : 2 * width] = part_of(kept, width, width)
        own[:, 2 * width :] = part_of(kept, 0, width)
    start(last)
    stage[...] = count_dot(counts[...], part_of(terms[...], first, width))
    build_table(base, turn, taper, table)

    def transform(t):
        tiles[t].wait()
        start(tiles[t + 2 : t + 3])
        lane = iota((tile, LANES), 1) % 2 == 0
        even = []
        odd = []
        for g in range(half // LANES):
            front = x[t * tile : (t + 1) * tile, g * LANES : (g + 1) * LANES]
            back = x[t * tile : (t + 1) * tile, half + g * LANES : half + (g + 1) * LANES]
            back = pltpu.roll(back, 1, 1)
            even.append(jnp.where(lane, front, back))
            odd.append(jnp.where(lane, back, front))
        spectrum[t % 2, :, : 2 * width] = dot(jnp.concatenate(even, axis=1), table[0])
        spectrum[t % 2, :, 2 * width :] = dot(jnp.concatenate(odd, axis=1), table[1])

    def collect(t):
        ec, es, oc, os = (
            spectrum[t % 2, :, k * width : (k + 1) * width] for k in range(4)
        )
        re_low, im_low = ec + oc, es + os
        re_high, im_high = ec - oc, es - os
        if lead:
            zero = iota((tile, width), 1) == 0
            im_low = jnp.where(zero, 0.0, im_low)
            re_high = jnp.where(zero, es, re_high)
            im_high = jnp.where(zero, os, im_high)
        power = jnp.concatenate(
            [re_low * re_low + im_low * im_low, re_high * re_high + im_high * im_high], axis=1
        )
        amp = 0.5 * jnp.log(power + 0.01)
        upper = amp.astype(BF16)
        lower = (amp - upper.astype(F32)).astype(BF16)
        ids_t = every[:, t * tile : (t + 1) * tile]
        total[...] += dot(ids_t, upper) + dot(ids_t, lower)

    transform(0)
    for t in range(1, len(tiles)):
        transform(t)
        collect(t - 1)
    collect(len(tiles) - 1)
    stage[:, :width] = total[:, :width] - stage[:, :width]
    stage[:, width:] = ascend(total[:, width:], lead) - stage[:, width:]
    out = [pltpu.make_async_copy(stage.at[:num_slot], pay_hbm.at[:, : 2 * width], sems.at[0])]
    if head:
        out.append(pltpu.make_async_copy(stage.at[num_slot:], joint_hbm, sems.at[1]))
    else:
        odd = lax.axis_index("rcv") % 2 == 1
        cut = rows - num_slot
        for m in range(2 * width // LANES):
            lo, hi = 2 * m * LANES, (2 * m + 1) * LANES
            if hi < 2 * width:
                sums = joint0[:, lo:hi], joint0[:, hi : hi + LANES]
            else:
                lo, hi = lo - 2 * width, hi - 2 * width
                sums = stage[num_slot:, lo:hi], stage[num_slot:, hi : hi + LANES]
            both = own[:, 2 * m * LANES : (2 * m + 1) * LANES], own[:, (2 * m + 1) * LANES : (2 * m + 2) * LANES]
            at = slice(m * LANES, (m + 1) * LANES)
            swapped[0, :cut, at] = jnp.where(odd, sums[1], sums[0])
            swapped[1, :cut, at] = jnp.where(odd, sums[0], sums[1])
            swapped[0, cut:, at] = jnp.where(odd, both[1], both[0])
            swapped[1, cut:, at] = jnp.where(odd, both[0], both[1])
        out.append(pltpu.make_async_copy(swapped.at[0], joint_hbm, sems.at[1]))
        out.append(pltpu.make_async_copy(swapped.at[1], extra_hbm, sems.at[2]))
    start(out)
    wait(last + out)


def owner_hot(sent, base, owned):
    col = iota(sent.shape, 1)
    asked = jnp.sum(jnp.where(col == base, sent, 0.0), axis=1, keepdims=True).astype(jnp.int32)
    return hot(iota((sent.shape[0], owned), 1) == asked)


def pack_kernel(
    num_off, num_src, slots, src_n, rcv_n, sent_hbm, pair_hbm, _, out_hbm,
    sent, pair, out, sems,
):
    half = pair.shape[1]
    cut = joint_rows(num_off, num_src)
    owned = (pair.shape[0] - cut) // 2
    copies = [
        pltpu.make_async_copy(sent_hbm, sent, sems.at[0]),
        pltpu.make_async_copy(pair_hbm, pair, sems.at[1]),
    ]
    start(copies)
    copies[0].wait()
    num = sent.shape[0]
    group = lax.axis_index("src")
    every_src = src_n * num_src
    col = iota((LANES, every_src), 0)
    pick = hot(col == num_off + iota((LANES, every_src), 1) % num_src).astype(BF16)
    from_group = iota((num, every_src), 0) // (slots * rcv_n)
    from_group = from_group == iota((num, every_src), 1) // num_src
    off_of = []
    src_of = []
    for k in range(2):
        part = sent[:, k * LANES : (k + 1) * LANES]
        chosen = owner_hot(part, num_off + num_src, owned).astype(BF16)
        upper, lower = halves(part)
        by_src = [jnp.where(from_group, dot(v, pick), 0.0).astype(BF16) for v in (upper, lower)]
        off_of.append((dot(chosen, upper, TN) + dot(chosen, lower, TN))[:, :num_off])
        src_of.append(dot(chosen, by_src[0], TN) + dot(chosen, by_src[1], TN))
    wait(copies[1:])
    terms = pair[cut:, :]
    sums = pair[:cut, :]
    off_sum = sums[:num_off] - count_dot_tn(jnp.concatenate(off_of, axis=0), terms)
    src_sum = -count_dot_tn(jnp.concatenate(src_of, axis=0), terms)
    mine = sums[num_off : num_off + num_src]
    per_off = slots // max(1, num_off // (src_n * rcv_n))
    per_src = slots // (num_src // rcv_n)
    if num_off * per_off < num or per_off > rcv_n:
        out[...] = jnp.zeros_like(out)
    copies = [
        pltpu.make_async_copy(
            out.at[h], out_hbm.at[:, half + h * LANES : half + (h + 1) * LANES], sems.at[h]
        )
        for h in range(2)
    ]
    for m in range(rcv_n):
        at = slice(m * LANES, (m + 1) * LANES)
        out[0, pl.ds(m, num_off, stride=per_off), :] = off_sum[:, at]
    copies[0].start()
    for m in range(rcv_n):
        at = slice(m * LANES, (m + 1) * LANES)
        for i in range(src_n):
            to = pl.ds(i * num_src * per_src + m, num_src, stride=per_src)
            source = src_sum[i * num_src : (i + 1) * num_src, at]
            out[1, to, :] = source + jnp.where(group == i, mine[:, at], 0.0)
    copies[1].start()
    wait(copies)


def shares_kernel(
    num_off, num_src, slots, edge, got_hbm, sums_hbm, offset_hbm, source_hbm,
    off_out, src_out, sent, tail, offset, source, rows, block, sems,
):
    rcv_n = lax.axis_size("rcv")
    piece = src_out.shape[1]
    rest = sums_hbm.shape[1] - piece
    copies = [
        pltpu.make_async_copy(got_hbm.at[:, :LANES], sent, sems.at[0]),
        pltpu.make_async_copy(sums_hbm.at[:, rest:], tail, sems.at[1]),
        pltpu.make_async_copy(offset_hbm, offset, sems.at[2]),
        pltpu.make_async_copy(source_hbm, source, sems.at[3]),
    ]
    start(copies)
    wait(copies)
    peers = sent.shape[0] // slots
    base = num_off + num_src
    both = sent[0:slots]
    for d in range(1, peers):
        both = both + sent[d * slots : (d + 1) * slots]
    for k in range(2):
        value = tail[k * slots : (k + 1) * slots]
        for d in range(k + 2, peers, 2):
            value = value + tail[d * slots : (d + 1) * slots]
        rows[:, k * LANES : (k + 1) * LANES] = value[:, :LANES]
        rows[:, piece + k * LANES : piece + (k + 1) * LANES] = value[:, LANES:]
    col = iota(both.shape, 1)
    num_o = jnp.sum(jnp.where(col == base + 1, both, 0.0), axis=1, keepdims=True)
    num_s = jnp.sum(jnp.where(col == base + 2, both, 0.0), axis=1, keepdims=True)
    here = lax.axis_index("rcv")
    off_rows = max(1, num_off // peers)
    src_rows = num_src // rcv_n
    at_off = (lax.axis_index("src") * rcv_n + here) * off_rows
    for count, num, at, first, terms in (
        (off_rows, num_o, slice(0, piece), at_off, offset),
        (src_rows, num_s, slice(piece, 2 * piece), here * src_rows, source),
    ):
        last = terms.shape[0] - 1
        parts = [
            jnp.concatenate(
                [rows[j * (slots // count) + m : j * (slots // count) + m + 1, at] for j in range(count)],
                axis=0,
            )
            for m in range(rcv_n)
        ]
        whole = jnp.concatenate(parts, axis=1)
        e, r = edge // 2, (whole.shape[1] - edge) // 2
        whole = join(
            whole[:, edge : edge + r], whole[:, edge + r :], whole[:, :e], whole[:, e:edge]
        )
        old = jnp.concatenate(
            [terms[pl.ds(jnp.minimum(first + j, last), 1), :] for j in range(count)], axis=0
        )
        new = old + whole / (num[:count] + 1.0)
        block[:, at] = jnp.zeros((slots, piece), F32)
        for j in range(count):
            for m in range(rcv_n):
                to = j * (slots // count) + m
                block[to : to + 1, at] = new[j : j + 1, m * piece : (m + 1) * piece]
    src_out[...] = block[:, piece:]
    done = block[:, :piece]
    for d in range(peers):
        off_out[d * slots : (d + 1) * slots, :] = done


def receiver_kernel(num_off, num_src, got_hbm, sums_hbm, terms_hbm, out, got, sums, terms, sems):
    edge = got.shape[1] - LANES
    rest = sums.shape[1]
    copies = [
        pltpu.make_async_copy(got_hbm.at[:, : edge + LANES], got, sems.at[0]),
        pltpu.make_async_copy(sums_hbm.at[:, :rest], sums, sems.at[1]),
        pltpu.make_async_copy(terms_hbm, terms, sems.at[2]),
    ]
    start(copies)
    wait(copies)
    sent = got[:, edge:]
    value = terms[...]
    chosen = owner_hot(sent, num_off + num_src, value.shape[0]).astype(BF16)
    per_slot = jnp.where(iota(sent.shape, 1) < num_off, sent, 0.0)
    num = jnp.sum(chosen_sum(chosen, per_slot), axis=1, keepdims=True)
    one = chosen_sum(chosen, got[:, :edge])
    two = chosen_sum(chosen, sums[...])
    edge //= 2
    rest //= 2
    total = join(two[:, :rest], two[:, rest:], one[:, :edge], one[:, edge:])
    out[...] = value + (total - num * value) / (num + 1.0)


def source_kernel(rcv_n, *refs):
    src_out, rest, sems = refs[rcv_n:]
    copies = [pltpu.make_async_copy(refs[k], rest.at[k], sems.at[k]) for k in range(rcv_n)]
    start(copies)
    wait(copies)
    slots, piece = rest.shape[1:]
    count = src_out.shape[0] // rcv_n
    here = lax.axis_index("rcv")
    for j in range(rcv_n):
        value = jnp.zeros((slots, piece), F32)
        for k in range(rcv_n):
            value = value + jnp.where((here + rcv_n - k) % rcv_n == j, rest[k], 0.0)
        for i in range(count):
            for m in range(rcv_n):
                row = i * (slots // count) + m
                src_out[j * count + i : j * count + i + 1, m * piece : (m + 1) * piece] = (
                    value[row : row + 1]
                )


def swap(value, slots):
    shape = value.shape
    value = value.reshape(shape[0] // slots, slots, shape[1])
    value = lax.all_to_all(value, AXES, split_axis=0, concat_axis=0, tiled=True)
    return value.reshape(shape)


def local(
    traces,
    trace_source,
    trace_offset,
    trace_slot,
    request_list,
    source_terms,
    receiver_terms,
    offset_terms,
):
    src_n = lax.axis_size("src")
    rcv_n = lax.axis_size("rcv")
    peers = src_n * rcv_n
    slots = request_list.shape[2]
    num_tr, samples = traces.shape
    owned, freq = receiver_terms.shape
    num_src = source_terms.shape[0]
    num_off = offset_terms.shape[0]
    num_slot = peers * slots
    joint = joint_rows(num_off, num_src)
    rows = num_slot + joint
    half = freq // 2
    edge = half // 2
    rest = half - edge
    piece = freq // rcv_n
    off_rows = max(1, num_off // peers)
    tile = min(512, num_tr)
    assert slots == num_src and off_rows * rcv_n <= slots and num_off + num_src + 3 <= LANES
    assert samples == 2 * freq and freq % (4 * LANES) == 0 and owned <= 256
    assert rcv_n % 2 == 0 and piece == 2 * LANES and edge == rest
    ids = [v.reshape(1, num_tr) for v in (trace_slot, trace_offset, trace_source)]
    lists = jnp.swapaxes(request_list, 1, 2).reshape(slots, peers)
    vmem = pl.BlockSpec(memory_space=pltpu.VMEM)
    hbm = pl.BlockSpec(memory_space=pltpu.HBM)
    anywhere = pl.BlockSpec(memory_space=pl.ANY)

    def static(kernel, *args):
        return lambda *refs: kernel(*args, *refs)

    def shape(*dims):
        return jax.ShapeDtypeStruct(dims, F32)

    def spectra(head, width, counts, joint0):
        lead = not head
        first = 0 if lead else half - width
        consts = [jnp.asarray(v) for v in twiddles(samples, first, first + width)]
        return pl.pallas_call(
            static(spectra_kernel, num_off, num_src, rcv_n, head, lead, tile),
            out_shape=(
                shape(num_slot, 2 * width + (2 * LANES if head else piece)),
                shape(joint, 2 * width) if head else shape(joint + owned, half),
                shape(rows, LANES) if head else shape(joint + owned, half),
            ),
            in_specs=[hbm] * 13,
            out_specs=(hbm, hbm, hbm),
            scratch_shapes=[
                pltpu.VMEM((joint, half), F32),
                pltpu.VMEM((2, joint + owned, half), F32),
                pltpu.VMEM((num_tr, samples), BF16),
                pltpu.VMEM((3, 1, num_tr), jnp.int32),
                pltpu.VMEM((slots, peers), jnp.int32),
                pltpu.VMEM((LANES, freq), F32),
                pltpu.VMEM((owned, freq), F32),
                pltpu.VMEM((rows, LANES), F32),
                pltpu.VMEM((num_slot, 2 * LANES), F32),
                pltpu.VMEM(consts[0].shape, F32),
                pltpu.VMEM(consts[1].shape, F32),
                pltpu.VMEM(consts[2].shape, F32),
                pltpu.VMEM((2, freq, 2 * width), BF16),
                pltpu.VMEM((rows, num_tr), BF16),
                pltpu.VMEM((rows, 2 * width), F32),
                pltpu.VMEM((rows, 2 * width), F32),
                pltpu.VMEM((2, tile, 4 * width), F32),
                pltpu.SemaphoreType.DMA((11,)),
                pltpu.SemaphoreType.DMA((num_tr // tile,)),
            ],
            compiler_params=pltpu.CompilerParams(vmem_limit_bytes=56 * 2**20),
            name="spectra%d" % head,
        )(traces, *ids, lists, offset_terms, source_terms, receiver_terms, counts, joint0, *consts)

    pay, joint0, counts = spectra(True, edge, offset_terms, source_terms)
    got = swap(pay, slots)
    sent = got[:, 2 * edge :]
    pay, keep, mate = spectra(False, rest, counts, joint0)
    mate = lax.ppermute(mate, "rcv", [(j, j ^ 1) for j in range(rcv_n)])
    pair = jnp.concatenate([keep[:joint] + mate[:joint], keep[joint:], mate[joint:]], axis=0)
    pay = pl.pallas_call(
        static(pack_kernel, num_off, num_src, slots, src_n, rcv_n),
        out_shape=shape(*pay.shape),
        in_specs=[anywhere, hbm, hbm],
        out_specs=hbm,
        scratch_shapes=[
            pltpu.VMEM((num_slot, 2 * LANES), F32),
            pltpu.VMEM((joint + 2 * owned, half), F32),
            pltpu.VMEM((2, num_slot, LANES), F32),
            pltpu.SemaphoreType.DMA((2,)),
        ],
        input_output_aliases={2: 0},
        name="pack",
    )(sent, pair, pay)
    sums = swap(pay, slots)

    off_new, src_new = pl.pallas_call(
        static(shares_kernel, num_off, num_src, slots, 2 * edge),
        out_shape=(shape(num_slot, piece), shape(slots, piece)),
        in_specs=[anywhere, anywhere, hbm, hbm],
        out_specs=(vmem, vmem),
        scratch_shapes=[
            pltpu.VMEM((num_slot, LANES), F32),
            pltpu.VMEM((num_slot, piece), F32),
            pltpu.VMEM((num_off, freq), F32),
            pltpu.VMEM((num_src, freq), F32),
            pltpu.VMEM((slots, 2 * piece), F32),
            pltpu.VMEM((slots, 2 * piece), F32),
            pltpu.SemaphoreType.DMA((4,)),
        ],
        name="shares",
    )(sent, sums, offset_terms, source_terms)
    every = swap(off_new, slots)
    parts = [src_new]
    for k in range(1, rcv_n):
        ring = [(j, (j + k) % rcv_n) for j in range(rcv_n)]
        parts.append(lax.ppermute(src_new, "rcv", ring))
    receiver_new = pl.pallas_call(
        static(receiver_kernel, num_off, num_src),
        out_shape=shape(owned, freq),
        in_specs=[anywhere, anywhere, hbm],
        out_specs=vmem,
        scratch_shapes=[
            pltpu.VMEM((num_slot, 2 * edge + LANES), F32),
            pltpu.VMEM((num_slot, 2 * rest), F32),
            pltpu.VMEM((owned, freq), F32),
            pltpu.SemaphoreType.DMA((3,)),
        ],
        name="receiver",
    )(got, sums, receiver_terms)
    source_new = pl.pallas_call(
        static(source_kernel, rcv_n),
        out_shape=shape(num_src, freq),
        in_specs=[anywhere] * rcv_n,
        out_specs=vmem,
        scratch_shapes=[
            pltpu.VMEM((rcv_n, slots, piece), F32),
            pltpu.SemaphoreType.DMA((rcv_n,)),
        ],
        name="source",
    )(*parts)
    every = every.reshape(peers, off_rows, slots // off_rows, piece)[:, :, :rcv_n]
    offset_new = every.reshape(peers * off_rows, freq)[:num_off]
    return (source_new, receiver_new, offset_new)


def solution(mesh):
    return jax.shard_map(
        local,
        mesh=mesh,
        in_specs=(
            P(AXES, None),
            P(AXES),
            P(AXES),
            P(AXES),
            P(AXES, None, None),
            P("src", None),
            P(AXES, None),
            P(),
        ),
        out_specs=(P("src", None), P(AXES, None), P()),
        check_vma=False,
    )
```

```python
import math

import jax
import jax.numpy as jnp
import numpy as np
from jax import lax
from jax.experimental import pallas as pl
from jax.experimental.pallas import tpu as pltpu
from jax.sharding import PartitionSpec as P

AXES = ("src", "rcv")
LANES = 128
F32 = jnp.float32
BF16 = jnp.bfloat16
NT = (((1,), (1,)), ((), ()))
TN = (((0,), (0,)), ((), ()))
NN = (((1,), (0,)), ((), ()))


def twiddles(samples, first, last):
    half = samples // 2
    quarter = samples // 4
    lane = np.arange(LANES)
    even = np.where(lane % 2 == 0, lane, half - 1 + lane)
    odd = np.where(lane % 2 == 1, lane, half - 1 + lane + np.where(lane == 0, LANES, 0))
    freq = np.arange(quarter)
    groups = half // LANES
    unit = 2.0 * math.pi / samples
    base = []
    taper = []
    for rows, fold in ((even, -np.cos(even * quarter * unit)), (odd, np.sin(odd * quarter * unit))):
        phase = (rows[:, None] * freq[None, :] % samples) * unit
        sine = np.sin(phase)
        sine[:, 0] = np.round(fold)
        base += [np.cos(phase), sine]
        at = rows[:, None] + LANES * np.arange(groups)[None, :]
        taper.append((0.5 - 0.5 * np.cos((at + 0.5) * unit)) / math.sqrt(samples))
    turn = (LANES * np.arange(groups)[:, None] * freq[None, :] % samples) * unit
    turn = np.stack([np.cos(turn), np.sin(turn)])
    return (
        np.stack(base)[:, :, first:last].astype(np.float32),
        turn[:, :, first:last].astype(np.float32),
        np.stack(taper).astype(np.float32),
    )


def dot(a, b, dims=NN):
    return lax.dot_general(a, b, dims, preferred_element_type=F32)


def exact(a, b, dims=NN):
    return lax.dot_general(
        a, b, dims, precision=lax.Precision.HIGHEST, preferred_element_type=F32
    )


def pieces(value):
    one = value.astype(BF16)
    rest = value - one.astype(F32)
    two = rest.astype(BF16)
    return one, two, (rest - two.astype(F32)).astype(BF16)


def count_dot(counts, terms):
    counts = jnp.concatenate(halves(counts), axis=1)
    one, two, three = (jnp.concatenate([v, v], axis=0) for v in pieces(terms))
    return dot(counts, one) + dot(counts, two) + dot(counts, three)


def halves(counts):
    upper = counts.astype(BF16)
    return upper, (counts - upper.astype(F32)).astype(BF16)


def count_dot_tn(counts, terms):
    counts = jnp.concatenate(halves(counts), axis=0)
    one, two, three = (jnp.concatenate([v, v], axis=0) for v in pieces(terms))
    return dot(counts, one, TN) + dot(counts, two, TN) + dot(counts, three, TN)


def chosen_sum(chosen, value):
    one, two, three = pieces(value)
    return dot(chosen, one, TN) + dot(chosen, two, TN) + dot(chosen, three, TN)


def iota(shape, axis):
    return lax.broadcasted_iota(jnp.int32, shape, axis)


def hot(mask):
    return jnp.where(mask, 1.0, 0.0).astype(F32)


def ascend(value, lead):
    width = value.shape[1]
    row = iota((width, width), 0)
    col = iota((width, width), 1)
    if lead:
        pick = row == jnp.where(col == 0, 0, width - col)
    else:
        pick = row == width - 1 - col
    pick = hot(pick).astype(BF16)
    one, two, three = pieces(value)
    return dot(one, pick) + dot(two, pick) + dot(three, pick)


def join(low0, high0, low1, high1):
    edge = high1.shape[1]
    whole = jnp.concatenate([high1, high0], axis=1)
    col = iota(whole.shape, 1)
    shifted = pltpu.roll(whole, 1, 1)
    high = jnp.where(col <= edge, shifted, whole)
    high = jnp.where(col == 0, high0[:, :1], high)
    return jnp.concatenate([low0, low1, high], axis=1)


def part_of(value, first, width):
    half = value.shape[1] // 2
    high = value[:, half:]
    if first == 0:
        tail = high[:, half - width :]
        tail = jnp.where(iota(tail.shape, 1) == 0, high[:, :1], tail)
    else:
        tail = pltpu.roll(high, half - 1, 1)[:, :width]
    return jnp.concatenate([value[:, first : first + width], tail], axis=1)


def joint_rows(num_off, num_src):
    return -(-(num_off + num_src) // 16) * 16


def start(copies):
    for copy in copies:
        copy.start()


def wait(copies):
    for copy in copies:
        copy.wait()


def build_table(base, turn, taper, table):
    groups = taper.shape[2]
    width = base.shape[2]
    for side in range(2):
        for g in range(groups):
            cos0 = base[2 * side]
            sin0 = base[2 * side + 1]
            cos1 = turn[0, g : g + 1, :]
            sin1 = turn[1, g : g + 1, :]
            scale = taper[side, :, g : g + 1]
            at = slice(g * LANES, (g + 1) * LANES)
            table[side, at, :width] = ((cos0 * cos1 - sin0 * sin1) * scale).astype(BF16)
            table[side, at, width:] = ((sin0 * cos1 + cos0 * sin1) * -scale).astype(BF16)


def ident_rows(num_slot, num_off, rows, slot, off, src):
    top = iota((num_slot, slot.shape[1]), 0) == slot
    low = iota((rows - num_slot, slot.shape[1]), 0)
    low = (low == off) | (low == src + num_off)
    return jnp.concatenate([hot(top).astype(BF16), hot(low).astype(BF16)], axis=0)


def spectra_kernel(
    num_off, num_src, rcv_n, head, lead, tile,
    x_hbm, slot_hbm, off_hbm, src_hbm, lists_hbm, offset_hbm, source_hbm, own_hbm,
    counts_hbm, joint0_hbm, base_hbm, turn_hbm, taper_hbm, pay_hbm, joint_hbm, extra_hbm,
    joint0, swapped, x, ids, lists, terms, own, counts, extra, base, turn, taper, table, every, total, stage, spectrum, sems, x_sems,
):
    slots, peers = lists.shape
    num_slot = peers * slots
    rows = total.shape[0]
    width = base.shape[2]
    half = x.shape[1] // 2
    first = 0 if lead else width
    group = lax.axis_index("src")
    near = [
        pltpu.make_async_copy(base_hbm, base, sems.at[0]),
        pltpu.make_async_copy(turn_hbm, turn, sems.at[1]),
        pltpu.make_async_copy(taper_hbm, taper, sems.at[2]),
    ]
    far = [
        pltpu.make_async_copy(slot_hbm, ids.at[0], sems.at[3]),
        pltpu.make_async_copy(off_hbm, ids.at[1], sems.at[4]),
        pltpu.make_async_copy(src_hbm, ids.at[2], sems.at[5]),
    ]
    late = [
        pltpu.make_async_copy(offset_hbm, terms.at[0:num_off], sems.at[6]),
        pltpu.make_async_copy(source_hbm, terms.at[num_off : num_off + num_src], sems.at[7]),
    ]
    if head:
        far.append(pltpu.make_async_copy(lists_hbm, lists, sems.at[8]))
    else:
        far.append(pltpu.make_async_copy(own_hbm, own, sems.at[8]))
        far.append(pltpu.make_async_copy(counts_hbm, counts, sems.at[9]))
        far.append(pltpu.make_async_copy(joint0_hbm, joint0, sems.at[10]))
        far += late
    tiles = [
        pltpu.make_async_copy(
            x_hbm.at[t * tile : (t + 1) * tile], x.at[t * tile : (t + 1) * tile], x_sems.at[t]
        )
        for t in range(x.shape[0] // tile)
    ]
    start(far + near)
    spare = num_off + num_src
    terms[spare:, :] = jnp.zeros((terms.shape[0] - spare, terms.shape[1]), F32)
    total[...] = jnp.zeros_like(total)
    wait(far + near)
    start(late + tiles[:2] if head else tiles[:2])
    src = ids[2] - group * num_src
    every[...] = ident_rows(num_slot, num_off, rows, ids[0], ids[1], src)
    last = []
    if head:
        at = iota((LANES, x.shape[0]), 0)
        joint = hot((at == ids[1]) | (at == src + num_off)).astype(BF16)
        counts[...] = dot(every[...], joint, NT)
        part = counts[:num_slot]
        whole = jnp.sum(part, axis=0, keepdims=True)
        row = iota((num_slot, LANES), 0)
        col = iota((num_slot, LANES), 1)
        peer = row // slots
        inner = row % slots
        off_rows = max(1, num_off // peers)
        src_rows = num_src // rcv_n
        is_off = (col == peer * off_rows + inner) & (inner < off_rows) & (col < num_off)
        is_src = (col == num_off + peer % rcv_n * src_rows + inner) & (inner < src_rows)
        is_src = is_src & (peer // rcv_n == group)
        num_o = jnp.sum(jnp.where(is_off, whole, 0.0), axis=1, keepdims=True)
        num_s = jnp.sum(jnp.where(is_src, whole, 0.0), axis=1, keepdims=True)
        spread = hot(iota((num_slot, peers), 0) // slots == iota((num_slot, peers), 1))
        listed = dot(spread.astype(BF16), lists[...].astype(F32).astype(BF16), NT)
        mine = iota((num_slot, slots), 0) % slots == iota((num_slot, slots), 1)
        asked = jnp.sum(jnp.where(mine, listed, 0.0), axis=1, keepdims=True)
        part = jnp.where(col == spare, asked, part)
        part = jnp.where(col == spare + 1, num_o, part)
        extra[:, :LANES] = jnp.where(col == spare + 2, num_s, part)
        for p in range(peers):
            mate = p ^ 1
            extra[p * slots : (p + 1) * slots, LANES:] = extra[
                mate * slots : (mate + 1) * slots, :LANES
            ]
        last.append(pltpu.make_async_copy(extra, pay_hbm.at[:, 2 * width :], sems.at[9]))
        last.append(pltpu.make_async_copy(counts, extra_hbm, sems.at[10]))
    else:
        kept = own[...]
        own[:, : 2 * width] = part_of(kept, width, width)
        own[:, 2 * width :] = part_of(kept, 0, width)
    start(last)
    build_table(base, turn, taper, table)
    if head:
        wait(late)
    stage[...] = count_dot(counts[...], part_of(terms[...], first, width))

    def transform(t):
        tiles[t].wait()
        start(tiles[t + 2 : t + 3])
        lane = iota((tile, LANES), 1) % 2 == 0
        even = []
        odd = []
        for g in range(half // LANES):
            front = x[t * tile : (t + 1) * tile, g * LANES : (g + 1) * LANES]
            back = x[t * tile : (t + 1) * tile, half + g * LANES : half + (g + 1) * LANES]
            back = pltpu.roll(back, 1, 1)
            even.append(jnp.where(lane, front, back))
            odd.append(jnp.where(lane, back, front))
        spectrum[t % 2, :, : 2 * width] = dot(jnp.concatenate(even, axis=1), table[0])
        spectrum[t % 2, :, 2 * width :] = dot(jnp.concatenate(odd, axis=1), table[1])

    def collect(t):
        ec, es, oc, os = (
            spectrum[t % 2, :, k * width : (k + 1) * width] for k in range(4)
        )
        re_low, im_low = ec + oc, es + os
        re_high, im_high = ec - oc, es - os
        if lead:
            zero = iota((tile, width), 1) == 0
            im_low = jnp.where(zero, 0.0, im_low)
            re_high = jnp.where(zero, es, re_high)
            im_high = jnp.where(zero, os, im_high)
        power = jnp.concatenate(
            [re_low * re_low + im_low * im_low, re_high * re_high + im_high * im_high], axis=1
        )
        amp = 0.5 * jnp.log(power + 0.01)
        upper = amp.astype(BF16)
        lower = (amp - upper.astype(F32)).astype(BF16)
        ids_t = every[:, t * tile : (t + 1) * tile]
        total[...] += dot(ids_t, upper) + dot(ids_t, lower)

    transform(0)
    for t in range(1, len(tiles)):
        transform(t)
        collect(t - 1)
    collect(len(tiles) - 1)
    stage[:, :width] = total[:, :width] - stage[:, :width]
    stage[:, width:] = ascend(total[:, width:], lead) - stage[:, width:]
    out = [pltpu.make_async_copy(stage.at[:num_slot], pay_hbm.at[:, : 2 * width], sems.at[0])]
    if head:
        out.append(pltpu.make_async_copy(stage.at[num_slot:], joint_hbm, sems.at[1]))
    else:
        odd = lax.axis_index("rcv") % 2 == 1
        cut = rows - num_slot
        for m in range(2 * width // LANES):
            lo, hi = 2 * m * LANES, (2 * m + 1) * LANES
            if hi < 2 * width:
                sums = joint0[:, lo:hi], joint0[:, hi : hi + LANES]
            else:
                lo, hi = lo - 2 * width, hi - 2 * width
                sums = stage[num_slot:, lo:hi], stage[num_slot:, hi : hi + LANES]
            both = own[:, 2 * m * LANES : (2 * m + 1) * LANES], own[:, (2 * m + 1) * LANES : (2 * m + 2) * LANES]
            at = slice(m * LANES, (m + 1) * LANES)
            swapped[0, :cut, at] = jnp.where(odd, sums[1], sums[0])
            swapped[1, :cut, at] = jnp.where(odd, sums[0], sums[1])
            swapped[0, cut:, at] = jnp.where(odd, both[1], both[0])
            swapped[1, cut:, at] = jnp.where(odd, both[0], both[1])
        out.append(pltpu.make_async_copy(swapped.at[0], joint_hbm, sems.at[1]))
        out.append(pltpu.make_async_copy(swapped.at[1], extra_hbm, sems.at[2]))
    start(out)
    wait(last + out)


def owner_hot(sent, base, owned):
    col = iota(sent.shape, 1)
    asked = jnp.sum(jnp.where(col == base, sent, 0.0), axis=1, keepdims=True).astype(jnp.int32)
    return hot(iota((sent.shape[0], owned), 1) == asked)


def pack_kernel(
    num_off, num_src, slots, src_n, rcv_n, sent_hbm, pair_hbm, _, out_hbm,
    sent, pair, out, sems,
):
    half = pair.shape[1]
    cut = joint_rows(num_off, num_src)
    owned = (pair.shape[0] - cut) // 2
    copies = [
        pltpu.make_async_copy(sent_hbm, sent, sems.at[0]),
        pltpu.make_async_copy(pair_hbm, pair, sems.at[1]),
    ]
    start(copies)
    copies[0].wait()
    num = sent.shape[0]
    group = lax.axis_index("src")
    every_src = src_n * num_src
    col = iota((LANES, every_src), 0)
    pick = hot(col == num_off + iota((LANES, every_src), 1) % num_src).astype(BF16)
    from_group = iota((num, every_src), 0) // (slots * rcv_n)
    from_group = from_group == iota((num, every_src), 1) // num_src
    off_of = []
    src_of = []
    for k in range(2):
        part = sent[:, k * LANES : (k + 1) * LANES]
        chosen = owner_hot(part, num_off + num_src, owned).astype(BF16)
        upper, lower = halves(part)
        by_src = [jnp.where(from_group, dot(v, pick), 0.0).astype(BF16) for v in (upper, lower)]
        off_of.append((dot(chosen, upper, TN) + dot(chosen, lower, TN))[:, :num_off])
        src_of.append(dot(chosen, by_src[0], TN) + dot(chosen, by_src[1], TN))
    wait(copies[1:])
    terms = pair[cut:, :]
    sums = pair[:cut, :]
    off_sum = sums[:num_off] - count_dot_tn(jnp.concatenate(off_of, axis=0), terms)
    src_sum = -count_dot_tn(jnp.concatenate(src_of, axis=0), terms)
    mine = sums[num_off : num_off + num_src]
    per_off = slots // max(1, num_off // (src_n * rcv_n))
    per_src = slots // (num_src // rcv_n)
    if num_off * per_off < num or per_off > rcv_n:
        out[...] = jnp.zeros_like(out)
    copies = [
        pltpu.make_async_copy(
            out.at[h], out_hbm.at[:, half + h * LANES : half + (h + 1) * LANES], sems.at[h]
        )
        for h in range(2)
    ]
    for m in range(rcv_n):
        at = slice(m * LANES, (m + 1) * LANES)
        out[0, pl.ds(m, num_off, stride=per_off), :] = off_sum[:, at]
    copies[0].start()
    for m in range(rcv_n):
        at = slice(m * LANES, (m + 1) * LANES)
        for i in range(src_n):
            to = pl.ds(i * num_src * per_src + m, num_src, stride=per_src)
            source = src_sum[i * num_src : (i + 1) * num_src, at]
            out[1, to, :] = source + jnp.where(group == i, mine[:, at], 0.0)
    copies[1].start()
    wait(copies)


def shares_kernel(
    num_off, num_src, slots, edge, got_hbm, sums_hbm, offset_hbm, source_hbm,
    off_out, src_out, sent, tail, offset, source, rows, block, sems,
):
    rcv_n = lax.axis_size("rcv")
    piece = src_out.shape[1]
    rest = sums_hbm.shape[1] - piece
    copies = [
        pltpu.make_async_copy(got_hbm.at[:, :LANES], sent, sems.at[0]),
        pltpu.make_async_copy(sums_hbm.at[:, rest:], tail, sems.at[1]),
        pltpu.make_async_copy(offset_hbm, offset, sems.at[2]),
        pltpu.make_async_copy(source_hbm, source, sems.at[3]),
    ]
    start(copies)
    wait(copies)
    peers = sent.shape[0] // slots
    base = num_off + num_src
    both = sent[0:slots]
    for d in range(1, peers):
        both = both + sent[d * slots : (d + 1) * slots]
    for k in range(2):
        value = tail[k * slots : (k + 1) * slots]
        for d in range(k + 2, peers, 2):
            value = value + tail[d * slots : (d + 1) * slots]
        rows[:, k * LANES : (k + 1) * LANES] = value[:, :LANES]
        rows[:, piece + k * LANES : piece + (k + 1) * LANES] = value[:, LANES:]
    col = iota(both.shape, 1)
    num_o = jnp.sum(jnp.where(col == base + 1, both, 0.0), axis=1, keepdims=True)
    num_s = jnp.sum(jnp.where(col == base + 2, both, 0.0), axis=1, keepdims=True)
    here = lax.axis_index("rcv")
    off_rows = max(1, num_off // peers)
    src_rows = num_src // rcv_n
    at_off = (lax.axis_index("src") * rcv_n + here) * off_rows
    for count, num, at, first, terms in (
        (off_rows, num_o, slice(0, piece), at_off, offset),
        (src_rows, num_s, slice(piece, 2 * piece), here * src_rows, source),
    ):
        last = terms.shape[0] - 1
        parts = [
            jnp.concatenate(
                [rows[j * (slots // count) + m : j * (slots // count) + m + 1, at] for j in range(count)],
                axis=0,
            )
            for m in range(rcv_n)
        ]
        whole = jnp.concatenate(parts, axis=1)
        e, r = edge // 2, (whole.shape[1] - edge) // 2
        whole = join(
            whole[:, edge : edge + r], whole[:, edge + r :], whole[:, :e], whole[:, e:edge]
        )
        old = jnp.concatenate(
            [terms[pl.ds(jnp.minimum(first + j, last), 1), :] for j in range(count)], axis=0
        )
        new = old + whole / (num[:count] + 1.0)
        block[:, at] = jnp.zeros((slots, piece), F32)
        for j in range(count):
            for m in range(rcv_n):
                to = j * (slots // count) + m
                block[to : to + 1, at] = new[j : j + 1, m * piece : (m + 1) * piece]
    src_out[...] = block[:, piece:]
    done = block[:, :piece]
    for d in range(peers):
        off_out[d * slots : (d + 1) * slots, :] = done


def receiver_kernel(num_off, num_src, got_hbm, sums_hbm, terms_hbm, out, got, sums, terms, sems):
    edge = got.shape[1] - LANES
    rest = sums.shape[1]
    copies = [
        pltpu.make_async_copy(got_hbm.at[:, : edge + LANES], got, sems.at[0]),
        pltpu.make_async_copy(sums_hbm.at[:, :rest], sums, sems.at[1]),
        pltpu.make_async_copy(terms_hbm, terms, sems.at[2]),
    ]
    start(copies)
    wait(copies)
    sent = got[:, edge:]
    value = terms[...]
    chosen = owner_hot(sent, num_off + num_src, value.shape[0]).astype(BF16)
    per_slot = jnp.where(iota(sent.shape, 1) < num_off, sent, 0.0)
    num = jnp.sum(chosen_sum(chosen, per_slot), axis=1, keepdims=True)
    one = chosen_sum(chosen, got[:, :edge])
    two = chosen_sum(chosen, sums[...])
    edge //= 2
    rest //= 2
    total = join(two[:, :rest], two[:, rest:], one[:, :edge], one[:, edge:])
    out[...] = value + (total - num * value) / (num + 1.0)


def source_kernel(rcv_n, *refs):
    src_out, rest, sems = refs[rcv_n:]
    copies = [pltpu.make_async_copy(refs[k], rest.at[k], sems.at[k]) for k in range(rcv_n)]
    start(copies)
    wait(copies)
    slots, piece = rest.shape[1:]
    count = src_out.shape[0] // rcv_n
    here = lax.axis_index("rcv")
    for j in range(rcv_n):
        value = jnp.zeros((slots, piece), F32)
        for k in range(rcv_n):
            value = value + jnp.where((here + rcv_n - k) % rcv_n == j, rest[k], 0.0)
        for i in range(count):
            for m in range(rcv_n):
                row = i * (slots // count) + m
                src_out[j * count + i : j * count + i + 1, m * piece : (m + 1) * piece] = (
                    value[row : row + 1]
                )


def swap(value, slots):
    shape = value.shape
    value = value.reshape(shape[0] // slots, slots, shape[1])
    value = lax.all_to_all(value, AXES, split_axis=0, concat_axis=0, tiled=True)
    return value.reshape(shape)


def local(
    traces,
    trace_source,
    trace_offset,
    trace_slot,
    request_list,
    source_terms,
    receiver_terms,
    offset_terms,
):
    src_n = lax.axis_size("src")
    rcv_n = lax.axis_size("rcv")
    peers = src_n * rcv_n
    slots = request_list.shape[2]
    num_tr, samples = traces.shape
    owned, freq = receiver_terms.shape
    num_src = source_terms.shape[0]
    num_off = offset_terms.shape[0]
    num_slot = peers * slots
    joint = joint_rows(num_off, num_src)
    rows = num_slot + joint
    half = freq // 2
    edge = half // 2
    rest = half - edge
    piece = freq // rcv_n
    off_rows = max(1, num_off // peers)
    tile = min(512, num_tr)
    assert slots == num_src and off_rows * rcv_n <= slots and num_off + num_src + 3 <= LANES
    assert samples == 2 * freq and freq % (4 * LANES) == 0 and owned <= 256
    assert rcv_n % 2 == 0 and piece == 2 * LANES and edge == rest
    ids = [v.reshape(1, num_tr) for v in (trace_slot, trace_offset, trace_source)]
    lists = jnp.swapaxes(request_list, 1, 2).reshape(slots, peers)
    vmem = pl.BlockSpec(memory_space=pltpu.VMEM)
    hbm = pl.BlockSpec(memory_space=pltpu.HBM)
    anywhere = pl.BlockSpec(memory_space=pl.ANY)

    def static(kernel, *args):
        return lambda *refs: kernel(*args, *refs)

    def shape(*dims):
        return jax.ShapeDtypeStruct(dims, F32)

    def spectra(head, width, counts, joint0):
        lead = not head
        first = 0 if lead else half - width
        consts = [jnp.asarray(v) for v in twiddles(samples, first, first + width)]
        return pl.pallas_call(
            static(spectra_kernel, num_off, num_src, rcv_n, head, lead, tile),
            out_shape=(
                shape(num_slot, 2 * width + (2 * LANES if head else piece)),
                shape(joint, 2 * width) if head else shape(joint + owned, half),
                shape(rows, LANES) if head else shape(joint + owned, half),
            ),
            in_specs=[hbm] * 13,
            out_specs=(hbm, hbm, hbm),
            scratch_shapes=[
                pltpu.VMEM((joint, half), F32),
                pltpu.VMEM((2, joint + owned, half), F32),
                pltpu.VMEM((num_tr, samples), BF16),
                pltpu.VMEM((3, 1, num_tr), jnp.int32),
                pltpu.VMEM((slots, peers), jnp.int32),
                pltpu.VMEM((LANES, freq), F32),
                pltpu.VMEM((owned, freq), F32),
                pltpu.VMEM((rows, LANES), F32),
                pltpu.VMEM((num_slot, 2 * LANES), F32),
                pltpu.VMEM(consts[0].shape, F32),
                pltpu.VMEM(consts[1].shape, F32),
                pltpu.VMEM(consts[2].shape, F32),
                pltpu.VMEM((2, freq, 2 * width), BF16),
                pltpu.VMEM((rows, num_tr), BF16),
                pltpu.VMEM((rows, 2 * width), F32),
                pltpu.VMEM((rows, 2 * width), F32),
                pltpu.VMEM((2, tile, 4 * width), F32),
                pltpu.SemaphoreType.DMA((11,)),
                pltpu.SemaphoreType.DMA((num_tr // tile,)),
            ],
            compiler_params=pltpu.CompilerParams(vmem_limit_bytes=56 * 2**20),
            name="spectra%d" % head,
        )(traces, *ids, lists, offset_terms, source_terms, receiver_terms, counts, joint0, *consts)

    pay, joint0, counts = spectra(True, edge, offset_terms, source_terms)
    got = swap(pay, slots)
    sent = got[:, 2 * edge :]
    pay, keep, mate = spectra(False, rest, counts, joint0)
    mate = lax.ppermute(mate, "rcv", [(j, j ^ 1) for j in range(rcv_n)])
    pair = jnp.concatenate([keep[:joint] + mate[:joint], keep[joint:], mate[joint:]], axis=0)
    pay = pl.pallas_call(
        static(pack_kernel, num_off, num_src, slots, src_n, rcv_n),
        out_shape=shape(*pay.shape),
        in_specs=[anywhere, hbm, hbm],
        out_specs=hbm,
        scratch_shapes=[
            pltpu.VMEM((num_slot, 2 * LANES), F32),
            pltpu.VMEM((joint + 2 * owned, half), F32),
            pltpu.VMEM((2, num_slot, LANES), F32),
            pltpu.SemaphoreType.DMA((2,)),
        ],
        input_output_aliases={2: 0},
        name="pack",
    )(sent, pair, pay)
    sums = swap(pay, slots)

    off_new, src_new = pl.pallas_call(
        static(shares_kernel, num_off, num_src, slots, 2 * edge),
        out_shape=(shape(num_slot, piece), shape(slots, piece)),
        in_specs=[anywhere, anywhere, hbm, hbm],
        out_specs=(vmem, vmem),
        scratch_shapes=[
            pltpu.VMEM((num_slot, LANES), F32),
            pltpu.VMEM((num_slot, piece), F32),
            pltpu.VMEM((num_off, freq), F32),
            pltpu.VMEM((num_src, freq), F32),
            pltpu.VMEM((slots, 2 * piece), F32),
            pltpu.VMEM((slots, 2 * piece), F32),
            pltpu.SemaphoreType.DMA((4,)),
        ],
        name="shares",
    )(sent, sums, offset_terms, source_terms)
    every = swap(off_new, slots)
    parts = [src_new]
    for k in range(1, rcv_n):
        ring = [(j, (j + k) % rcv_n) for j in range(rcv_n)]
        parts.append(lax.ppermute(src_new, "rcv", ring))
    receiver_new = pl.pallas_call(
        static(receiver_kernel, num_off, num_src),
        out_shape=shape(owned, freq),
        in_specs=[anywhere, anywhere, hbm],
        out_specs=vmem,
        scratch_shapes=[
            pltpu.VMEM((num_slot, 2 * edge + LANES), F32),
            pltpu.VMEM((num_slot, 2 * rest), F32),
            pltpu.VMEM((owned, freq), F32),
            pltpu.SemaphoreType.DMA((3,)),
        ],
        name="receiver",
    )(got, sums, receiver_terms)
    source_new = pl.pallas_call(
        static(source_kernel, rcv_n),
        out_shape=shape(num_src, freq),
        in_specs=[anywhere] * rcv_n,
        out_specs=vmem,
        scratch_shapes=[
            pltpu.VMEM((rcv_n, slots, piece), F32),
            pltpu.SemaphoreType.DMA((rcv_n,)),
        ],
        name="source",
    )(*parts)
    every = every.reshape(peers, off_rows, slots // off_rows, piece)[:, :, :rcv_n]
    offset_new = every.reshape(peers * off_rows, freq)[:num_off]
    return (source_new, receiver_new, offset_new)


def solution(mesh):
    return jax.shard_map(
        local,
        mesh=mesh,
        in_specs=(
            P(AXES, None),
            P(AXES),
            P(AXES),
            P(AXES),
            P(AXES, None, None),
            P("src", None),
            P(AXES, None),
            P(),
        ),
        out_specs=(P("src", None), P(AXES, None), P()),
        check_vma=False,
    )
```

```python
import math

import jax
import jax.numpy as jnp
import numpy as np
from jax import lax
from jax.experimental import pallas as pl
from jax.experimental.pallas import tpu as pltpu
from jax.sharding import PartitionSpec as P

AXES = ("src", "rcv")
LANES = 128
F32 = jnp.float32
BF16 = jnp.bfloat16
NT = (((1,), (1,)), ((), ()))
TN = (((0,), (0,)), ((), ()))
NN = (((1,), (0,)), ((), ()))


def twiddles(samples, first, last):
    half = samples // 2
    quarter = samples // 4
    lane = np.arange(LANES)
    even = np.where(lane % 2 == 0, lane, half - 1 + lane)
    odd = np.where(lane % 2 == 1, lane, half - 1 + lane + np.where(lane == 0, LANES, 0))
    freq = np.arange(quarter)
    groups = half // LANES
    unit = 2.0 * math.pi / samples
    base = []
    taper = []
    for rows, fold in ((even, -np.cos(even * quarter * unit)), (odd, np.sin(odd * quarter * unit))):
        phase = (rows[:, None] * freq[None, :] % samples) * unit
        sine = np.sin(phase)
        sine[:, 0] = np.round(fold)
        base += [np.cos(phase), sine]
        at = rows[:, None] + LANES * np.arange(groups)[None, :]
        taper.append((0.5 - 0.5 * np.cos((at + 0.5) * unit)) / math.sqrt(samples))
    turn = (LANES * np.arange(groups)[:, None] * freq[None, :] % samples) * unit
    turn = np.stack([np.cos(turn), np.sin(turn)])
    return (
        np.stack(base)[:, :, first:last].astype(np.float32),
        turn[:, :, first:last].astype(np.float32),
        np.stack(taper).astype(np.float32),
    )


def dot(a, b, dims=NN):
    return lax.dot_general(a, b, dims, preferred_element_type=F32)


def exact(a, b, dims=NN):
    return lax.dot_general(
        a, b, dims, precision=lax.Precision.HIGHEST, preferred_element_type=F32
    )


def pieces(value):
    one = value.astype(BF16)
    rest = value - one.astype(F32)
    two = rest.astype(BF16)
    return one, two, (rest - two.astype(F32)).astype(BF16)


def count_dot(counts, terms):
    counts = jnp.concatenate(halves(counts), axis=1)
    one, two, three = (jnp.concatenate([v, v], axis=0) for v in pieces(terms))
    return dot(counts, one) + dot(counts, two) + dot(counts, three)


def halves(counts):
    upper = counts.astype(BF16)
    return upper, (counts - upper.astype(F32)).astype(BF16)


def count_dot_tn(counts, terms):
    counts = jnp.concatenate(halves(counts), axis=0)
    one, two, three = (jnp.concatenate([v, v], axis=0) for v in pieces(terms))
    return dot(counts, one, TN) + dot(counts, two, TN) + dot(counts, three, TN)


def chosen_sum(chosen, value):
    one, two, three = pieces(value)
    return dot(chosen, one, TN) + dot(chosen, two, TN) + dot(chosen, three, TN)


def iota(shape, axis):
    return lax.broadcasted_iota(jnp.int32, shape, axis)


def hot(mask):
    return jnp.where(mask, 1.0, 0.0).astype(F32)


def ascend(value, lead):
    width = value.shape[1]
    row = iota((width, width), 0)
    col = iota((width, width), 1)
    if lead:
        pick = row == jnp.where(col == 0, 0, width - col)
    else:
        pick = row == width - 1 - col
    pick = hot(pick).astype(BF16)
    one, two, three = pieces(value)
    return dot(one, pick) + dot(two, pick) + dot(three, pick)


def join(low0, high0, low1, high1):
    edge = high1.shape[1]
    whole = jnp.concatenate([high1, high0], axis=1)
    col = iota(whole.shape, 1)
    shifted = pltpu.roll(whole, 1, 1)
    high = jnp.where(col <= edge, shifted, whole)
    high = jnp.where(col == 0, high0[:, :1], high)
    return jnp.concatenate([low0, low1, high], axis=1)


def part_of(value, first, width):
    half = value.shape[1] // 2
    high = value[:, half:]
    if first == 0:
        tail = high[:, half - width :]
        tail = jnp.where(iota(tail.shape, 1) == 0, high[:, :1], tail)
    else:
        tail = pltpu.roll(high, half - 1, 1)[:, :width]
    return jnp.concatenate([value[:, first : first + width], tail], axis=1)


def joint_rows(num_off, num_src):
    return -(-(num_off + num_src) // 16) * 16


def start(copies):
    for copy in copies:
        copy.start()


def wait(copies):
    for copy in copies:
        copy.wait()


def build_table(base, turn, taper, table):
    groups = taper.shape[2]
    width = base.shape[2]
    for side in range(2):
        for g in range(groups):
            cos0 = base[2 * side]
            sin0 = base[2 * side + 1]
            cos1 = turn[0, g : g + 1, :]
            sin1 = turn[1, g : g + 1, :]
            scale = taper[side, :, g : g + 1]
            at = slice(g * LANES, (g + 1) * LANES)
            table[side, at, :width] = ((cos0 * cos1 - sin0 * sin1) * scale).astype(BF16)
            table[side, at, width:] = ((sin0 * cos1 + cos0 * sin1) * -scale).astype(BF16)


def ident_rows(num_slot, num_off, rows, slot, off, src):
    top = iota((num_slot, slot.shape[1]), 0) == slot
    low = iota((rows - num_slot, slot.shape[1]), 0)
    low = (low == off) | (low == src + num_off)
    return jnp.concatenate([hot(top).astype(BF16), hot(low).astype(BF16)], axis=0)


def spectra_kernel(
    num_off, num_src, rcv_n, head, lead, tile,
    x_hbm, slot_hbm, off_hbm, src_hbm, lists_hbm, offset_hbm, source_hbm, own_hbm,
    counts_hbm, joint0_hbm, base_hbm, turn_hbm, taper_hbm, pay_hbm, joint_hbm, extra_hbm,
    joint0, swapped, x, ids, lists, terms, own, counts, extra, base, turn, taper, table, every, total, stage, spectrum, sems, x_sems,
):
    slots, peers = lists.shape
    num_slot = peers * slots
    rows = total.shape[0]
    width = base.shape[2]
    half = x.shape[1] // 2
    first = 0 if lead else width
    group = lax.axis_index("src")
    near = [
        pltpu.make_async_copy(base_hbm, base, sems.at[0]),
        pltpu.make_async_copy(turn_hbm, turn, sems.at[1]),
        pltpu.make_async_copy(taper_hbm, taper, sems.at[2]),
    ]
    far = [
        pltpu.make_async_copy(slot_hbm, ids.at[0], sems.at[3]),
        pltpu.make_async_copy(off_hbm, ids.at[1], sems.at[4]),
        pltpu.make_async_copy(src_hbm, ids.at[2], sems.at[5]),
        pltpu.make_async_copy(offset_hbm, terms.at[0:num_off], sems.at[6]),
        pltpu.make_async_copy(source_hbm, terms.at[num_off : num_off + num_src], sems.at[7]),
    ]
    if head:
        far.append(pltpu.make_async_copy(lists_hbm, lists, sems.at[8]))
    else:
        far.append(pltpu.make_async_copy(own_hbm, own, sems.at[8]))
        far.append(pltpu.make_async_copy(counts_hbm, counts, sems.at[9]))
        far.append(pltpu.make_async_copy(joint0_hbm, joint0, sems.at[10]))
    tiles = [
        pltpu.make_async_copy(
            x_hbm.at[t * tile : (t + 1) * tile], x.at[t * tile : (t + 1) * tile], x_sems.at[t]
        )
        for t in range(x.shape[0] // tile)
    ]
    start(far + near)
    spare = num_off + num_src
    terms[spare:, :] = jnp.zeros((terms.shape[0] - spare, terms.shape[1]), F32)
    total[...] = jnp.zeros_like(total)
    wait(far + near)
    start(tiles)
    src = ids[2] - group * num_src
    every[...] = ident_rows(num_slot, num_off, rows, ids[0], ids[1], src)
    last = []
    if head:
        at = iota((LANES, x.shape[0]), 0)
        joint = hot((at == ids[1]) | (at == src + num_off)).astype(BF16)
        counts[...] = dot(every[...], joint, NT)
        part = counts[:num_slot]
        whole = jnp.sum(part, axis=0, keepdims=True)
        row = iota((num_slot, LANES), 0)
        col = iota((num_slot, LANES), 1)
        peer = row // slots
        inner = row % slots
        off_rows = max(1, num_off // peers)
        src_rows = num_src // rcv_n
        is_off = (col == peer * off_rows + inner) & (inner < off_rows) & (col < num_off)
        is_src = (col == num_off + peer % rcv_n * src_rows + inner) & (inner < src_rows)
        is_src = is_src & (peer // rcv_n == group)
        num_o = jnp.sum(jnp.where(is_off, whole, 0.0), axis=1, keepdims=True)
        num_s = jnp.sum(jnp.where(is_src, whole, 0.0), axis=1, keepdims=True)
        spread = hot(iota((num_slot, peers), 0) // slots == iota((num_slot, peers), 1))
        listed = dot(spread.astype(BF16), lists[...].astype(F32).astype(BF16), NT)
        mine = iota((num_slot, slots), 0) % slots == iota((num_slot, slots), 1)
        asked = jnp.sum(jnp.where(mine, listed, 0.0), axis=1, keepdims=True)
        part = jnp.where(col == spare, asked, part)
        part = jnp.where(col == spare + 1, num_o, part)
        extra[:, :LANES] = jnp.where(col == spare + 2, num_s, part)
        for p in range(peers):
            mate = p ^ 1
            extra[p * slots : (p + 1) * slots, LANES:] = extra[
                mate * slots : (mate + 1) * slots, :LANES
            ]
        last.append(pltpu.make_async_copy(extra, pay_hbm.at[:, 2 * width :], sems.at[6]))
        last.append(pltpu.make_async_copy(counts, extra_hbm, sems.at[7]))
    else:
        kept = own[...]
        own[:, : 2 * width] = part_of(kept, width, width)
        own[:, 2 * width :] = part_of(kept, 0, width)
    start(last)
    stage[...] = count_dot(counts[...], part_of(terms[...], first, width))
    build_table(base, turn, taper, table)

    def transform(t):
        tiles[t].wait()
        lane = iota((tile, LANES), 1) % 2 == 0
        even = []
        odd = []
        for g in range(half // LANES):
            front = x[t * tile : (t + 1) * tile, g * LANES : (g + 1) * LANES]
            back = x[t * tile : (t + 1) * tile, half + g * LANES : half + (g + 1) * LANES]
            back = pltpu.roll(back, 1, 1)
            even.append(jnp.where(lane, front, back))
            odd.append(jnp.where(lane, back, front))
        spectrum[t % 2, :, : 2 * width] = dot(jnp.concatenate(even, axis=1), table[0])
        spectrum[t % 2, :, 2 * width :] = dot(jnp.concatenate(odd, axis=1), table[1])

    def collect(t):
        ec, es, oc, os = (
            spectrum[t % 2, :, k * width : (k + 1) * width] for k in range(4)
        )
        re_low, im_low = ec + oc, es + os
        re_high, im_high = ec - oc, es - os
        if lead:
            zero = iota((tile, width), 1) == 0
            im_low = jnp.where(zero, 0.0, im_low)
            re_high = jnp.where(zero, es, re_high)
            im_high = jnp.where(zero, os, im_high)
        power = jnp.concatenate(
            [re_low * re_low + im_low * im_low, re_high * re_high + im_high * im_high], axis=1
        )
        amp = 0.5 * jnp.log(power + 0.01)
        upper = amp.astype(BF16)
        lower = (amp - upper.astype(F32)).astype(BF16)
        ids_t = every[:, t * tile : (t + 1) * tile]
        total[...] += dot(ids_t, upper) + dot(ids_t, lower)

    transform(0)
    for t in range(1, len(tiles)):
        transform(t)
        collect(t - 1)
    collect(len(tiles) - 1)
    stage[:, :width] = total[:, :width] - stage[:, :width]
    stage[:, width:] = ascend(total[:, width:], lead) - stage[:, width:]
    out = [pltpu.make_async_copy(stage.at[:num_slot], pay_hbm.at[:, : 2 * width], sems.at[0])]
    if head:
        out.append(pltpu.make_async_copy(stage.at[num_slot:], joint_hbm, sems.at[1]))
    else:
        odd = lax.axis_index("rcv") % 2 == 1
        cut = rows - num_slot
        for m in range(2 * width // LANES):
            lo, hi = 2 * m * LANES, (2 * m + 1) * LANES
            if hi < 2 * width:
                sums = joint0[:, lo:hi], joint0[:, hi : hi + LANES]
            else:
                lo, hi = lo - 2 * width, hi - 2 * width
                sums = stage[num_slot:, lo:hi], stage[num_slot:, hi : hi + LANES]
            both = own[:, 2 * m * LANES : (2 * m + 1) * LANES], own[:, (2 * m + 1) * LANES : (2 * m + 2) * LANES]
            at = slice(m * LANES, (m + 1) * LANES)
            swapped[0, :cut, at] = jnp.where(odd, sums[1], sums[0])
            swapped[1, :cut, at] = jnp.where(odd, sums[0], sums[1])
            swapped[0, cut:, at] = jnp.where(odd, both[1], both[0])
            swapped[1, cut:, at] = jnp.where(odd, both[0], both[1])
        out.append(pltpu.make_async_copy(swapped.at[0], joint_hbm, sems.at[1]))
        out.append(pltpu.make_async_copy(swapped.at[1], extra_hbm, sems.at[2]))
    start(out)
    wait(last + out)


def owner_hot(sent, base, owned):
    col = iota(sent.shape, 1)
    asked = jnp.sum(jnp.where(col == base, sent, 0.0), axis=1, keepdims=True).astype(jnp.int32)
    return hot(iota((sent.shape[0], owned), 1) == asked)


def pack_kernel(
    num_off, num_src, slots, src_n, rcv_n, sent_hbm, pair_hbm, _, out_hbm,
    sent, pair, out, sems,
):
    half = pair.shape[1]
    cut = joint_rows(num_off, num_src)
    owned = (pair.shape[0] - cut) // 2
    copies = [
        pltpu.make_async_copy(sent_hbm, sent, sems.at[0]),
        pltpu.make_async_copy(pair_hbm, pair, sems.at[1]),
    ]
    start(copies)
    copies[0].wait()
    num = sent.shape[0]
    group = lax.axis_index("src")
    every_src = src_n * num_src
    col = iota((LANES, every_src), 0)
    pick = hot(col == num_off + iota((LANES, every_src), 1) % num_src).astype(BF16)
    from_group = iota((num, every_src), 0) // (slots * rcv_n)
    from_group = from_group == iota((num, every_src), 1) // num_src
    off_of = []
    src_of = []
    for k in range(2):
        part = sent[:, k * LANES : (k + 1) * LANES]
        chosen = owner_hot(part, num_off + num_src, owned).astype(BF16)
        upper, lower = halves(part)
        by_src = [jnp.where(from_group, dot(v, pick), 0.0).astype(BF16) for v in (upper, lower)]
        off_of.append((dot(chosen, upper, TN) + dot(chosen, lower, TN))[:, :num_off])
        src_of.append(dot(chosen, by_src[0], TN) + dot(chosen, by_src[1], TN))
    wait(copies[1:])
    terms = pair[cut:, :]
    sums = pair[:cut, :]
    off_sum = sums[:num_off] - count_dot_tn(jnp.concatenate(off_of, axis=0), terms)
    src_sum = -count_dot_tn(jnp.concatenate(src_of, axis=0), terms)
    mine = sums[num_off : num_off + num_src]
    per_off = slots // max(1, num_off // (src_n * rcv_n))
    per_src = slots // (num_src // rcv_n)
    if num_off * per_off < num or per_off > rcv_n:
        out[...] = jnp.zeros_like(out)
    copies = [
        pltpu.make_async_copy(
            out.at[h], out_hbm.at[:, half + h * LANES : half + (h + 1) * LANES], sems.at[h]
        )
        for h in range(2)
    ]
    for m in range(rcv_n):
        at = slice(m * LANES, (m + 1) * LANES)
        out[0, pl.ds(m, num_off, stride=per_off), :] = off_sum[:, at]
    copies[0].start()
    for m in range(rcv_n):
        at = slice(m * LANES, (m + 1) * LANES)
        for i in range(src_n):
            to = pl.ds(i * num_src * per_src + m, num_src, stride=per_src)
            source = src_sum[i * num_src : (i + 1) * num_src, at]
            out[1, to, :] = source + jnp.where(group == i, mine[:, at], 0.0)
    copies[1].start()
    wait(copies)


def shares_kernel(
    num_off, num_src, slots, edge, got_hbm, sums_hbm, offset_hbm, source_hbm,
    off_out, src_out, sent, tail, offset, source, rows, block, sems,
):
    rcv_n = lax.axis_size("rcv")
    piece = src_out.shape[1]
    rest = sums_hbm.shape[1] - piece
    copies = [
        pltpu.make_async_copy(got_hbm.at[:, :LANES], sent, sems.at[0]),
        pltpu.make_async_copy(sums_hbm.at[:, rest:], tail, sems.at[1]),
        pltpu.make_async_copy(offset_hbm, offset, sems.at[2]),
        pltpu.make_async_copy(source_hbm, source, sems.at[3]),
    ]
    start(copies)
    wait(copies)
    peers = sent.shape[0] // slots
    base = num_off + num_src
    both = sent[0:slots]
    for d in range(1, peers):
        both = both + sent[d * slots : (d + 1) * slots]
    for k in range(2):
        value = tail[k * slots : (k + 1) * slots]
        for d in range(k + 2, peers, 2):
            value = value + tail[d * slots : (d + 1) * slots]
        rows[:, k * LANES : (k + 1) * LANES] = value[:, :LANES]
        rows[:, piece + k * LANES : piece + (k + 1) * LANES] = value[:, LANES:]
    col = iota(both.shape, 1)
    num_o = jnp.sum(jnp.where(col == base + 1, both, 0.0), axis=1, keepdims=True)
    num_s = jnp.sum(jnp.where(col == base + 2, both, 0.0), axis=1, keepdims=True)
    here = lax.axis_index("rcv")
    off_rows = max(1, num_off // peers)
    src_rows = num_src // rcv_n
    at_off = (lax.axis_index("src") * rcv_n + here) * off_rows
    for count, num, at, first, terms in (
        (off_rows, num_o, slice(0, piece), at_off, offset),
        (src_rows, num_s, slice(piece, 2 * piece), here * src_rows, source),
    ):
        last = terms.shape[0] - 1
        parts = [
            jnp.concatenate(
                [rows[j * (slots // count) + m : j * (slots // count) + m + 1, at] for j in range(count)],
                axis=0,
            )
            for m in range(rcv_n)
        ]
        whole = jnp.concatenate(parts, axis=1)
        e, r = edge // 2, (whole.shape[1] - edge) // 2
        whole = join(
            whole[:, edge : edge + r], whole[:, edge + r :], whole[:, :e], whole[:, e:edge]
        )
        old = jnp.concatenate(
            [terms[pl.ds(jnp.minimum(first + j, last), 1), :] for j in range(count)], axis=0
        )
        new = old + whole / (num[:count] + 1.0)
        block[:, at] = jnp.zeros((slots, piece), F32)
        for j in range(count):
            for m in range(rcv_n):
                to = j * (slots // count) + m
                block[to : to + 1, at] = new[j : j + 1, m * piece : (m + 1) * piece]
    src_out[...] = block[:, piece:]
    done = block[:, :piece]
    for d in range(peers):
        off_out[d * slots : (d + 1) * slots, :] = done


def receiver_kernel(num_off, num_src, got_hbm, sums_hbm, terms_hbm, out, got, sums, terms, sems):
    edge = got.shape[1] - LANES
    rest = sums.shape[1]
    copies = [
        pltpu.make_async_copy(got_hbm.at[:, : edge + LANES], got, sems.at[0]),
        pltpu.make_async_copy(sums_hbm.at[:, :rest], sums, sems.at[1]),
        pltpu.make_async_copy(terms_hbm, terms, sems.at[2]),
    ]
    start(copies)
    wait(copies)
    sent = got[:, edge:]
    value = terms[...]
    chosen = owner_hot(sent, num_off + num_src, value.shape[0]).astype(BF16)
    per_slot = jnp.where(iota(sent.shape, 1) < num_off, sent, 0.0)
    num = jnp.sum(chosen_sum(chosen, per_slot), axis=1, keepdims=True)
    one = chosen_sum(chosen, got[:, :edge])
    two = chosen_sum(chosen, sums[...])
    edge //= 2
    rest //= 2
    total = join(two[:, :rest], two[:, rest:], one[:, :edge], one[:, edge:])
    out[...] = value + (total - num * value) / (num + 1.0)


def source_kernel(rcv_n, *refs):
    src_out, rest, sems = refs[rcv_n:]
    copies = [pltpu.make_async_copy(refs[k], rest.at[k], sems.at[k]) for k in range(rcv_n)]
    start(copies)
    wait(copies)
    slots, piece = rest.shape[1:]
    count = src_out.shape[0] // rcv_n
    here = lax.axis_index("rcv")
    for j in range(rcv_n):
        value = jnp.zeros((slots, piece), F32)
        for k in range(rcv_n):
            value = value + jnp.where((here + rcv_n - k) % rcv_n == j, rest[k], 0.0)
        for i in range(count):
            for m in range(rcv_n):
                row = i * (slots // count) + m
                src_out[j * count + i : j * count + i + 1, m * piece : (m + 1) * piece] = (
                    value[row : row + 1]
                )


def swap(value, slots):
    shape = value.shape
    value = value.reshape(shape[0] // slots, slots, shape[1])
    value = lax.all_to_all(value, AXES, split_axis=0, concat_axis=0, tiled=True)
    return value.reshape(shape)


def local(
    traces,
    trace_source,
    trace_offset,
    trace_slot,
    request_list,
    source_terms,
    receiver_terms,
    offset_terms,
):
    src_n = lax.axis_size("src")
    rcv_n = lax.axis_size("rcv")
    peers = src_n * rcv_n
    slots = request_list.shape[2]
    num_tr, samples = traces.shape
    owned, freq = receiver_terms.shape
    num_src = source_terms.shape[0]
    num_off = offset_terms.shape[0]
    num_slot = peers * slots
    joint = joint_rows(num_off, num_src)
    rows = num_slot + joint
    half = freq // 2
    edge = half // 2
    rest = half - edge
    piece = freq // rcv_n
    off_rows = max(1, num_off // peers)
    tile = min(1024, num_tr)
    assert slots == num_src and off_rows * rcv_n <= slots and num_off + num_src + 3 <= LANES
    assert samples == 2 * freq and freq % (4 * LANES) == 0 and owned <= 256
    assert rcv_n % 2 == 0 and piece == 2 * LANES and edge == rest
    ids = [v.reshape(1, num_tr) for v in (trace_slot, trace_offset, trace_source)]
    lists = jnp.swapaxes(request_list, 1, 2).reshape(slots, peers)
    vmem = pl.BlockSpec(memory_space=pltpu.VMEM)
    hbm = pl.BlockSpec(memory_space=pltpu.HBM)
    anywhere = pl.BlockSpec(memory_space=pl.ANY)

    def static(kernel, *args):
        return lambda *refs: kernel(*args, *refs)

    def shape(*dims):
        return jax.ShapeDtypeStruct(dims, F32)

    def spectra(head, width, counts, joint0):
        lead = not head
        first = 0 if lead else half - width
        consts = [jnp.asarray(v) for v in twiddles(samples, first, first + width)]
        return pl.pallas_call(
            static(spectra_kernel, num_off, num_src, rcv_n, head, lead, tile),
            out_shape=(
                shape(num_slot, 2 * width + (2 * LANES if head else piece)),
                shape(joint, 2 * width) if head else shape(joint + owned, half),
                shape(rows, LANES) if head else shape(joint + owned, half),
            ),
            in_specs=[hbm] * 13,
            out_specs=(hbm, hbm, hbm),
            scratch_shapes=[
                pltpu.VMEM((joint, half), F32),
                pltpu.VMEM((2, joint + owned, half), F32),
                pltpu.VMEM((num_tr, samples), BF16),
                pltpu.VMEM((3, 1, num_tr), jnp.int32),
                pltpu.VMEM((slots, peers), jnp.int32),
                pltpu.VMEM((LANES, freq), F32),
                pltpu.VMEM((owned, freq), F32),
                pltpu.VMEM((rows, LANES), F32),
                pltpu.VMEM((num_slot, 2 * LANES), F32),
                pltpu.VMEM(consts[0].shape, F32),
                pltpu.VMEM(consts[1].shape, F32),
                pltpu.VMEM(consts[2].shape, F32),
                pltpu.VMEM((2, freq, 2 * width), BF16),
                pltpu.VMEM((rows, num_tr), BF16),
                pltpu.VMEM((rows, 2 * width), F32),
                pltpu.VMEM((rows, 2 * width), F32),
                pltpu.VMEM((2, tile, 4 * width), F32),
                pltpu.SemaphoreType.DMA((11,)),
                pltpu.SemaphoreType.DMA((num_tr // tile,)),
            ],
            compiler_params=pltpu.CompilerParams(vmem_limit_bytes=56 * 2**20),
            name="spectra%d" % head,
        )(traces, *ids, lists, offset_terms, source_terms, receiver_terms, counts, joint0, *consts)

    pay, joint0, counts = spectra(True, edge, offset_terms, source_terms)
    got = swap(pay, slots)
    sent = got[:, 2 * edge :]
    pay, keep, mate = spectra(False, rest, counts, joint0)
    mate = lax.ppermute(mate, "rcv", [(j, j ^ 1) for j in range(rcv_n)])
    pair = jnp.concatenate([keep[:joint] + mate[:joint], keep[joint:], mate[joint:]], axis=0)
    pay = pl.pallas_call(
        static(pack_kernel, num_off, num_src, slots, src_n, rcv_n),
        out_shape=shape(*pay.shape),
        in_specs=[anywhere, hbm, hbm],
        out_specs=hbm,
        scratch_shapes=[
            pltpu.VMEM((num_slot, 2 * LANES), F32),
            pltpu.VMEM((joint + 2 * owned, half), F32),
            pltpu.VMEM((2, num_slot, LANES), F32),
            pltpu.SemaphoreType.DMA((2,)),
        ],
        input_output_aliases={2: 0},
        name="pack",
    )(sent, pair, pay)
    sums = swap(pay, slots)

    off_new, src_new = pl.pallas_call(
        static(shares_kernel, num_off, num_src, slots, 2 * edge),
        out_shape=(shape(num_slot, piece), shape(slots, piece)),
        in_specs=[anywhere, anywhere, hbm, hbm],
        out_specs=(vmem, vmem),
        scratch_shapes=[
            pltpu.VMEM((num_slot, LANES), F32),
            pltpu.VMEM((num_slot, piece), F32),
            pltpu.VMEM((num_off, freq), F32),
            pltpu.VMEM((num_src, freq), F32),
            pltpu.VMEM((slots, 2 * piece), F32),
            pltpu.VMEM((slots, 2 * piece), F32),
            pltpu.SemaphoreType.DMA((4,)),
        ],
        name="shares",
    )(sent, sums, offset_terms, source_terms)
    every = swap(off_new, slots)
    parts = [src_new]
    for k in range(1, rcv_n):
        ring = [(j, (j + k) % rcv_n) for j in range(rcv_n)]
        parts.append(lax.ppermute(src_new, "rcv", ring))
    receiver_new = pl.pallas_call(
        static(receiver_kernel, num_off, num_src),
        out_shape=shape(owned, freq),
        in_specs=[anywhere, anywhere, hbm],
        out_specs=vmem,
        scratch_shapes=[
            pltpu.VMEM((num_slot, 2 * edge + LANES), F32),
            pltpu.VMEM((num_slot, 2 * rest), F32),
            pltpu.VMEM((owned, freq), F32),
            pltpu.SemaphoreType.DMA((3,)),
        ],
        name="receiver",
    )(got, sums, receiver_terms)
    source_new = pl.pallas_call(
        static(source_kernel, rcv_n),
        out_shape=shape(num_src, freq),
        in_specs=[anywhere] * rcv_n,
        out_specs=vmem,
        scratch_shapes=[
            pltpu.VMEM((rcv_n, slots, piece), F32),
            pltpu.SemaphoreType.DMA((rcv_n,)),
        ],
        name="source",
    )(*parts)
    every = every.reshape(peers, off_rows, slots // off_rows, piece)[:, :, :rcv_n]
    offset_new = every.reshape(peers * off_rows, freq)[:num_off]
    return (source_new, receiver_new, offset_new)


def solution(mesh):
    return jax.shard_map(
        local,
        mesh=mesh,
        in_specs=(
            P(AXES, None),
            P(AXES),
            P(AXES),
            P(AXES),
            P(AXES, None, None),
            P("src", None),
            P(AXES, None),
            P(),
        ),
        out_specs=(P("src", None), P(AXES, None), P()),
        check_vma=False,
    )
```

```python
import math

import jax
import jax.numpy as jnp
import numpy as np
from jax import lax
from jax.experimental import pallas as pl
from jax.experimental.pallas import tpu as pltpu
from jax.sharding import PartitionSpec as P

AXES = ("src", "rcv")
LANES = 128
F32 = jnp.float32
BF16 = jnp.bfloat16
NT = (((1,), (1,)), ((), ()))
TN = (((0,), (0,)), ((), ()))
NN = (((1,), (0,)), ((), ()))


def twiddles(samples, first, last):
    half = samples // 2
    quarter = samples // 4
    lane = np.arange(LANES)
    even = np.where(lane % 2 == 0, lane, half - 1 + lane)
    odd = np.where(lane % 2 == 1, lane, half - 1 + lane + np.where(lane == 0, LANES, 0))
    freq = np.arange(quarter)
    groups = half // LANES
    unit = 2.0 * math.pi / samples
    base = []
    taper = []
    for rows, fold in ((even, -np.cos(even * quarter * unit)), (odd, np.sin(odd * quarter * unit))):
        phase = (rows[:, None] * freq[None, :] % samples) * unit
        sine = np.sin(phase)
        sine[:, 0] = np.round(fold)
        base += [np.cos(phase), sine]
        at = rows[:, None] + LANES * np.arange(groups)[None, :]
        taper.append((0.5 - 0.5 * np.cos((at + 0.5) * unit)) / math.sqrt(samples))
    turn = (LANES * np.arange(groups)[:, None] * freq[None, :] % samples) * unit
    turn = np.stack([np.cos(turn), np.sin(turn)])
    return (
        np.stack(base)[:, :, first:last].astype(np.float32),
        turn[:, :, first:last].astype(np.float32),
        np.stack(taper).astype(np.float32),
    )


def dot(a, b, dims=NN):
    return lax.dot_general(a, b, dims, preferred_element_type=F32)


def exact(a, b, dims=NN):
    return lax.dot_general(
        a, b, dims, precision=lax.Precision.HIGHEST, preferred_element_type=F32
    )


def pieces(value):
    one = value.astype(BF16)
    rest = value - one.astype(F32)
    two = rest.astype(BF16)
    return one, two, (rest - two.astype(F32)).astype(BF16)


def count_dot(counts, terms):
    counts = jnp.concatenate(halves(counts), axis=1)
    one, two, three = (jnp.concatenate([v, v], axis=0) for v in pieces(terms))
    return dot(counts, one) + dot(counts, two) + dot(counts, three)


def halves(counts):
    upper = counts.astype(BF16)
    return upper, (counts - upper.astype(F32)).astype(BF16)


def count_dot_tn(counts, terms):
    counts = jnp.concatenate(halves(counts), axis=0)
    one, two, three = (jnp.concatenate([v, v], axis=0) for v in pieces(terms))
    return dot(counts, one, TN) + dot(counts, two, TN) + dot(counts, three, TN)


def chosen_sum(chosen, value):
    one, two, three = pieces(value)
    return dot(chosen, one, TN) + dot(chosen, two, TN) + dot(chosen, three, TN)


def iota(shape, axis):
    return lax.broadcasted_iota(jnp.int32, shape, axis)


def hot(mask):
    return jnp.where(mask, 1.0, 0.0).astype(F32)


def ascend(value, lead):
    width = value.shape[1]
    row = iota((width, width), 0)
    col = iota((width, width), 1)
    if lead:
        pick = row == jnp.where(col == 0, 0, width - col)
    else:
        pick = row == width - 1 - col
    pick = hot(pick).astype(BF16)
    one, two, three = pieces(value)
    return dot(one, pick) + dot(two, pick) + dot(three, pick)


def join(low0, high0, low1, high1):
    edge = high1.shape[1]
    whole = jnp.concatenate([high1, high0], axis=1)
    col = iota(whole.shape, 1)
    shifted = pltpu.roll(whole, 1, 1)
    high = jnp.where(col <= edge, shifted, whole)
    high = jnp.where(col == 0, high0[:, :1], high)
    return jnp.concatenate([low0, low1, high], axis=1)


def part_of(value, first, width):
    half = value.shape[1] // 2
    high = value[:, half:]
    if first == 0:
        tail = high[:, half - width :]
        tail = jnp.where(iota(tail.shape, 1) == 0, high[:, :1], tail)
    else:
        tail = pltpu.roll(high, half - 1, 1)[:, :width]
    return jnp.concatenate([value[:, first : first + width], tail], axis=1)


def joint_rows(num_off, num_src):
    return -(-(num_off + num_src) // 16) * 16


def start(copies):
    for copy in copies:
        copy.start()


def wait(copies):
    for copy in copies:
        copy.wait()


def build_table(base, turn, taper, table):
    groups = taper.shape[2]
    width = base.shape[2]
    for side in range(2):
        for g in range(groups):
            cos0 = base[2 * side]
            sin0 = base[2 * side + 1]
            cos1 = turn[0, g : g + 1, :]
            sin1 = turn[1, g : g + 1, :]
            scale = taper[side, :, g : g + 1]
            at = slice(g * LANES, (g + 1) * LANES)
            table[side, at, :width] = ((cos0 * cos1 - sin0 * sin1) * scale).astype(BF16)
            table[side, at, width:] = ((sin0 * cos1 + cos0 * sin1) * -scale).astype(BF16)


def ident_rows(num_slot, num_off, rows, slot, off, src):
    top = iota((num_slot, slot.shape[1]), 0) == slot
    low = iota((rows - num_slot, slot.shape[1]), 0)
    low = (low == off) | (low == src + num_off)
    return jnp.concatenate([hot(top).astype(BF16), hot(low).astype(BF16)], axis=0)


def spectra_kernel(
    num_off, num_src, rcv_n, head, lead, tile,
    x_hbm, slot_hbm, off_hbm, src_hbm, lists_hbm, offset_hbm, source_hbm, own_hbm,
    counts_hbm, joint0_hbm, base_hbm, turn_hbm, taper_hbm, pay_hbm, joint_hbm, extra_hbm,
    joint0, swapped, x, ids, lists, terms, own, counts, extra, base, turn, taper, table, every, total, stage, spectrum, sems, x_sems,
):
    slots, peers = lists.shape
    num_slot = peers * slots
    rows = total.shape[0]
    width = base.shape[2]
    half = x.shape[1] // 2
    first = 0 if lead else width
    group = lax.axis_index("src")
    near = [
        pltpu.make_async_copy(base_hbm, base, sems.at[0]),
        pltpu.make_async_copy(turn_hbm, turn, sems.at[1]),
        pltpu.make_async_copy(taper_hbm, taper, sems.at[2]),
    ]
    far = [
        pltpu.make_async_copy(slot_hbm, ids.at[0], sems.at[3]),
        pltpu.make_async_copy(off_hbm, ids.at[1], sems.at[4]),
        pltpu.make_async_copy(src_hbm, ids.at[2], sems.at[5]),
        pltpu.make_async_copy(offset_hbm, terms.at[0:num_off], sems.at[6]),
        pltpu.make_async_copy(source_hbm, terms.at[num_off : num_off + num_src], sems.at[7]),
    ]
    if head:
        far.append(pltpu.make_async_copy(lists_hbm, lists, sems.at[8]))
    else:
        far.append(pltpu.make_async_copy(own_hbm, own, sems.at[8]))
        far.append(pltpu.make_async_copy(counts_hbm, counts, sems.at[9]))
        far.append(pltpu.make_async_copy(joint0_hbm, joint0, sems.at[10]))
    tiles = [
        pltpu.make_async_copy(
            x_hbm.at[t * tile : (t + 1) * tile], x.at[t * tile : (t + 1) * tile], x_sems.at[t]
        )
        for t in range(x.shape[0] // tile)
    ]
    start(far + near)
    spare = num_off + num_src
    terms[spare:, :] = jnp.zeros((terms.shape[0] - spare, terms.shape[1]), F32)
    total[...] = jnp.zeros_like(total)
    wait(far + near)
    start(tiles)
    src = ids[2] - group * num_src
    every[...] = ident_rows(num_slot, num_off, rows, ids[0], ids[1], src)
    last = []
    if head:
        at = iota((LANES, x.shape[0]), 0)
        joint = hot((at == ids[1]) | (at == src + num_off)).astype(BF16)
        counts[...] = dot(every[...], joint, NT)
        part = counts[:num_slot]
        whole = jnp.sum(part, axis=0, keepdims=True)
        row = iota((num_slot, LANES), 0)
        col = iota((num_slot, LANES), 1)
        peer = row // slots
        inner = row % slots
        off_rows = max(1, num_off // peers)
        src_rows = num_src // rcv_n
        is_off = (col == peer * off_rows + inner) & (inner < off_rows) & (col < num_off)
        is_src = (col == num_off + peer % rcv_n * src_rows + inner) & (inner < src_rows)
        is_src = is_src & (peer // rcv_n == group)
        num_o = jnp.sum(jnp.where(is_off, whole, 0.0), axis=1, keepdims=True)
        num_s = jnp.sum(jnp.where(is_src, whole, 0.0), axis=1, keepdims=True)
        spread = hot(iota((num_slot, peers), 0) // slots == iota((num_slot, peers), 1))
        listed = dot(spread.astype(BF16), lists[...].astype(F32).astype(BF16), NT)
        mine = iota((num_slot, slots), 0) % slots == iota((num_slot, slots), 1)
        asked = jnp.sum(jnp.where(mine, listed, 0.0), axis=1, keepdims=True)
        part = jnp.where(col == spare, asked, part)
        part = jnp.where(col == spare + 1, num_o, part)
        extra[:, :LANES] = jnp.where(col == spare + 2, num_s, part)
        for p in range(peers):
            mate = p ^ 1
            extra[p * slots : (p + 1) * slots, LANES:] = extra[
                mate * slots : (mate + 1) * slots, :LANES
            ]
        last.append(pltpu.make_async_copy(extra, pay_hbm.at[:, 2 * width :], sems.at[6]))
        last.append(pltpu.make_async_copy(counts, extra_hbm, sems.at[7]))
    else:
        kept = own[...]
        own[:, : 2 * width] = part_of(kept, width, width)
        own[:, 2 * width :] = part_of(kept, 0, width)
    start(last)
    stage[...] = count_dot(counts[...], part_of(terms[...], first, width))
    build_table(base, turn, taper, table)

    def transform(t):
        tiles[t].wait()
        lane = iota((tile, LANES), 1) % 2 == 0
        even = []
        odd = []
        for g in range(half // LANES):
            front = x[t * tile : (t + 1) * tile, g * LANES : (g + 1) * LANES]
            back = x[t * tile : (t + 1) * tile, half + g * LANES : half + (g + 1) * LANES]
            back = pltpu.roll(back, 1, 1)
            even.append(jnp.where(lane, front, back))
            odd.append(jnp.where(lane, back, front))
        spectrum[t % 2, :, : 2 * width] = dot(jnp.concatenate(even, axis=1), table[0])
        spectrum[t % 2, :, 2 * width :] = dot(jnp.concatenate(odd, axis=1), table[1])

    def collect(t):
        ec, es, oc, os = (
            spectrum[t % 2, :, k * width : (k + 1) * width] for k in range(4)
        )
        re_low, im_low = ec + oc, es + os
        re_high, im_high = ec - oc, es - os
        if lead:
            zero = iota((tile, width), 1) == 0
            im_low = jnp.where(zero, 0.0, im_low)
            re_high = jnp.where(zero, es, re_high)
            im_high = jnp.where(zero, os, im_high)
        power = jnp.concatenate(
            [re_low * re_low + im_low * im_low, re_high * re_high + im_high * im_high], axis=1
        )
        amp = 0.5 * jnp.log(power + 0.01)
        upper = amp.astype(BF16)
        lower = (amp - upper.astype(F32)).astype(BF16)
        ids_t = every[:, t * tile : (t + 1) * tile]
        total[...] += dot(ids_t, upper) + dot(ids_t, lower)

    transform(0)
    for t in range(1, len(tiles)):
        collect(t - 1)
        transform(t)
    collect(len(tiles) - 1)
    stage[:, :width] = total[:, :width] - stage[:, :width]
    stage[:, width:] = ascend(total[:, width:], lead) - stage[:, width:]
    out = [pltpu.make_async_copy(stage.at[:num_slot], pay_hbm.at[:, : 2 * width], sems.at[0])]
    if head:
        out.append(pltpu.make_async_copy(stage.at[num_slot:], joint_hbm, sems.at[1]))
    else:
        odd = lax.axis_index("rcv") % 2 == 1
        cut = rows - num_slot
        for m in range(2 * width // LANES):
            lo, hi = 2 * m * LANES, (2 * m + 1) * LANES
            if hi < 2 * width:
                sums = joint0[:, lo:hi], joint0[:, hi : hi + LANES]
            else:
                lo, hi = lo - 2 * width, hi - 2 * width
                sums = stage[num_slot:, lo:hi], stage[num_slot:, hi : hi + LANES]
            both = own[:, 2 * m * LANES : (2 * m + 1) * LANES], own[:, (2 * m + 1) * LANES : (2 * m + 2) * LANES]
            at = slice(m * LANES, (m + 1) * LANES)
            swapped[0, :cut, at] = jnp.where(odd, sums[1], sums[0])
            swapped[1, :cut, at] = jnp.where(odd, sums[0], sums[1])
            swapped[0, cut:, at] = jnp.where(odd, both[1], both[0])
            swapped[1, cut:, at] = jnp.where(odd, both[0], both[1])
        out.append(pltpu.make_async_copy(swapped.at[0], joint_hbm, sems.at[1]))
        out.append(pltpu.make_async_copy(swapped.at[1], extra_hbm, sems.at[2]))
    start(out)
    wait(last + out)


def owner_hot(sent, base, owned):
    col = iota(sent.shape, 1)
    asked = jnp.sum(jnp.where(col == base, sent, 0.0), axis=1, keepdims=True).astype(jnp.int32)
    return hot(iota((sent.shape[0], owned), 1) == asked)


def pack_kernel(
    num_off, num_src, slots, src_n, rcv_n, sent_hbm, pair_hbm, _, out_hbm,
    sent, pair, out, sems,
):
    half = pair.shape[1]
    cut = joint_rows(num_off, num_src)
    owned = (pair.shape[0] - cut) // 2
    copies = [
        pltpu.make_async_copy(sent_hbm, sent, sems.at[0]),
        pltpu.make_async_copy(pair_hbm, pair, sems.at[1]),
    ]
    start(copies)
    copies[0].wait()
    num = sent.shape[0]
    group = lax.axis_index("src")
    every_src = src_n * num_src
    col = iota((LANES, every_src), 0)
    pick = hot(col == num_off + iota((LANES, every_src), 1) % num_src).astype(BF16)
    from_group = iota((num, every_src), 0) // (slots * rcv_n)
    from_group = from_group == iota((num, every_src), 1) // num_src
    off_of = []
    src_of = []
    for k in range(2):
        part = sent[:, k * LANES : (k + 1) * LANES]
        chosen = owner_hot(part, num_off + num_src, owned).astype(BF16)
        upper, lower = halves(part)
        by_src = [jnp.where(from_group, dot(v, pick), 0.0).astype(BF16) for v in (upper, lower)]
        off_of.append((dot(chosen, upper, TN) + dot(chosen, lower, TN))[:, :num_off])
        src_of.append(dot(chosen, by_src[0], TN) + dot(chosen, by_src[1], TN))
    wait(copies[1:])
    terms = pair[cut:, :]
    sums = pair[:cut, :]
    off_sum = sums[:num_off] - count_dot_tn(jnp.concatenate(off_of, axis=0), terms)
    src_sum = -count_dot_tn(jnp.concatenate(src_of, axis=0), terms)
    mine = sums[num_off : num_off + num_src]
    per_off = slots // max(1, num_off // (src_n * rcv_n))
    per_src = slots // (num_src // rcv_n)
    if num_off * per_off < num or per_off > rcv_n:
        out[...] = jnp.zeros_like(out)
    copies = [
        pltpu.make_async_copy(
            out.at[h], out_hbm.at[:, half + h * LANES : half + (h + 1) * LANES], sems.at[h]
        )
        for h in range(2)
    ]
    for m in range(rcv_n):
        at = slice(m * LANES, (m + 1) * LANES)
        out[0, pl.ds(m, num_off, stride=per_off), :] = off_sum[:, at]
    copies[0].start()
    for m in range(rcv_n):
        at = slice(m * LANES, (m + 1) * LANES)
        for i in range(src_n):
            to = pl.ds(i * num_src * per_src + m, num_src, stride=per_src)
            source = src_sum[i * num_src : (i + 1) * num_src, at]
            out[1, to, :] = source + jnp.where(group == i, mine[:, at], 0.0)
    copies[1].start()
    wait(copies)


def shares_kernel(
    num_off, num_src, slots, edge, got_hbm, sums_hbm, offset_hbm, source_hbm,
    off_out, src_out, sent, tail, offset, source, rows, block, sems,
):
    rcv_n = lax.axis_size("rcv")
    piece = src_out.shape[1]
    rest = sums_hbm.shape[1] - piece
    copies = [
        pltpu.make_async_copy(got_hbm.at[:, :LANES], sent, sems.at[0]),
        pltpu.make_async_copy(sums_hbm.at[:, rest:], tail, sems.at[1]),
        pltpu.make_async_copy(offset_hbm, offset, sems.at[2]),
        pltpu.make_async_copy(source_hbm, source, sems.at[3]),
    ]
    start(copies)
    wait(copies)
    peers = sent.shape[0] // slots
    base = num_off + num_src
    both = sent[0:slots]
    for d in range(1, peers):
        both = both + sent[d * slots : (d + 1) * slots]
    for k in range(2):
        value = tail[k * slots : (k + 1) * slots]
        for d in range(k + 2, peers, 2):
            value = value + tail[d * slots : (d + 1) * slots]
        rows[:, k * LANES : (k + 1) * LANES] = value[:, :LANES]
        rows[:, piece + k * LANES : piece + (k + 1) * LANES] = value[:, LANES:]
    col = iota(both.shape, 1)
    num_o = jnp.sum(jnp.where(col == base + 1, both, 0.0), axis=1, keepdims=True)
    num_s = jnp.sum(jnp.where(col == base + 2, both, 0.0), axis=1, keepdims=True)
    here = lax.axis_index("rcv")
    off_rows = max(1, num_off // peers)
    src_rows = num_src // rcv_n
    at_off = (lax.axis_index("src") * rcv_n + here) * off_rows
    for count, num, at, first, terms in (
        (off_rows, num_o, slice(0, piece), at_off, offset),
        (src_rows, num_s, slice(piece, 2 * piece), here * src_rows, source),
    ):
        last = terms.shape[0] - 1
        parts = [
            jnp.concatenate(
                [rows[j * (slots // count) + m : j * (slots // count) + m + 1, at] for j in range(count)],
                axis=0,
            )
            for m in range(rcv_n)
        ]
        whole = jnp.concatenate(parts, axis=1)
        e, r = edge // 2, (whole.shape[1] - edge) // 2
        whole = join(
            whole[:, edge : edge + r], whole[:, edge + r :], whole[:, :e], whole[:, e:edge]
        )
        old = jnp.concatenate(
            [terms[pl.ds(jnp.minimum(first + j, last), 1), :] for j in range(count)], axis=0
        )
        new = old + whole / (num[:count] + 1.0)
        block[:, at] = jnp.zeros((slots, piece), F32)
        for j in range(count):
            for m in range(rcv_n):
                to = j * (slots // count) + m
                block[to : to + 1, at] = new[j : j + 1, m * piece : (m + 1) * piece]
    src_out[...] = block[:, piece:]
    done = block[:, :piece]
    for d in range(peers):
        off_out[d * slots : (d + 1) * slots, :] = done


def receiver_kernel(num_off, num_src, got_hbm, sums_hbm, terms_hbm, out, got, sums, terms, sems):
    edge = got.shape[1] - LANES
    rest = sums.shape[1]
    copies = [
        pltpu.make_async_copy(got_hbm.at[:, : edge + LANES], got, sems.at[0]),
        pltpu.make_async_copy(sums_hbm.at[:, :rest], sums, sems.at[1]),
        pltpu.make_async_copy(terms_hbm, terms, sems.at[2]),
    ]
    start(copies)
    wait(copies)
    sent = got[:, edge:]
    value = terms[...]
    chosen = owner_hot(sent, num_off + num_src, value.shape[0]).astype(BF16)
    per_slot = jnp.where(iota(sent.shape, 1) < num_off, sent, 0.0)
    num = jnp.sum(chosen_sum(chosen, per_slot), axis=1, keepdims=True)
    one = chosen_sum(chosen, got[:, :edge])
    two = chosen_sum(chosen, sums[...])
    edge //= 2
    rest //= 2
    total = join(two[:, :rest], two[:, rest:], one[:, :edge], one[:, edge:])
    out[...] = value + (total - num * value) / (num + 1.0)


def source_kernel(rcv_n, *refs):
    src_out, rest, sems = refs[rcv_n:]
    copies = [pltpu.make_async_copy(refs[k], rest.at[k], sems.at[k]) for k in range(rcv_n)]
    start(copies)
    wait(copies)
    slots, piece = rest.shape[1:]
    count = src_out.shape[0] // rcv_n
    here = lax.axis_index("rcv")
    for j in range(rcv_n):
        value = jnp.zeros((slots, piece), F32)
        for k in range(rcv_n):
            value = value + jnp.where((here + rcv_n - k) % rcv_n == j, rest[k], 0.0)
        for i in range(count):
            for m in range(rcv_n):
                row = i * (slots // count) + m
                src_out[j * count + i : j * count + i + 1, m * piece : (m + 1) * piece] = (
                    value[row : row + 1]
                )


def swap(value, slots):
    shape = value.shape
    value = value.reshape(shape[0] // slots, slots, shape[1])
    value = lax.all_to_all(value, AXES, split_axis=0, concat_axis=0, tiled=True)
    return value.reshape(shape)


def local(
    traces,
    trace_source,
    trace_offset,
    trace_slot,
    request_list,
    source_terms,
    receiver_terms,
    offset_terms,
):
    src_n = lax.axis_size("src")
    rcv_n = lax.axis_size("rcv")
    peers = src_n * rcv_n
    slots = request_list.shape[2]
    num_tr, samples = traces.shape
    owned, freq = receiver_terms.shape
    num_src = source_terms.shape[0]
    num_off = offset_terms.shape[0]
    num_slot = peers * slots
    joint = joint_rows(num_off, num_src)
    rows = num_slot + joint
    half = freq // 2
    edge = half // 2
    rest = half - edge
    piece = freq // rcv_n
    off_rows = max(1, num_off // peers)
    tile = min(512, num_tr)
    assert slots == num_src and off_rows * rcv_n <= slots and num_off + num_src + 3 <= LANES
    assert samples == 2 * freq and freq % (4 * LANES) == 0 and owned <= 256
    assert rcv_n % 2 == 0 and piece == 2 * LANES and edge == rest
    ids = [v.reshape(1, num_tr) for v in (trace_slot, trace_offset, trace_source)]
    lists = jnp.swapaxes(request_list, 1, 2).reshape(slots, peers)
    vmem = pl.BlockSpec(memory_space=pltpu.VMEM)
    hbm = pl.BlockSpec(memory_space=pltpu.HBM)
    anywhere = pl.BlockSpec(memory_space=pl.ANY)

    def static(kernel, *args):
        return lambda *refs: kernel(*args, *refs)

    def shape(*dims):
        return jax.ShapeDtypeStruct(dims, F32)

    def spectra(head, width, counts, joint0):
        lead = not head
        first = 0 if lead else half - width
        consts = [jnp.asarray(v) for v in twiddles(samples, first, first + width)]
        return pl.pallas_call(
            static(spectra_kernel, num_off, num_src, rcv_n, head, lead, tile),
            out_shape=(
                shape(num_slot, 2 * width + (2 * LANES if head else piece)),
                shape(joint, 2 * width) if head else shape(joint + owned, half),
                shape(rows, LANES) if head else shape(joint + owned, half),
            ),
            in_specs=[hbm] * 13,
            out_specs=(hbm, hbm, hbm),
            scratch_shapes=[
                pltpu.VMEM((joint, half), F32),
                pltpu.VMEM((2, joint + owned, half), F32),
                pltpu.VMEM((num_tr, samples), BF16),
                pltpu.VMEM((3, 1, num_tr), jnp.int32),
                pltpu.VMEM((slots, peers), jnp.int32),
                pltpu.VMEM((LANES, freq), F32),
                pltpu.VMEM((owned, freq), F32),
                pltpu.VMEM((rows, LANES), F32),
                pltpu.VMEM((num_slot, 2 * LANES), F32),
                pltpu.VMEM(consts[0].shape, F32),
                pltpu.VMEM(consts[1].shape, F32),
                pltpu.VMEM(consts[2].shape, F32),
                pltpu.VMEM((2, freq, 2 * width), BF16),
                pltpu.VMEM((rows, num_tr), BF16),
                pltpu.VMEM((rows, 2 * width), F32),
                pltpu.VMEM((rows, 2 * width), F32),
                pltpu.VMEM((2, tile, 4 * width), F32),
                pltpu.SemaphoreType.DMA((11,)),
                pltpu.SemaphoreType.DMA((num_tr // tile,)),
            ],
            compiler_params=pltpu.CompilerParams(vmem_limit_bytes=56 * 2**20),
            name="spectra%d" % head,
        )(traces, *ids, lists, offset_terms, source_terms, receiver_terms, counts, joint0, *consts)

    pay, joint0, counts = spectra(True, edge, offset_terms, source_terms)
    got = swap(pay, slots)
    sent = got[:, 2 * edge :]
    pay, keep, mate = spectra(False, rest, counts, joint0)
    mate = lax.ppermute(mate, "rcv", [(j, j ^ 1) for j in range(rcv_n)])
    pair = jnp.concatenate([keep[:joint] + mate[:joint], keep[joint:], mate[joint:]], axis=0)
    pay = pl.pallas_call(
        static(pack_kernel, num_off, num_src, slots, src_n, rcv_n),
        out_shape=shape(*pay.shape),
        in_specs=[anywhere, hbm, hbm],
        out_specs=hbm,
        scratch_shapes=[
            pltpu.VMEM((num_slot, 2 * LANES), F32),
            pltpu.VMEM((joint + 2 * owned, half), F32),
            pltpu.VMEM((2, num_slot, LANES), F32),
            pltpu.SemaphoreType.DMA((2,)),
        ],
        input_output_aliases={2: 0},
        name="pack",
    )(sent, pair, pay)
    sums = swap(pay, slots)

    off_new, src_new = pl.pallas_call(
        static(shares_kernel, num_off, num_src, slots, 2 * edge),
        out_shape=(shape(num_slot, piece), shape(slots, piece)),
        in_specs=[anywhere, anywhere, hbm, hbm],
        out_specs=(vmem, vmem),
        scratch_shapes=[
            pltpu.VMEM((num_slot, LANES), F32),
            pltpu.VMEM((num_slot, piece), F32),
            pltpu.VMEM((num_off, freq), F32),
            pltpu.VMEM((num_src, freq), F32),
            pltpu.VMEM((slots, 2 * piece), F32),
            pltpu.VMEM((slots, 2 * piece), F32),
            pltpu.SemaphoreType.DMA((4,)),
        ],
        name="shares",
    )(sent, sums, offset_terms, source_terms)
    every = swap(off_new, slots)
    parts = [src_new]
    for k in range(1, rcv_n):
        ring = [(j, (j + k) % rcv_n) for j in range(rcv_n)]
        parts.append(lax.ppermute(src_new, "rcv", ring))
    receiver_new = pl.pallas_call(
        static(receiver_kernel, num_off, num_src),
        out_shape=shape(owned, freq),
        in_specs=[anywhere, anywhere, hbm],
        out_specs=vmem,
        scratch_shapes=[
            pltpu.VMEM((num_slot, 2 * edge + LANES), F32),
            pltpu.VMEM((num_slot, 2 * rest), F32),
            pltpu.VMEM((owned, freq), F32),
            pltpu.SemaphoreType.DMA((3,)),
        ],
        name="receiver",
    )(got, sums, receiver_terms)
    source_new = pl.pallas_call(
        static(source_kernel, rcv_n),
        out_shape=shape(num_src, freq),
        in_specs=[anywhere] * rcv_n,
        out_specs=vmem,
        scratch_shapes=[
            pltpu.VMEM((rcv_n, slots, piece), F32),
            pltpu.SemaphoreType.DMA((rcv_n,)),
        ],
        name="source",
    )(*parts)
    every = every.reshape(peers, off_rows, slots // off_rows, piece)[:, :, :rcv_n]
    offset_new = every.reshape(peers * off_rows, freq)[:num_off]
    return (source_new, receiver_new, offset_new)


def solution(mesh):
    return jax.shard_map(
        local,
        mesh=mesh,
        in_specs=(
            P(AXES, None),
            P(AXES),
            P(AXES),
            P(AXES),
            P(AXES, None, None),
            P("src", None),
            P(AXES, None),
            P(),
        ),
        out_specs=(P("src", None), P(AXES, None), P()),
        check_vma=False,
    )
```
